32 devices in a mesh: freq: 2 (over x), atom: 16 (over z, y, core).
Axes of the slice: x: 2, y: 2, z: 4, core: 2. Of those that a mesh axis runs over, the one named last changes fastest.
Arguments:
- ham_diag: float32 [2, 128, 128], replicated
- ham_coup: float32 [1, 128, 128], replicated, may hold values from -0.25 to 0.25
- neighbors: int32 [256, 64], replicated, may hold values from 0 to 127, as said below
- pair_count: int32 [256], replicated, may hold values from 16 to 64
- shifts: int32 [8], replicated, may hold values from 1 to 16
- g_pairs: float32 [2, 32, 16384], P(None, ('freq', 'atom')), may hold values from -3 to 3
- emit_coup: float32 [2, 8, 16384], replicated, may hold values from -0.09375 to 0.09375
- absorb_coup: float32 [2, 8, 16384], replicated, may hold values from -0.09375 to 0.09375
Outputs:
- green: float32 [2, 32, 2, 128, 128], P(None, ('freq', 'atom'))
The draws below stay inside these ranges and needn't reach their ends.
Inputs may be any that keep to these rules, and one draw needn't show every extreme that they name: `neighbors`: entry 0 of each row is the atom's own index within its slab (atom index modulo 128); the entries of a row are distinct.
All inputs are finite; a program needn't handle non-finite values.
Results may differ from the reference program's by a relative error of at most 0.0001.
Values sent between devices are 32-bit elements; how exact they have to be, the bound alone decides.
No kernel may reach another device: no remote copies, remote signals or barrier semaphores. Data moves between devices by JAX's collectives and lax.ppermute only.
A program may use at most 128 MiB of HBM per device.

```python
import math
import jax
import jax.numpy as jnp
from jax import lax

ORB = 128
SLABS = 2
NBR = 64
MODES = 8
HALO = 16
INV_STEPS = 22
ATOMS = 256
PAIRS = 16384
NE = 32


def draw_ham_diag(key, part):
    sample = jax.random.normal(key, (SLABS, ORB, ORB), jnp.float32)
    return (sample + jnp.swapaxes(sample, 1, 2)) * (0.5 / math.sqrt(ORB))


def draw_neighbors(key, part):
    strides = jax.random.randint(key, (ATOMS, NBR), 1, 3)
    offsets = jnp.cumsum(strides, axis=1) - strides[:, :1]
    own_index = jnp.arange(ATOMS, dtype=jnp.int32) % ORB
    return ((own_index[:, None] + offsets) % ORB).astype(jnp.int32)


def draw_pair_count(key, part):
    counts = jax.random.randint(key, (ATOMS,), NBR // 4, NBR + 1)
    top_slot = jax.random.randint(jax.random.fold_in(key, 7), (), 0, ATOMS)
    low_slot = (top_slot + 1 + jax.random.randint(jax.random.fold_in(key, 8), (), 0, ATOMS - 1)) % ATOMS
    return counts.at[top_slot].set(NBR).at[low_slot].set(NBR // 4).astype(jnp.int32)


def draw_shifts(key, part):
    values = jax.random.randint(key, (MODES,), 1, HALO + 1)
    top_slot = jax.random.randint(jax.random.fold_in(key, 5), (), 0, MODES)
    low_slot = (top_slot + 1 + jax.random.randint(jax.random.fold_in(key, 6), (), 0, MODES - 1)) % MODES
    return values.at[top_slot].set(HALO).at[low_slot].set(1).astype(jnp.int32)


def steps_of(rng, shape, pieces, low, largest):
    def one(dim, blocks):
        draws = jax.random.uniform(jax.random.fold_in(jax.random.fold_in(rng, 6), dim), (blocks,), jnp.float32, low / len(pieces), largest / len(pieces))
        return jnp.repeat(jnp.exp(draws), shape[dim] // blocks).reshape((-1,) + (1,) * (len(shape) - dim - 1))

    factor_of = one(*pieces[0])
    for cut in pieces[1:]:
        factor_of = factor_of * one(*cut)
    return factor_of


def centred(stream_key, extent, scale, most, pieces=(), kind=jnp.bfloat16):
    values = jax.random.normal(stream_key, extent, jnp.float32) * scale
    if len(pieces) > 0:
        values = steps_of(stream_key, extent, pieces, -0.22, 0.18) * values
    return jnp.clip(values, min=-most, max=most).astype(kind)


def setup_inputs(seed: int = 0) -> dict:
    arg_keys = jax.random.split(jax.random.key(seed), 9)
    return {
        "ham_diag": draw_ham_diag(jax.random.fold_in(arg_keys[8], 71), 0),
        "ham_coup": centred(arg_keys[1], (SLABS - 1, ORB, ORB), (4 * ORB) ** -0.5, 0.25, (), jnp.float32),
        "neighbors": draw_neighbors(jax.random.fold_in(arg_keys[8], 71), 0),
        "pair_count": draw_pair_count(jax.random.fold_in(arg_keys[8], 71), 0),
        "shifts": draw_shifts(jax.random.fold_in(arg_keys[8], 71), 0),
        "g_pairs": centred(arg_keys[5], (2, NE, PAIRS), 0.5, 3.0, ((1, 32),), jnp.float32),
        "emit_coup": centred(arg_keys[6], (2, MODES, PAIRS), 0.015, 0.09375, (), jnp.float32),
        "absorb_coup": centred(arg_keys[7], (2, MODES, PAIRS), 0.015, 0.09375, (), jnp.float32),
    }


BROADEN = 0.8
ENERGY_LOW = -2.5
ENERGY_SPAN = 5.0


def matmul(left, right):
    return jnp.dot(left, right, precision=lax.Precision.HIGHEST, preferred_element_type=jnp.float32)


def complex_product(left, right):
    first = matmul(left[0], right[0])
    second = matmul(left[1], right[1])
    third = matmul(left[0] + left[1], right[0] + right[1])
    return (first - second, third - first - second)


def sandwich(outer_left, inner, outer_right):
    return (matmul(matmul(outer_left, inner[0]), outer_right),
            matmul(matmul(outer_left, inner[1]), outer_right))


def invert(real_part, imag_part):
    order = real_part.shape[0]
    unit_matrix = jnp.eye(order, dtype=real_part.dtype)
    scale = 1.0 / (jnp.sum(real_part * real_part) + jnp.sum(imag_part * imag_part))
    start = (real_part.T * scale, -imag_part.T * scale)

    def newton_step(index, current):
        product = complex_product((real_part, imag_part), current)
        residue = (2.0 * unit_matrix - product[0], -product[1])
        return complex_product(current, residue)

    return lax.fori_loop(0, INV_STEPS, newton_step, start)


def slab_green(sigma_blocks, energy, ham_diag, ham_coup):
    slabs = ham_diag.shape[0]
    order = ham_diag.shape[1]
    unit_matrix = jnp.eye(order, dtype=ham_diag.dtype)
    diag_real = [energy * unit_matrix - ham_diag[slab_index] - sigma_blocks[0, slab_index] for slab_index in range(slabs)]
    diag_imag = [BROADEN * unit_matrix - sigma_blocks[1, slab_index] for slab_index in range(slabs)]
    right_parts = [None] * slabs
    right_parts[slabs - 1] = invert(diag_real[slabs - 1], diag_imag[slabs - 1])
    for slab_index in range(slabs - 2, -1, -1):
        coupling = ham_coup[slab_index]
        folded = sandwich(coupling, right_parts[slab_index + 1], coupling.T)
        right_parts[slab_index] = invert(diag_real[slab_index] - folded[0], diag_imag[slab_index] - folded[1])
    blocks = [right_parts[0]]
    for slab_index in range(1, slabs):
        coupling = ham_coup[slab_index - 1]
        carried = sandwich(coupling.T, blocks[-1], coupling)
        own_part = right_parts[slab_index]
        update = complex_product(complex_product(own_part, carried), own_part)
        blocks.append((own_part[0] + update[0], own_part[1] + update[1]))
    return jnp.stack([jnp.stack([entry[0] for entry in blocks]), jnp.stack([entry[1] for entry in blocks])])


def sigma_blocks_of(sigma_pairs, neighbors, live):
    values = sigma_pairs.reshape(2, SLABS, ORB, NBR) * live
    slab_ids = jnp.broadcast_to(jnp.arange(SLABS, dtype=jnp.int32)[:, None, None], (SLABS, ORB, NBR))
    row_ids = jnp.broadcast_to(jnp.arange(ORB, dtype=jnp.int32)[None, :, None], (SLABS, ORB, NBR))
    columns = neighbors.reshape(SLABS, ORB, NBR)
    empty = jnp.zeros((2, SLABS, ORB, ORB), sigma_pairs.dtype)
    return empty.at[:, slab_ids, row_ids, columns].add(values)


def convolve(source, base, length, shifts, emit_coup, absorb_coup):
    width = source.shape[2]
    real_sum = jnp.zeros((length, width), source.dtype)
    imag_sum = jnp.zeros((length, width), source.dtype)
    for mode_index in range(MODES):
        shift_now = shifts[mode_index]
        below = lax.dynamic_slice_in_dim(source, (base - shift_now).astype(jnp.int32), length, 1)
        above = lax.dynamic_slice_in_dim(source, (base + shift_now).astype(jnp.int32), length, 1)
        emit_real = emit_coup[0, mode_index][None, :]
        emit_imag = emit_coup[1, mode_index][None, :]
        absorb_real = absorb_coup[0, mode_index][None, :]
        absorb_imag = absorb_coup[1, mode_index][None, :]
        real_sum = real_sum + emit_real * below[0] - emit_imag * below[1] + absorb_real * above[0] - absorb_imag * above[1]
        imag_sum = imag_sum + emit_real * below[1] + emit_imag * below[0] + absorb_real * above[1] + absorb_imag * above[0]
    return jnp.stack([real_sum, imag_sum])


def reference(ham_diag, ham_coup, neighbors, pair_count, shifts, g_pairs, emit_coup, absorb_coup):
    energy_count = g_pairs.shape[1]
    padded = jnp.pad(g_pairs, ((0, 0), (HALO, HALO), (0, 0)))
    sigma = convolve(padded, HALO, energy_count, shifts, emit_coup, absorb_coup)
    live = (jnp.arange(NBR, dtype=jnp.int32)[None, :] < pair_count[:, None]).astype(jnp.float32).reshape(SLABS, ORB, NBR)
    energies = ENERGY_LOW + ENERGY_SPAN * jnp.arange(energy_count).astype(jnp.float32) / energy_count
    by_energy = jnp.moveaxis(sigma, 1, 0).reshape(energy_count // 16, 16, 2, PAIRS)

    def solve_one(sigma_pairs, energy):
        return slab_green(sigma_blocks_of(sigma_pairs, neighbors, live), energy, ham_diag, ham_coup)

    def solve_batch(energy_batch):
        return jax.vmap(solve_one)(energy_batch[0], energy_batch[1])

    green = lax.map(solve_batch, (by_energy, energies.reshape(energy_count // 16, 16)))
    green = green.reshape(energy_count, 2, SLABS, ORB, ORB)
    return jnp.moveaxis(green, 1, 0)
```

```python
import functools

import jax
import jax.numpy as jnp
from jax import lax
from jax.experimental import pallas as pl
from jax.experimental.pallas import tpu as pltpu
from jax.sharding import PartitionSpec as P

HALO = 16
INV_STEPS = 22
EXACT_STEPS = 2

BROADEN = 0.8
ENERGY_LOW = -2.5
ENERGY_SPAN = 5.0

LANES = 128
RESIDUAL_LIMIT = 1e-4

AXES = ("freq", "atom")
VMEM = pltpu.MemorySpace.VMEM
SMEM = pltpu.MemorySpace.SMEM


def prepare_kernel(own_ref, neighbors_ref, count_ref, emit_ref, absorb_ref, table_ref, coef_ref):
    slabs, order, _ = table_ref.shape
    slots = neighbors_ref.shape[1]
    half = coef_ref.shape[3] // 2
    slot_id = lax.broadcasted_iota(jnp.int32, (slots, order), 0)
    column = lax.broadcasted_iota(jnp.int32, (order, order), 0)
    lane = lax.broadcasted_iota(jnp.int32, (order, order), 1)
    offset = lax.rem(lane, LANES // slots) * slots
    for slab in range(slabs):
        listed = neighbors_ref[slab * order : (slab + 1) * order, :].T
        listed = jnp.where(slot_id < count_ref[slab : slab + 1, :], listed, -1)
        found = jnp.full((order, order), -1, jnp.int32)
        for slot in range(slots):
            found = jnp.where(listed[slot : slot + 1, :] == column, slot, found)
        table_ref[slab] = jnp.where(found >= 0, found + offset, -1).T
    for side, weights_ref in enumerate((emit_ref, absorb_ref)):
        for row in range(half):
            lanes = slice(row * LANES, (row + 1) * LANES)
            real = weights_ref[0, :, lanes]
            imag = weights_ref[1, :, lanes]
            coef_ref[side, 0, :, row, :] = real
            coef_ref[side, 0, :, half + row, :] = real
            coef_ref[side, 1, :, row, :] = -imag
            coef_ref[side, 1, :, half + row, :] = imag


def prepare(own, neighbors, pair_count, emit_coup, absorb_coup, slabs, order, rows_per):
    modes = emit_coup.shape[1]
    blocks = emit_coup.shape[2] // (rows_per * LANES)
    weights = pl.BlockSpec(
        (2, modes, rows_per * LANES),
        lambda i, own_ref: (0, 0, jnp.minimum(own_ref[0], blocks - 1)),
    )
    whole = lambda *shape: pl.BlockSpec(shape, lambda i, own_ref: (0,) * len(shape))
    return pl.pallas_call(
        prepare_kernel,
        out_shape=(
            jax.ShapeDtypeStruct((slabs, order, order), jnp.int32),
            jax.ShapeDtypeStruct((2, 2, modes, 2 * rows_per, LANES), jnp.float32),
        ),
        grid_spec=pltpu.PrefetchScalarGridSpec(
            num_scalar_prefetch=1,
            grid=(1,),
            in_specs=[
                whole(*neighbors.shape),
                whole(slabs, order),
                weights,
                weights,
            ],
            out_specs=(
                whole(slabs, order, order),
                whole(2, 2, modes, 2 * rows_per, LANES),
            ),
        ),
        name="prepare",
    )(own, neighbors, pair_count.reshape(slabs, order), emit_coup, absorb_coup)


def convolve_kernel(shifts_ref, cells_ref, coef_ref, out_ref, plain_ref, swapped_ref):
    energies, height, _ = cells_ref.shape
    modes = coef_ref.shape[2]
    edge = jnp.zeros((HALO, height, LANES), jnp.float32)
    for ref in (plain_ref, swapped_ref):
        ref[0:HALO] = edge
        ref[HALO + energies : 2 * HALO + energies] = edge
    group = 32 if energies % 32 == 0 else 1

    def load(index, carry):
        for step in range(group):
            energy = index * group + step
            cell = cells_ref[energy]
            plain_ref[HALO + energy] = cell
            swapped_ref[HALO + energy] = jnp.concatenate(
                [cell[height // 2 :], cell[: height // 2]], axis=0
            )
        return carry

    def combine(index, carry):
        base = HALO + index * group
        total = [jnp.zeros((height, LANES), jnp.float32)] * group
        for mode in range(modes):
            shift = shifts_ref[mode]
            for side in range(2):
                first = base + (shift if side else -shift)
                direct = coef_ref[side, 0, mode]
                crossed = coef_ref[side, 1, mode]
                for step in range(group):
                    total[step] = (
                        total[step]
                        + direct * plain_ref[first + step]
                        + crossed * swapped_ref[first + step]
                    )
        for step in range(group):
            out_ref[index * group + step] = total[step]
        return carry

    lax.fori_loop(0, energies // group, load, 0)
    lax.fori_loop(0, energies // group, combine, 0)


def convolve(shifts, cells, coef):
    energies, height, _ = cells.shape
    padded = pltpu.VMEM((energies + 2 * HALO, height, LANES), jnp.float32)
    return pl.pallas_call(
        convolve_kernel,
        out_shape=jax.ShapeDtypeStruct(cells.shape, jnp.float32),
        in_specs=[
            pl.BlockSpec(memory_space=SMEM),
            pl.BlockSpec(memory_space=VMEM),
            pl.BlockSpec(memory_space=VMEM),
        ],
        out_specs=pl.BlockSpec(memory_space=VMEM),
        scratch_shapes=[padded, padded],
        name="convolve",
    )(shifts, cells, coef)


def embed(pair):
    order = pair.shape[1] // 2
    return jnp.concatenate(
        [pair, jnp.concatenate([-pair[:, order:], pair[:, :order]], axis=1)], axis=0
    )


def full_dot(left, right):
    return jnp.dot(left, right, precision=lax.Precision.HIGHEST, preferred_element_type=jnp.float32)


def narrow_dot(left, right):
    return jnp.dot(
        left.astype(jnp.bfloat16), right.astype(jnp.bfloat16), preferred_element_type=jnp.float32
    )


def halves(pair):
    order = pair.shape[1] // 2
    return pair[:, :order], pair[:, order:]


def pair_of(real, imag):
    return jnp.concatenate([real, imag], axis=1)


def unit_pair(order):
    row = lax.broadcasted_iota(jnp.int32, (order, 2 * order), 0)
    column = lax.broadcasted_iota(jnp.int32, (order, 2 * order), 1)
    return jnp.where(row == column, 1.0, 0.0).astype(jnp.float32)


def start_of(matrix):
    real, imag = halves(matrix)
    scale = 1.0 / jnp.sum(matrix * matrix)
    return pair_of(real.T * scale, imag.T * -scale)


def invert(matrix, state_ref):
    order = matrix.shape[0]
    start = start_of(matrix)
    state_ref[:order] = start
    state_ref[order:] = full_dot(matrix, embed(start))

    def step(index, carry):
        state = state_ref[...]
        narrow = state.astype(jnp.bfloat16)
        product = jnp.dot(narrow, embed(narrow[order:]), preferred_element_type=jnp.float32)
        state_ref[...] = (state - product) + state
        return carry

    lax.fori_loop(0, INV_STEPS - EXACT_STEPS, step, 0)
    current = state_ref[:order]
    unit = unit_pair(order)
    for _ in range(EXACT_STEPS):
        residual = unit - full_dot(matrix, embed(current))
        current = current + narrow_dot(current, embed(residual))
    return current, jnp.sum(residual * residual)


def invert_plain(matrix):
    unit = unit_pair(matrix.shape[0])

    def step(index, current):
        residue = 2.0 * unit - full_dot(matrix, embed(current))
        return full_dot(current, embed(residue))

    return lax.fori_loop(0, INV_STEPS, step, start_of(matrix))


def solve_kernel(own_ref, cells_ref, table_ref, diag_ref, coup_ref, out_ref, matrix_ref, state_ref, *, energies):
    slabs, order, _ = diag_ref.shape
    unit = unit_pair(order)
    position = jnp.full((8, LANES), own_ref[0], jnp.int32).astype(jnp.float32)
    energy = (ENERGY_LOW + ENERGY_SPAN * position / energies)[0:1, 0:1]
    row = lax.broadcasted_iota(jnp.int32, (8, LANES), 0)
    lines = cells_ref.shape[1] // 2
    line_of = row // (8 // lines)
    for slab in range(slabs):
        for block in range(order // 8):
            cell = cells_ref[slab * (order // 8) + block]
            rows = slice(block * 8, block * 8 + 8)
            table = table_ref[slab, rows, :]
            held = table >= 0
            lane = jnp.where(held, table, 0)
            for part in range(2):
                spread = jnp.take_along_axis(cell, line_of + part * lines, axis=0)
                sigma = jnp.where(held, jnp.take_along_axis(spread, lane, axis=1), 0.0)
                eye = unit[rows, :order]
                if part == 0:
                    entry = energy * eye - diag_ref[slab, rows, :] - sigma
                else:
                    entry = BROADEN * eye - sigma
                matrix_ref[slab, rows, part * order : (part + 1) * order] = entry

    coup = coup_ref[0]
    coup_t = coup.T

    def right_by(pair, other):
        real, imag = halves(pair)
        return pair_of(full_dot(real, other), full_dot(imag, other))

    def finish(invert_one):
        last, last_norm = invert_one(matrix_ref[1])
        left_of = full_dot(coup, last)
        right_of = right_by(last, coup_t)
        first, first_norm = invert_one(matrix_ref[0] - right_by(left_of, coup_t))
        update = full_dot(full_dot(right_of, embed(first)), embed(left_of))
        second = last + update
        for part in range(2):
            columns = slice(part * order, (part + 1) * order)
            out_ref[part, 0] = first[:, columns]
            out_ref[part, 1] = second[:, columns]
        return jnp.maximum(last_norm, first_norm), last_norm + first_norm

    worst, total = finish(lambda matrix: invert(matrix, state_ref))
    settled = jnp.logical_and(worst <= RESIDUAL_LIMIT, total == total)

    @pl.when(jnp.logical_not(settled))
    def _():
        finish(lambda matrix: (invert_plain(matrix), jnp.float32(0.0)))


def solve(own, cells, table, ham_diag, ham_coup, energies):
    slabs, order, _ = ham_diag.shape
    vmem = pl.BlockSpec(memory_space=VMEM)
    return pl.pallas_call(
        functools.partial(solve_kernel, energies=energies),
        out_shape=jax.ShapeDtypeStruct((2, slabs, order, order), jnp.float32),
        in_specs=[pl.BlockSpec(memory_space=SMEM), vmem, vmem, vmem, vmem],
        out_specs=vmem,
        scratch_shapes=[
            pltpu.VMEM((slabs, order, 2 * order), jnp.float32),
            pltpu.VMEM((2 * order, 2 * order), jnp.float32),
        ],
        name="solve",
    )(own, cells, table, ham_diag, ham_coup)


def on_device(ham_diag, ham_coup, neighbors, pair_count, shifts, g_pairs, emit_coup, absorb_coup):
    slabs, order, _ = ham_diag.shape
    atoms, slots = neighbors.shape
    devices = lax.axis_size("freq") * lax.axis_size("atom")
    own = (lax.axis_index("freq") * lax.axis_size("atom") + lax.axis_index("atom")).astype(jnp.int32).reshape(1)
    rows = g_pairs.shape[2] // LANES
    rows_per = -(-rows // devices)
    spare = rows_per * devices - rows

    cells = g_pairs.reshape(2, rows, LANES)
    if spare:
        cells = jnp.pad(cells, ((0, 0), (0, spare), (0, 0)))
    cells = cells.reshape(2, devices, rows_per, LANES).transpose(1, 0, 2, 3)
    cells = cells.reshape(devices, 2 * rows_per, LANES)
    owned = lax.all_to_all(cells, AXES, 0, 0, tiled=True)
    table, coef = prepare(own, neighbors, pair_count, emit_coup, absorb_coup, slabs, order, rows_per)
    sigma = convolve(shifts, owned, coef)
    sigma = lax.all_to_all(sigma, AXES, 0, 0, tiled=True)
    lines = 8 * slots // LANES
    if rows_per != lines:
        sigma = sigma.reshape(devices, 2, rows_per, LANES).transpose(1, 0, 2, 3)
        sigma = sigma.reshape(2, devices * rows_per, LANES)[:, :rows]
        sigma = sigma.reshape(2, rows // lines, lines, LANES).transpose(1, 0, 2, 3)
        sigma = sigma.reshape(rows // lines, 2 * lines, LANES)
    green = solve(own, sigma, table, ham_diag, ham_coup, devices)
    return green.reshape(2, 1, slabs, order, order)


def solution(mesh):
    return jax.shard_map(
        on_device,
        mesh=mesh,
        in_specs=(P(), P(), P(), P(), P(), P(None, ("freq", "atom"), None), P(), P()),
        out_specs=P(None, ("freq", "atom"), None, None, None),
        check_vma=False,
    )
```

```python
import functools

import jax
import jax.numpy as jnp
from jax import lax
from jax.experimental import pallas as pl
from jax.experimental.pallas import tpu as pltpu
from jax.sharding import PartitionSpec as P

HALO = 16
INV_STEPS = 22
EXACT_STEPS = 2

BROADEN = 0.8
ENERGY_LOW = -2.5
ENERGY_SPAN = 5.0

LANES = 128
RESIDUAL_LIMIT = 1e-4

AXES = ("freq", "atom")
VMEM = pltpu.MemorySpace.VMEM
SMEM = pltpu.MemorySpace.SMEM


def prepare_kernel(own_ref, neighbors_ref, count_ref, emit_ref, absorb_ref, table_ref, coef_ref):
    slabs, order, _ = table_ref.shape
    slots = neighbors_ref.shape[1]
    half = coef_ref.shape[3] // 2
    slot_id = lax.broadcasted_iota(jnp.int32, (slots, order), 0)
    column = lax.broadcasted_iota(jnp.int32, (order, order), 0)
    lane = lax.broadcasted_iota(jnp.int32, (order, order), 1)
    offset = lax.rem(lane, LANES // slots) * slots
    for slab in range(slabs):
        listed = neighbors_ref[slab * order : (slab + 1) * order, :].T
        listed = jnp.where(slot_id < count_ref[slab : slab + 1, :], listed, -1)
        found = jnp.full((order, order), -1, jnp.int32)
        for slot in range(slots):
            found = jnp.where(listed[slot : slot + 1, :] == column, slot, found)
        table_ref[slab] = jnp.where(found >= 0, found + offset, -1).T
    for side, weights_ref in enumerate((emit_ref, absorb_ref)):
        for row in range(half):
            lanes = slice(row * LANES, (row + 1) * LANES)
            real = weights_ref[0, :, lanes]
            imag = weights_ref[1, :, lanes]
            coef_ref[side, 0, :, row, :] = real
            coef_ref[side, 0, :, half + row, :] = real
            coef_ref[side, 1, :, row, :] = -imag
            coef_ref[side, 1, :, half + row, :] = imag


def prepare(own, neighbors, pair_count, emit_coup, absorb_coup, slabs, order, rows_per):
    modes = emit_coup.shape[1]
    blocks = emit_coup.shape[2] // (rows_per * LANES)
    weights = pl.BlockSpec(
        (2, modes, rows_per * LANES),
        lambda i, own_ref: (0, 0, jnp.minimum(own_ref[0], blocks - 1)),
    )
    whole = lambda *shape: pl.BlockSpec(shape, lambda i, own_ref: (0,) * len(shape))
    return pl.pallas_call(
        prepare_kernel,
        out_shape=(
            jax.ShapeDtypeStruct((slabs, order, order), jnp.int32),
            jax.ShapeDtypeStruct((2, 2, modes, 2 * rows_per, LANES), jnp.float32),
        ),
        grid_spec=pltpu.PrefetchScalarGridSpec(
            num_scalar_prefetch=1,
            grid=(1,),
            in_specs=[
                whole(*neighbors.shape),
                whole(slabs, order),
                weights,
                weights,
            ],
            out_specs=(
                whole(slabs, order, order),
                whole(2, 2, modes, 2 * rows_per, LANES),
            ),
        ),
        compiler_params=pltpu.CompilerParams(vmem_limit_bytes=16 * 2**20),
        name="prepare",
    )(own, neighbors, pair_count.reshape(slabs, order), emit_coup, absorb_coup)


def convolve_kernel(shifts_ref, cells_ref, coef_ref, out_ref, plain_ref, swapped_ref):
    energies, height, _ = cells_ref.shape
    modes = coef_ref.shape[2]
    edge = jnp.zeros((HALO, height, LANES), jnp.float32)
    for ref in (plain_ref, swapped_ref):
        ref[0:HALO] = edge
        ref[HALO + energies : 2 * HALO + energies] = edge
    group = 32 if energies % 32 == 0 else 1

    def load(index, carry):
        for step in range(group):
            energy = index * group + step
            cell = cells_ref[energy]
            plain_ref[HALO + energy] = cell
            swapped_ref[HALO + energy] = jnp.concatenate(
                [cell[height // 2 :], cell[: height // 2]], axis=0
            )
        return carry

    def combine(index, carry):
        base = HALO + index * group
        total = [jnp.zeros((height, LANES), jnp.float32)] * group
        for mode in range(modes):
            shift = shifts_ref[mode]
            for side in range(2):
                first = base + (shift if side else -shift)
                direct = coef_ref[side, 0, mode]
                crossed = coef_ref[side, 1, mode]
                for step in range(group):
                    total[step] = (
                        total[step]
                        + direct * plain_ref[first + step]
                        + crossed * swapped_ref[first + step]
                    )
        for step in range(group):
            out_ref[index * group + step] = total[step]
        return carry

    lax.fori_loop(0, energies // group, load, 0)
    lax.fori_loop(0, energies // group, combine, 0)


def convolve(shifts, cells, coef):
    energies, height, _ = cells.shape
    padded = pltpu.VMEM((energies + 2 * HALO, height, LANES), jnp.float32)
    return pl.pallas_call(
        convolve_kernel,
        out_shape=jax.ShapeDtypeStruct(cells.shape, jnp.float32),
        in_specs=[
            pl.BlockSpec(memory_space=SMEM),
            pl.BlockSpec(memory_space=VMEM),
            pl.BlockSpec(memory_space=VMEM),
        ],
        out_specs=pl.BlockSpec(memory_space=VMEM),
        scratch_shapes=[padded, padded],
        compiler_params=pltpu.CompilerParams(vmem_limit_bytes=16 * 2**20),
        name="convolve",
    )(shifts, cells, coef)


def embed(pair):
    order = pair.shape[1] // 2
    return jnp.concatenate(
        [pair, jnp.concatenate([-pair[:, order:], pair[:, :order]], axis=1)], axis=0
    )


def full_dot(left, right):
    return jnp.dot(left, right, precision=lax.Precision.HIGHEST, preferred_element_type=jnp.float32)


def narrow_dot(left, right):
    return jnp.dot(
        left.astype(jnp.bfloat16), right.astype(jnp.bfloat16), preferred_element_type=jnp.float32
    )


def halves(pair):
    order = pair.shape[1] // 2
    return pair[:, :order], pair[:, order:]


def pair_of(real, imag):
    return jnp.concatenate([real, imag], axis=1)


def unit_pair(order):
    row = lax.broadcasted_iota(jnp.int32, (order, 2 * order), 0)
    column = lax.broadcasted_iota(jnp.int32, (order, 2 * order), 1)
    return jnp.where(row == column, 1.0, 0.0).astype(jnp.float32)


def start_of(matrix):
    real, imag = halves(matrix)
    scale = 1.0 / jnp.sum(matrix * matrix)
    return pair_of(real.T * scale, imag.T * -scale)


def invert(matrix, state_ref):
    order = matrix.shape[0]
    start = start_of(matrix)
    state_ref[:order] = start
    state_ref[order:] = full_dot(matrix, embed(start))

    def step(index, carry):
        state = state_ref[...]
        narrow = state.astype(jnp.bfloat16)
        product = jnp.dot(narrow, embed(narrow[order:]), preferred_element_type=jnp.float32)
        state_ref[...] = (state - product) + state
        return carry

    lax.fori_loop(0, INV_STEPS - EXACT_STEPS, step, 0)
    current = state_ref[:order]
    unit = unit_pair(order)
    for _ in range(EXACT_STEPS):
        residual = unit - full_dot(matrix, embed(current))
        current = current + narrow_dot(current, embed(residual))
    return current, jnp.sum(residual * residual)


def invert_plain(matrix):
    unit = unit_pair(matrix.shape[0])

    def step(index, current):
        residue = 2.0 * unit - full_dot(matrix, embed(current))
        return full_dot(current, embed(residue))

    return lax.fori_loop(0, INV_STEPS, step, start_of(matrix))


def solve_kernel(own_ref, cells_ref, table_ref, diag_ref, coup_ref, out_ref, matrix_ref, state_ref, *, energies):
    slabs, order, _ = diag_ref.shape
    unit = unit_pair(order)
    position = jnp.full((8, LANES), own_ref[0], jnp.int32).astype(jnp.float32)
    energy = (ENERGY_LOW + ENERGY_SPAN * position / energies)[0:1, 0:1]
    row = lax.broadcasted_iota(jnp.int32, (8, LANES), 0)
    lines = cells_ref.shape[1] // 2
    line_of = row // (8 // lines)
    for slab in range(slabs):
        for block in range(order // 8):
            cell = cells_ref[slab * (order // 8) + block]
            rows = slice(block * 8, block * 8 + 8)
            table = table_ref[slab, rows, :]
            held = table >= 0
            lane = jnp.where(held, table, 0)
            for part in range(2):
                spread = jnp.take_along_axis(cell, line_of + part * lines, axis=0)
                sigma = jnp.where(held, jnp.take_along_axis(spread, lane, axis=1), 0.0)
                eye = unit[rows, :order]
                if part == 0:
                    entry = energy * eye - diag_ref[slab, rows, :] - sigma
                else:
                    entry = BROADEN * eye - sigma
                matrix_ref[slab, rows, part * order : (part + 1) * order] = entry

    coup = coup_ref[0]
    coup_t = coup.T

    def right_by(pair, other):
        real, imag = halves(pair)
        return pair_of(full_dot(real, other), full_dot(imag, other))

    def finish(invert_one):
        last, last_norm = invert_one(matrix_ref[1])
        left_of = full_dot(coup, last)
        right_of = right_by(last, coup_t)
        first, first_norm = invert_one(matrix_ref[0] - right_by(left_of, coup_t))
        update = full_dot(full_dot(right_of, embed(first)), embed(left_of))
        second = last + update
        for part in range(2):
            columns = slice(part * order, (part + 1) * order)
            out_ref[part, 0] = first[:, columns]
            out_ref[part, 1] = second[:, columns]
        return jnp.maximum(last_norm, first_norm), last_norm + first_norm

    worst, total = finish(lambda matrix: invert(matrix, state_ref))
    settled = jnp.logical_and(worst <= RESIDUAL_LIMIT, total == total)

    @pl.when(jnp.logical_not(settled))
    def _():
        finish(lambda matrix: (invert_plain(matrix), jnp.float32(0.0)))


def solve(own, cells, table, ham_diag, ham_coup, energies):
    slabs, order, _ = ham_diag.shape
    vmem = pl.BlockSpec(memory_space=VMEM)
    return pl.pallas_call(
        functools.partial(solve_kernel, energies=energies),
        out_shape=jax.ShapeDtypeStruct((2, slabs, order, order), jnp.float32),
        in_specs=[pl.BlockSpec(memory_space=SMEM), vmem, vmem, vmem, vmem],
        out_specs=vmem,
        scratch_shapes=[
            pltpu.VMEM((slabs, order, 2 * order), jnp.float32),
            pltpu.VMEM((2 * order, 2 * order), jnp.float32),
        ],
        compiler_params=pltpu.CompilerParams(vmem_limit_bytes=16 * 2**20),
        name="solve",
    )(own, cells, table, ham_diag, ham_coup)


def on_device(ham_diag, ham_coup, neighbors, pair_count, shifts, g_pairs, emit_coup, absorb_coup):
    slabs, order, _ = ham_diag.shape
    atoms, slots = neighbors.shape
    devices = lax.axis_size("freq") * lax.axis_size("atom")
    own = (lax.axis_index("freq") * lax.axis_size("atom") + lax.axis_index("atom")).astype(jnp.int32).reshape(1)
    rows = g_pairs.shape[2] // LANES
    rows_per = -(-rows // devices)
    spare = rows_per * devices - rows

    cells = g_pairs.reshape(2, rows, LANES)
    if spare:
        cells = jnp.pad(cells, ((0, 0), (0, spare), (0, 0)))
    cells = cells.reshape(2, devices, rows_per, LANES).transpose(1, 0, 2, 3)
    cells = cells.reshape(devices, 2 * rows_per, LANES)
    owned = lax.all_to_all(cells, AXES, 0, 0, tiled=True)
    table, coef = prepare(own, neighbors, pair_count, emit_coup, absorb_coup, slabs, order, rows_per)
    sigma = convolve(shifts, owned, coef)
    sigma = lax.all_to_all(sigma, AXES, 0, 0, tiled=True)
    lines = 8 * slots // LANES
    if rows_per != lines:
        sigma = sigma.reshape(devices, 2, rows_per, LANES).transpose(1, 0, 2, 3)
        sigma = sigma.reshape(2, devices * rows_per, LANES)[:, :rows]
        sigma = sigma.reshape(2, rows // lines, lines, LANES).transpose(1, 0, 2, 3)
        sigma = sigma.reshape(rows // lines, 2 * lines, LANES)
    green = solve(own, sigma, table, ham_diag, ham_coup, devices)
    return green.reshape(2, 1, slabs, order, order)


def solution(mesh):
    return jax.shard_map(
        on_device,
        mesh=mesh,
        in_specs=(P(), P(), P(), P(), P(), P(None, ("freq", "atom"), None), P(), P()),
        out_specs=P(None, ("freq", "atom"), None, None, None),
        check_vma=False,
    )
```

```python
import functools

import jax
import jax.numpy as jnp
from jax import lax
from jax.experimental import pallas as pl
from jax.experimental.pallas import tpu as pltpu
from jax.sharding import PartitionSpec as P

HALO = 16
INV_STEPS = 22
EXACT_STEPS = 2

BROADEN = 0.8
ENERGY_LOW = -2.5
ENERGY_SPAN = 5.0

LANES = 128
RESIDUAL_LIMIT = 1e-5

AXES = ("freq", "atom")
VMEM = pltpu.MemorySpace.VMEM
SMEM = pltpu.MemorySpace.SMEM


def prepare_kernel(own_ref, neighbors_ref, count_ref, emit_ref, absorb_ref, table_ref, coef_ref):
    slabs, order, _ = table_ref.shape
    slots = neighbors_ref.shape[1]
    half = coef_ref.shape[3] // 2
    slot_id = lax.broadcasted_iota(jnp.int32, (slots, order), 0)
    column = lax.broadcasted_iota(jnp.int32, (order, order), 0)
    lane = lax.broadcasted_iota(jnp.int32, (order, order), 1)
    offset = lax.rem(lane, LANES // slots) * slots
    for slab in range(slabs):
        listed = neighbors_ref[slab * order : (slab + 1) * order, :].T
        listed = jnp.where(slot_id < count_ref[slab : slab + 1, :], listed, -1)
        found = jnp.full((order, order), -1, jnp.int32)
        for slot in range(slots):
            found = jnp.where(listed[slot : slot + 1, :] == column, slot, found)
        table_ref[slab] = jnp.where(found >= 0, found + offset, -1).T
    for side, weights_ref in enumerate((emit_ref, absorb_ref)):
        for row in range(half):
            lanes = slice(row * LANES, (row + 1) * LANES)
            real = weights_ref[0, :, lanes]
            imag = weights_ref[1, :, lanes]
            coef_ref[side, 0, :, row, :] = real
            coef_ref[side, 0, :, half + row, :] = real
            coef_ref[side, 1, :, row, :] = -imag
            coef_ref[side, 1, :, half + row, :] = imag


def prepare(own, neighbors, pair_count, emit_coup, absorb_coup, slabs, order, rows_per):
    modes = emit_coup.shape[1]
    blocks = emit_coup.shape[2] // (rows_per * LANES)
    weights = pl.BlockSpec(
        (2, modes, rows_per * LANES),
        lambda i, own_ref: (0, 0, jnp.minimum(own_ref[0], blocks - 1)),
    )
    whole = lambda *shape: pl.BlockSpec(shape, lambda i, own_ref: (0,) * len(shape))
    return pl.pallas_call(
        prepare_kernel,
        out_shape=(
            jax.ShapeDtypeStruct((slabs, order, order), jnp.int32),
            jax.ShapeDtypeStruct((2, 2, modes, 2 * rows_per, LANES), jnp.float32),
        ),
        grid_spec=pltpu.PrefetchScalarGridSpec(
            num_scalar_prefetch=1,
            grid=(1,),
            in_specs=[
                whole(*neighbors.shape),
                whole(slabs, order),
                weights,
                weights,
            ],
            out_specs=(
                whole(slabs, order, order),
                whole(2, 2, modes, 2 * rows_per, LANES),
            ),
        ),
        compiler_params=pltpu.CompilerParams(vmem_limit_bytes=16 * 2**20),
        name="prepare",
    )(own, neighbors, pair_count.reshape(slabs, order), emit_coup, absorb_coup)


def convolve_kernel(shifts_ref, cells_ref, coef_ref, out_ref, plain_ref, swapped_ref):
    energies, height, _ = cells_ref.shape
    modes = coef_ref.shape[2]
    edge = jnp.zeros((HALO, height, LANES), jnp.float32)
    for ref in (plain_ref, swapped_ref):
        ref[0:HALO] = edge
        ref[HALO + energies : 2 * HALO + energies] = edge
    group = 32 if energies % 32 == 0 else 1

    def load(index, carry):
        for step in range(group):
            energy = index * group + step
            cell = cells_ref[energy]
            plain_ref[HALO + energy] = cell
            swapped_ref[HALO + energy] = jnp.concatenate(
                [cell[height // 2 :], cell[: height // 2]], axis=0
            )
        return carry

    def combine(index, carry):
        base = HALO + index * group
        total = [jnp.zeros((height, LANES), jnp.float32)] * group
        for mode in range(modes):
            shift = shifts_ref[mode]
            for side in range(2):
                first = base + (shift if side else -shift)
                direct = coef_ref[side, 0, mode]
                crossed = coef_ref[side, 1, mode]
                for step in range(group):
                    total[step] = (
                        total[step]
                        + direct * plain_ref[first + step]
                        + crossed * swapped_ref[first + step]
                    )
        for step in range(group):
            out_ref[index * group + step] = total[step]
        return carry

    lax.fori_loop(0, energies // group, load, 0)
    lax.fori_loop(0, energies // group, combine, 0)


def convolve(shifts, cells, coef):
    energies, height, _ = cells.shape
    padded = pltpu.VMEM((energies + 2 * HALO, height, LANES), jnp.float32)
    return pl.pallas_call(
        convolve_kernel,
        out_shape=jax.ShapeDtypeStruct(cells.shape, jnp.float32),
        in_specs=[
            pl.BlockSpec(memory_space=SMEM),
            pl.BlockSpec(memory_space=VMEM),
            pl.BlockSpec(memory_space=VMEM),
        ],
        out_specs=pl.BlockSpec(memory_space=VMEM),
        scratch_shapes=[padded, padded],
        compiler_params=pltpu.CompilerParams(vmem_limit_bytes=16 * 2**20),
        name="convolve",
    )(shifts, cells, coef)


def embed(pair):
    order = pair.shape[1] // 2
    return jnp.concatenate(
        [pair, jnp.concatenate([-pair[:, order:], pair[:, :order]], axis=1)], axis=0
    )


def pieces(value, count):
    parts = []
    for index in range(count):
        parts.append(value.astype(jnp.bfloat16))
        if index + 1 < count:
            value = value - parts[-1].astype(jnp.float32)
    return parts


def unit_pair(order):
    row = lax.broadcasted_iota(jnp.int32, (order, 2 * order), 0)
    column = lax.broadcasted_iota(jnp.int32, (order, 2 * order), 1)
    return jnp.where(row == column, 1.0, 0.0).astype(jnp.float32)


def square_sum(pair):
    squares = pair * pair
    return jnp.sum(jnp.sum(squares, axis=0, keepdims=True), axis=1, keepdims=True)


def adjoint(pair):
    order = pair.shape[0]
    return jnp.concatenate([pair[:, :order].T, -pair[:, order:].T], axis=1)


class Multiplier:
    def __init__(self, blocks):
        self.blocks = blocks
        self.turn = 0

    def load(self, factor, transpose=False):
        stage = self.turn
        self.turn = 1 - stage
        for unit in range(2):
            pltpu.matmul_push_rhs(factor, stage, unit, transpose=transpose)
        return stage

    def feed(self, stage, *rows):
        for block, left in rows:
            half = left.shape[0] // 2
            for unit in range(2):
                pltpu.matmul_acc_lhs(
                    self.blocks[block][unit],
                    left[unit * half : (unit + 1) * half],
                    load_staged_rhs=stage,
                )
            stage = None

    def take(self, block):
        return jnp.concatenate(
            [pltpu.matmul_pop(self.blocks[block][unit]) for unit in range(2)], axis=0
        )

    def product(self, left, right, transpose=False):
        for index, factor in enumerate(right):
            stage = self.load(factor, transpose)
            self.feed(stage, *[(0, piece) for piece in left[: len(left) - index]])
        return self.take(0)


def iterate(mxu, matrix, follow, count):
    order = matrix.shape[0]
    split = pieces(matrix, 2)
    product = mxu.product(split, [embed(piece) for piece in split], transpose=True)
    scale = 1.0 / square_sum(matrix)
    x = adjoint(matrix) * scale
    y = product * scale
    for index in range(count):
        narrow = y.astype(jnp.bfloat16)
        stage = mxu.load(embed(narrow))
        mxu.feed(stage, (0, narrow))
        if index:
            x = (x - mxu.take(1)) + x
        mxu.feed(None, (1, x.astype(jnp.bfloat16)))
        y = (y - mxu.take(0)) + y
    x = (x - mxu.take(1)) + x

    high, low = pieces(x, 2)
    wide = mxu.load(embed(high))
    rest = mxu.load(embed(low))
    mxu.feed(wide, (0, split[0]), (0, split[1]))
    mxu.feed(None, (1, follow[0]), (1, follow[1]))
    mxu.feed(rest, (0, split[0]), (1, follow[0]))
    residual = unit_pair(order) - mxu.take(0)
    t = mxu.take(1)
    r_high, r_low = pieces(residual, 2)
    t_high, t_low = pieces(t, 2)
    wide = mxu.load(embed(r_high))
    rest = mxu.load(embed(r_low))
    mxu.feed(wide, (0, r_high), (1, high), (1, low), (2, t_high), (2, t_low))
    mxu.feed(rest, (1, high), (2, t_high))
    residual = mxu.take(0)
    stage = mxu.load(embed(residual.astype(jnp.bfloat16)))
    x = x + mxu.take(1)
    t = t + mxu.take(2)
    mxu.feed(stage, (0, x.astype(jnp.bfloat16)), (1, t.astype(jnp.bfloat16)))
    return x + mxu.take(0), t + mxu.take(1), square_sum(residual)


def iterate_plain(mxu, matrix):
    split = pieces(matrix, 3)
    unit = unit_pair(matrix.shape[0])

    def step(index, x):
        right = [embed(piece) for piece in pieces(x, 3)]
        residue = 2.0 * unit - mxu.product(split, right)
        return mxu.product(pieces(x, 3), [embed(piece) for piece in pieces(residue, 3)])

    return lax.fori_loop(0, INV_STEPS, step, adjoint(matrix) * (1.0 / square_sum(matrix)))


def solve_kernel(own_ref, cells_ref, table_ref, diag_ref, coup_ref, out_ref, matrix_ref, *, energies):
    slabs, order, _ = diag_ref.shape
    unit = unit_pair(order)
    position = jnp.full((8, LANES), own_ref[0], jnp.int32).astype(jnp.float32)
    energy = (ENERGY_LOW + ENERGY_SPAN * position / energies)[0:1, 0:1]
    row = lax.broadcasted_iota(jnp.int32, (8, LANES), 0)
    lines = cells_ref.shape[1] // 2
    line_of = row // (8 // lines)
    for slab in range(slabs):
        for block in range(order // 8):
            cell = cells_ref[slab * (order // 8) + block]
            rows = slice(block * 8, block * 8 + 8)
            table = table_ref[slab, rows, :]
            held = table >= 0
            lane = jnp.where(held, table, 0)
            for part in range(2):
                spread = jnp.take_along_axis(cell, line_of + part * lines, axis=0)
                sigma = jnp.where(held, jnp.take_along_axis(spread, lane, axis=1), 0.0)
                eye = unit[rows, :order]
                if part == 0:
                    entry = energy * eye - diag_ref[slab, rows, :] - sigma
                else:
                    entry = BROADEN * eye - sigma
                matrix_ref[slab, rows, part * order : (part + 1) * order] = entry

    coup = coup_ref[0]
    none = jnp.zeros_like(coup)
    coup_left = jnp.concatenate([coup, none], axis=1)
    coup_right = embed(jnp.concatenate([coup.T, none], axis=1))

    def store(first, second):
        for part in range(2):
            columns = slice(part * order, (part + 1) * order)
            out_ref[part, 0] = first[:, columns]
            out_ref[part, 1] = second[:, columns]

    def body(*accumulators):
        mxu = Multiplier([accumulators[2 * i : 2 * i + 2] for i in range(3)])
        right = pieces(coup_right, 2)
        last, left_of, last_norm = iterate(mxu, matrix_ref[1], pieces(coup_left, 2), INV_STEPS - EXACT_STEPS)
        matrix = matrix_ref[0] - mxu.product(pieces(left_of, 2), right)
        right_of = mxu.product(pieces(last, 2), right)
        first, both, first_norm = iterate(mxu, matrix, pieces(right_of, 2), INV_STEPS - EXACT_STEPS)
        update = mxu.product(pieces(both, 2), [embed(piece) for piece in pieces(left_of, 2)])
        store(first, last + update)
        worst = jnp.maximum(last_norm, first_norm)[0, 0]
        settled = jnp.logical_and(worst <= RESIDUAL_LIMIT, last_norm[0, 0] + first_norm[0, 0] <= 2.0 * RESIDUAL_LIMIT)

        @pl.when(jnp.logical_not(settled))
        def _():
            right = pieces(coup_right, 3)
            last = iterate_plain(mxu, matrix_ref[1])
            left_of = mxu.product(pieces(coup_left, 3), [embed(piece) for piece in pieces(last, 3)])
            right_of = mxu.product(pieces(last, 3), right)
            first = iterate_plain(mxu, matrix_ref[0] - mxu.product(pieces(left_of, 3), right))
            both = mxu.product(pieces(right_of, 3), [embed(piece) for piece in pieces(first, 3)])
            update = mxu.product(pieces(both, 3), [embed(piece) for piece in pieces(left_of, 3)])
            store(first, last + update)

    shape = (order // 2, 2 * order)
    pl.run_scoped(body, *[pltpu.ACC(unit)(shape, jnp.float32) for _ in range(3) for unit in range(2)])


def solve(own, cells, table, ham_diag, ham_coup, energies):
    slabs, order, _ = ham_diag.shape
    vmem = pl.BlockSpec(memory_space=VMEM)
    return pl.pallas_call(
        functools.partial(solve_kernel, energies=energies),
        out_shape=jax.ShapeDtypeStruct((2, slabs, order, order), jnp.float32),
        in_specs=[pl.BlockSpec(memory_space=SMEM), vmem, vmem, vmem, vmem],
        out_specs=vmem,
        scratch_shapes=[
            pltpu.VMEM((slabs, order, 2 * order), jnp.float32),
        ],
        compiler_params=pltpu.CompilerParams(vmem_limit_bytes=16 * 2**20),
        name="solve",
    )(own, cells, table, ham_diag, ham_coup)


def on_device(ham_diag, ham_coup, neighbors, pair_count, shifts, g_pairs, emit_coup, absorb_coup):
    slabs, order, _ = ham_diag.shape
    atoms, slots = neighbors.shape
    devices = lax.axis_size("freq") * lax.axis_size("atom")
    own = (lax.axis_index("freq") * lax.axis_size("atom") + lax.axis_index("atom")).astype(jnp.int32).reshape(1)
    rows = g_pairs.shape[2] // LANES
    rows_per = -(-rows // devices)
    spare = rows_per * devices - rows

    cells = g_pairs.reshape(2, rows, LANES)
    if spare:
        cells = jnp.pad(cells, ((0, 0), (0, spare), (0, 0)))
    cells = cells.reshape(2, devices, rows_per, LANES).transpose(1, 0, 2, 3)
    cells = cells.reshape(devices, 2 * rows_per, LANES)
    owned = lax.all_to_all(cells, AXES, 0, 0, tiled=True)
    table, coef = prepare(own, neighbors, pair_count, emit_coup, absorb_coup, slabs, order, rows_per)
    sigma = convolve(shifts, owned, coef)
    sigma = lax.all_to_all(sigma, AXES, 0, 0, tiled=True)
    lines = 8 * slots // LANES
    if rows_per != lines:
        sigma = sigma.reshape(devices, 2, rows_per, LANES).transpose(1, 0, 2, 3)
        sigma = sigma.reshape(2, devices * rows_per, LANES)[:, :rows]
        sigma = sigma.reshape(2, rows // lines, lines, LANES).transpose(1, 0, 2, 3)
        sigma = sigma.reshape(rows // lines, 2 * lines, LANES)
    green = solve(own, sigma, table, ham_diag, ham_coup, devices)
    return green.reshape(2, 1, slabs, order, order)


def solution(mesh):
    return jax.shard_map(
        on_device,
        mesh=mesh,
        in_specs=(P(), P(), P(), P(), P(), P(None, ("freq", "atom"), None), P(), P()),
        out_specs=P(None, ("freq", "atom"), None, None, None),
        check_vma=False,
    )
```

```python
import functools

import jax
import jax.numpy as jnp
from jax import lax
from jax.experimental import pallas as pl
from jax.experimental.pallas import tpu as pltpu
from jax.sharding import PartitionSpec as P

HALO = 16
INV_STEPS = 22
EXACT_STEPS = 2

BROADEN = 0.8
ENERGY_LOW = -2.5
ENERGY_SPAN = 5.0

LANES = 128
RESIDUAL_LIMIT = 1e-5

AXES = ("freq", "atom")
VMEM = pltpu.MemorySpace.VMEM
SMEM = pltpu.MemorySpace.SMEM


def prepare_kernel(own_ref, neighbors_ref, count_ref, emit_ref, absorb_ref, table_ref, coef_ref):
    slabs, order, _ = table_ref.shape
    slots = neighbors_ref.shape[1]
    half = coef_ref.shape[3] // 2
    slot_id = lax.broadcasted_iota(jnp.int32, (slots, order), 0)
    column = lax.broadcasted_iota(jnp.int32, (order, order), 0)
    lane = lax.broadcasted_iota(jnp.int32, (order, order), 1)
    offset = lax.rem(lane, LANES // slots) * slots
    for slab in range(slabs):
        listed = neighbors_ref[slab * order : (slab + 1) * order, :].T
        listed = jnp.where(slot_id < count_ref[slab : slab + 1, :], listed, -1)
        found = jnp.full((order, order), -1, jnp.int32)
        for slot in range(slots):
            found = jnp.where(listed[slot : slot + 1, :] == column, slot, found)
        table_ref[slab] = jnp.where(found >= 0, found + offset, -1).T
    for side, weights_ref in enumerate((emit_ref, absorb_ref)):
        for row in range(half):
            lanes = slice(row * LANES, (row + 1) * LANES)
            real = weights_ref[0, :, lanes]
            imag = weights_ref[1, :, lanes]
            coef_ref[side, 0, :, row, :] = real
            coef_ref[side, 0, :, half + row, :] = real
            coef_ref[side, 1, :, row, :] = imag
            coef_ref[side, 1, :, half + row, :] = -imag


def prepare(own, neighbors, pair_count, emit_coup, absorb_coup, slabs, order, rows_per):
    modes = emit_coup.shape[1]
    blocks = emit_coup.shape[2] // (rows_per * LANES)
    weights = pl.BlockSpec(
        (2, modes, rows_per * LANES),
        lambda i, own_ref: (0, 0, jnp.minimum(own_ref[0], blocks - 1)),
    )
    whole = lambda *shape: pl.BlockSpec(shape, lambda i, own_ref: (0,) * len(shape))
    return pl.pallas_call(
        prepare_kernel,
        out_shape=(
            jax.ShapeDtypeStruct((slabs, order, order), jnp.int32),
            jax.ShapeDtypeStruct((2, 2, modes, 2 * rows_per, LANES), jnp.float32),
        ),
        grid_spec=pltpu.PrefetchScalarGridSpec(
            num_scalar_prefetch=1,
            grid=(1,),
            in_specs=[
                whole(*neighbors.shape),
                whole(slabs, order),
                weights,
                weights,
            ],
            out_specs=(
                whole(slabs, order, order),
                whole(2, 2, modes, 2 * rows_per, LANES),
            ),
        ),
        compiler_params=pltpu.CompilerParams(vmem_limit_bytes=16 * 2**20),
        name="prepare",
    )(own, neighbors, pair_count.reshape(slabs, order), emit_coup, absorb_coup)


def convolve_kernel(shifts_hbm, cells_ref, coef_ref, out_ref, padded_ref, shifts_ref, sem):
    energies, height, _ = cells_ref.shape
    modes = coef_ref.shape[2]
    half = height // 2
    copy = pltpu.make_async_copy(shifts_hbm, shifts_ref, sem)
    copy.start()
    edge = jnp.zeros((HALO, height, LANES), jnp.float32)
    padded_ref[0:HALO] = edge
    padded_ref[HALO + energies : 2 * HALO + energies] = edge
    group = 16 if energies % 16 == 0 else 1

    def load(index, carry):
        rows = pl.ds(index * group, group)
        padded_ref[pl.ds(HALO + index * group, group)] = cells_ref[rows]
        return carry

    def combine(index, carry):
        base = HALO + index * group
        direct_sum = [jnp.zeros((height, LANES), jnp.float32)] * group
        crossed_sum = list(direct_sum)
        for mode in range(modes):
            shift = shifts_ref[mode]
            for side in range(2):
                first = base + (shift if side else -shift)
                direct = coef_ref[side, 0, mode]
                crossed = coef_ref[side, 1, mode]
                for step in range(group):
                    cell = padded_ref[first + step]
                    direct_sum[step] = direct_sum[step] + direct * cell
                    crossed_sum[step] = crossed_sum[step] + crossed * cell
        for step in range(group):
            turned = jnp.concatenate([crossed_sum[step][half:], crossed_sum[step][:half]], axis=0)
            out_ref[index * group + step] = direct_sum[step] + turned
        return carry

    lax.fori_loop(0, energies // group, load, 0, unroll=energies // group <= 2)
    copy.wait()
    lax.fori_loop(0, energies // group, combine, 0, unroll=energies // group <= 2)


def convolve(shifts, cells, coef):
    energies, height, _ = cells.shape
    return pl.pallas_call(
        convolve_kernel,
        out_shape=jax.ShapeDtypeStruct(cells.shape, jnp.float32),
        in_specs=[
            pl.BlockSpec(memory_space=pl.ANY),
            pl.BlockSpec(memory_space=VMEM),
            pl.BlockSpec(memory_space=VMEM),
        ],
        out_specs=pl.BlockSpec(memory_space=VMEM),
        scratch_shapes=[
            pltpu.VMEM((energies + 2 * HALO, height, LANES), jnp.float32),
            pltpu.SMEM(shifts.shape, jnp.int32),
            pltpu.SemaphoreType.DMA,
        ],
        compiler_params=pltpu.CompilerParams(vmem_limit_bytes=16 * 2**20),
        name="convolve",
    )(shifts, cells, coef)


def embed(pair):
    order = pair.shape[1] // 2
    return jnp.concatenate(
        [pair, jnp.concatenate([-pair[:, order:], pair[:, :order]], axis=1)], axis=0
    )


def pieces(value, count):
    parts = []
    for index in range(count):
        parts.append(value.astype(jnp.bfloat16))
        if index + 1 < count:
            value = value - parts[-1].astype(jnp.float32)
    return parts


def unit_pair(order):
    row = lax.broadcasted_iota(jnp.int32, (order, 2 * order), 0)
    column = lax.broadcasted_iota(jnp.int32, (order, 2 * order), 1)
    return jnp.where(row == column, 1.0, 0.0).astype(jnp.float32)


def square_sum(pair):
    squares = pair * pair
    return jnp.sum(jnp.sum(squares, axis=0, keepdims=True), axis=1, keepdims=True)


def adjoint(pair):
    order = pair.shape[0]
    return jnp.concatenate([pair[:, :order].T, -pair[:, order:].T], axis=1)


class Multiplier:
    def __init__(self, blocks):
        self.blocks = blocks
        self.turn = 0

    def load(self, factor, transpose=False):
        stage = self.turn
        self.turn = 1 - stage
        for unit in range(2):
            pltpu.matmul_push_rhs(factor, stage, unit, transpose=transpose)
        return stage

    def feed(self, stage, *rows):
        for block, left in rows:
            half = left.shape[0] // 2
            for unit in range(2):
                pltpu.matmul_acc_lhs(
                    self.blocks[block][unit],
                    left[unit * half : (unit + 1) * half],
                    load_staged_rhs=stage,
                )
            stage = None

    def take(self, block):
        return jnp.concatenate(
            [pltpu.matmul_pop(self.blocks[block][unit]) for unit in range(2)], axis=0
        )

    def product(self, left, right, transpose=False):
        for index, factor in enumerate(right):
            stage = self.load(factor, transpose)
            self.feed(stage, *[(0, piece) for piece in left[: len(left) - index]])
        return self.take(0)


def iterate(mxu, matrix, follow, count):
    order = matrix.shape[0]
    split = pieces(matrix, 2)
    product = mxu.product(split, [embed(piece) for piece in split], transpose=True)
    scale = 1.0 / square_sum(matrix)
    x = adjoint(matrix) * scale
    y = product * scale
    for index in range(count):
        narrow = y.astype(jnp.bfloat16)
        stage = mxu.load(embed(narrow))
        mxu.feed(stage, (0, narrow))
        if index:
            x = (x - mxu.take(1)) + x
        mxu.feed(None, (1, x.astype(jnp.bfloat16)))
        y = (y - mxu.take(0)) + y
    x = (x - mxu.take(1)) + x

    high, low = pieces(x, 2)
    wide = mxu.load(embed(high))
    rest = mxu.load(embed(low))
    mxu.feed(rest, (0, split[0]), (1, follow[0]))
    mxu.feed(wide, (0, split[0]), (0, split[1]), (1, follow[0]), (1, follow[1]))
    residual = unit_pair(order) - mxu.take(0)
    t = mxu.take(1)
    r_high, r_low = pieces(residual, 2)
    t_high, t_low = pieces(t, 2)
    wide = mxu.load(embed(r_high))
    rest = mxu.load(embed(r_low))
    mxu.feed(wide, (0, r_high), (1, high), (1, low), (2, t_high), (2, t_low))
    mxu.feed(rest, (1, high), (2, t_high))
    residual = mxu.take(0)
    stage = mxu.load(embed(residual.astype(jnp.bfloat16)))
    x = x + mxu.take(1)
    t = t + mxu.take(2)
    mxu.feed(stage, (0, x.astype(jnp.bfloat16)), (1, t.astype(jnp.bfloat16)))
    return x + mxu.take(0), t + mxu.take(1), square_sum(residual)


def iterate_plain(mxu, matrix):
    split = pieces(matrix, 3)
    unit = unit_pair(matrix.shape[0])

    def step(index, x):
        right = [embed(piece) for piece in pieces(x, 3)]
        residue = 2.0 * unit - mxu.product(split, right)
        return mxu.product(pieces(x, 3), [embed(piece) for piece in pieces(residue, 3)])

    return lax.fori_loop(0, INV_STEPS, step, adjoint(matrix) * (1.0 / square_sum(matrix)))


def pick(values, index, axis):
    return jnp.take_along_axis(values, index, axis=axis, mode="promise_in_bounds")


def solve_kernel(own_ref, cells_ref, table_ref, diag_ref, coup_ref, out_ref, matrix_ref, stage_ref, sems, *, energies):
    slabs, order, _ = diag_ref.shape
    unit = unit_pair(order)
    position = jnp.full((8, LANES), own_ref[0], jnp.int32).astype(jnp.float32)
    energy = (ENERGY_LOW + ENERGY_SPAN * position / energies)[0:1, 0:1]
    row = lax.broadcasted_iota(jnp.int32, (8, LANES), 0)
    lines = cells_ref.shape[1] // 2
    line_of = row // (8 // lines)

    def assemble(slab):
        for block in range(order // 8):
            cell = cells_ref[slab * (order // 8) + block]
            rows = slice(block * 8, block * 8 + 8)
            table = table_ref[slab, rows, :]
            held = table >= 0
            lane = jnp.where(held, table, 0)
            for part in range(2):
                spread = pick(cell, line_of + part * lines, 0)
                sigma = jnp.where(held, pick(spread, lane, 1), 0.0)
                eye = unit[rows, :order]
                if part == 0:
                    entry = energy * eye - diag_ref[slab, rows, :] - sigma
                else:
                    entry = BROADEN * eye - sigma
                matrix_ref[slab, rows, part * order : (part + 1) * order] = entry

    assemble(1)
    coup = coup_ref[0]
    none = jnp.zeros_like(coup)
    coup_left = jnp.concatenate([coup, none], axis=1)
    coup_right = embed(jnp.concatenate([coup.T, none], axis=1))

    def send(slab, pair):
        for part in range(2):
            stage_ref[part, slab] = pair[:, part * order : (part + 1) * order]
            pltpu.make_async_copy(stage_ref.at[part, slab], out_ref.at[part, slab], sems.at[part, slab]).start()

    def sent():
        for slab in range(slabs):
            for part in range(2):
                pltpu.make_async_copy(stage_ref.at[part, slab], out_ref.at[part, slab], sems.at[part, slab]).wait()

    def body(*accumulators):
        mxu = Multiplier([accumulators[2 * i : 2 * i + 2] for i in range(3)])
        right = pieces(coup_right, 2)
        last, left_of, last_norm = iterate(mxu, matrix_ref[1], pieces(coup_left, 2), INV_STEPS - EXACT_STEPS)
        assemble(0)
        matrix = matrix_ref[0] - mxu.product(pieces(left_of, 2), right)
        right_of = mxu.product(pieces(last, 2), right)
        first, both, first_norm = iterate(mxu, matrix, pieces(right_of, 2), INV_STEPS - EXACT_STEPS)
        send(0, first)
        update = mxu.product(pieces(both, 2), [embed(piece) for piece in pieces(left_of, 2)])
        send(1, last + update)
        worst = jnp.maximum(last_norm, first_norm)[0, 0]
        settled = jnp.logical_and(worst <= RESIDUAL_LIMIT, last_norm[0, 0] + first_norm[0, 0] <= 2.0 * RESIDUAL_LIMIT)
        sent()

        @pl.when(jnp.logical_not(settled))
        def _():
            right = pieces(coup_right, 3)
            last = iterate_plain(mxu, matrix_ref[1])
            left_of = mxu.product(pieces(coup_left, 3), [embed(piece) for piece in pieces(last, 3)])
            right_of = mxu.product(pieces(last, 3), right)
            first = iterate_plain(mxu, matrix_ref[0] - mxu.product(pieces(left_of, 3), right))
            both = mxu.product(pieces(right_of, 3), [embed(piece) for piece in pieces(first, 3)])
            update = mxu.product(pieces(both, 3), [embed(piece) for piece in pieces(left_of, 3)])
            send(0, first)
            send(1, last + update)
            sent()

    shape = (order // 2, 2 * order)
    pl.run_scoped(body, *[pltpu.ACC(unit)(shape, jnp.float32) for _ in range(3) for unit in range(2)])


def solve(own, cells, table, ham_diag, ham_coup, energies):
    slabs, order, _ = ham_diag.shape
    vmem = pl.BlockSpec(memory_space=VMEM)
    return pl.pallas_call(
        functools.partial(solve_kernel, energies=energies),
        out_shape=jax.ShapeDtypeStruct((2, slabs, order, order), jnp.float32),
        in_specs=[pl.BlockSpec(memory_space=SMEM), vmem, vmem, vmem, vmem],
        out_specs=pl.BlockSpec(memory_space=pl.ANY),
        scratch_shapes=[
            pltpu.VMEM((slabs, order, 2 * order), jnp.float32),
            pltpu.VMEM((2, slabs, order, order), jnp.float32),
            pltpu.SemaphoreType.DMA((2, slabs)),
        ],
        compiler_params=pltpu.CompilerParams(vmem_limit_bytes=16 * 2**20),
        name="solve",
    )(own, cells, table, ham_diag, ham_coup)


def on_device(ham_diag, ham_coup, neighbors, pair_count, shifts, g_pairs, emit_coup, absorb_coup):
    slabs, order, _ = ham_diag.shape
    atoms, slots = neighbors.shape
    devices = lax.axis_size("freq") * lax.axis_size("atom")
    own = (lax.axis_index("freq") * lax.axis_size("atom") + lax.axis_index("atom")).astype(jnp.int32).reshape(1)
    rows = g_pairs.shape[2] // LANES
    rows_per = -(-rows // devices)
    spare = rows_per * devices - rows

    cells = g_pairs.reshape(2, rows, LANES)
    if spare:
        cells = jnp.pad(cells, ((0, 0), (0, spare), (0, 0)))
    cells = cells.reshape(2, devices, rows_per, LANES).transpose(1, 0, 2, 3)
    cells = cells.reshape(devices, 2 * rows_per, LANES)
    owned = lax.all_to_all(cells, AXES, 0, 0, tiled=True)
    table, coef = prepare(own, neighbors, pair_count, emit_coup, absorb_coup, slabs, order, rows_per)
    sigma = convolve(shifts, owned, coef)
    sigma = lax.all_to_all(sigma, AXES, 0, 0, tiled=True)
    lines = 8 * slots // LANES
    if rows_per != lines:
        sigma = sigma.reshape(devices, 2, rows_per, LANES).transpose(1, 0, 2, 3)
        sigma = sigma.reshape(2, devices * rows_per, LANES)[:, :rows]
        sigma = sigma.reshape(2, rows // lines, lines, LANES).transpose(1, 0, 2, 3)
        sigma = sigma.reshape(rows // lines, 2 * lines, LANES)
    green = solve(own, sigma, table, ham_diag, ham_coup, devices)
    return green.reshape(2, 1, slabs, order, order)


def solution(mesh):
    return jax.shard_map(
        on_device,
        mesh=mesh,
        in_specs=(P(), P(), P(), P(), P(), P(None, ("freq", "atom"), None), P(), P()),
        out_specs=P(None, ("freq", "atom"), None, None, None),
        check_vma=False,
    )
```

```python
import functools

import jax
import jax.numpy as jnp
from jax import lax
from jax.experimental import pallas as pl
from jax.experimental.pallas import tpu as pltpu
from jax.sharding import PartitionSpec as P

HALO = 16
INV_STEPS = 22
EXACT_STEPS = 2

BROADEN = 0.8
ENERGY_LOW = -2.5
ENERGY_SPAN = 5.0

LANES = 128
RESIDUAL_LIMIT = 2e-5

AXES = ("freq", "atom")
VMEM = pltpu.MemorySpace.VMEM
SMEM = pltpu.MemorySpace.SMEM


def prepare_kernel(
    own_ref, neighbors_hbm, count_hbm, emit_hbm, absorb_hbm, table_ref, coef_ref, neighbors_ref, count_ref, weights_ref, sems
):
    slabs, order, _ = table_ref.shape
    slots = neighbors_ref.shape[0]
    half = coef_ref.shape[3] // 2
    width = half * LANES
    block = jnp.minimum(own_ref[0], emit_hbm.shape[2] // width - 1)
    lanes = pl.ds(pl.multiple_of(block * width, LANES), width)
    copies = [
        pltpu.make_async_copy(neighbors_hbm, neighbors_ref, sems.at[0]),
        pltpu.make_async_copy(count_hbm, count_ref, sems.at[1]),
        pltpu.make_async_copy(emit_hbm.at[:, :, lanes], weights_ref.at[0], sems.at[2]),
        pltpu.make_async_copy(absorb_hbm.at[:, :, lanes], weights_ref.at[1], sems.at[3]),
    ]
    for copy in copies:
        copy.start()
    copies[0].wait()
    copies[1].wait()
    slot_id = lax.broadcasted_iota(jnp.int32, (slots, order), 0)
    column = lax.broadcasted_iota(jnp.int32, (order, order), 0)
    lane = lax.broadcasted_iota(jnp.int32, (order, order), 1)
    offset = lax.rem(lane, LANES // slots) * slots
    for slab in range(slabs):
        listed = neighbors_ref[:, slab * order : (slab + 1) * order]
        listed = jnp.where(slot_id < count_ref[slab : slab + 1, :], listed, -1)
        found = jnp.full((order, order), -1, jnp.int32)
        for slot in range(slots):
            found = jnp.where(listed[slot : slot + 1, :] == column, slot, found)
        table_ref[slab] = jnp.where(found >= 0, found + offset, -1).T
    copies[2].wait()
    copies[3].wait()
    for side in range(2):
        for row in range(half):
            part = slice(row * LANES, (row + 1) * LANES)
            real = weights_ref[side, 0, :, part]
            imag = weights_ref[side, 1, :, part]
            coef_ref[side, 0, :, row, :] = real
            coef_ref[side, 0, :, half + row, :] = real
            coef_ref[side, 1, :, row, :] = imag
            coef_ref[side, 1, :, half + row, :] = -imag


def prepare(own, neighbors, pair_count, emit_coup, absorb_coup, slabs, order, rows_per):
    modes = emit_coup.shape[1]
    atoms, slots = neighbors.shape
    arrays = (neighbors.T, pair_count.reshape(slabs, order), emit_coup, absorb_coup)
    whole = lambda *shape: pl.BlockSpec(shape, lambda i, own_ref: (0,) * len(shape))
    return pl.pallas_call(
        prepare_kernel,
        out_shape=(
            jax.ShapeDtypeStruct((slabs, order, order), jnp.int32),
            jax.ShapeDtypeStruct((2, 2, modes, 2 * rows_per, LANES), jnp.float32),
        ),
        grid_spec=pltpu.PrefetchScalarGridSpec(
            num_scalar_prefetch=1,
            grid=(1,),
            in_specs=[pl.BlockSpec(memory_space=pltpu.HBM)] * 4,
            out_specs=(
                whole(slabs, order, order),
                whole(2, 2, modes, 2 * rows_per, LANES),
            ),
            scratch_shapes=[
                pltpu.VMEM((slots, atoms), jnp.int32),
                pltpu.VMEM((slabs, order), jnp.int32),
                pltpu.VMEM((2, 2, modes, rows_per * LANES), jnp.float32),
                pltpu.SemaphoreType.DMA((4,)),
            ],
        ),
        compiler_params=pltpu.CompilerParams(vmem_limit_bytes=16 * 2**20),
        name="prepare",
    )(own, *[pltpu.with_memory_space_constraint(array, pltpu.HBM) for array in arrays])


def convolve_kernel(shifts_hbm, cells_ref, coef_ref, out_ref, padded_ref, shifts_ref, sem):
    energies, height, _ = cells_ref.shape
    modes = coef_ref.shape[2]
    half = height // 2
    copy = pltpu.make_async_copy(shifts_hbm, shifts_ref, sem)
    copy.start()
    edge = jnp.zeros((HALO, height, LANES), jnp.float32)
    padded_ref[0:HALO] = edge
    padded_ref[HALO + energies : 2 * HALO + energies] = edge
    group = 16 if energies % 16 == 0 else 1

    def load(index, carry):
        rows = pl.ds(index * group, group)
        padded_ref[pl.ds(HALO + index * group, group)] = cells_ref[rows]
        return carry

    def combine(index, carry):
        base = HALO + index * group
        direct_sum = [jnp.zeros((height, LANES), jnp.float32)] * group
        crossed_sum = list(direct_sum)
        for mode in range(modes):
            shift = shifts_ref[mode]
            for side in range(2):
                first = base + (shift if side else -shift)
                direct = coef_ref[side, 0, mode]
                crossed = coef_ref[side, 1, mode]
                for step in range(group):
                    cell = padded_ref[first + step]
                    direct_sum[step] = direct_sum[step] + direct * cell
                    crossed_sum[step] = crossed_sum[step] + crossed * cell
        for step in range(group):
            turned = jnp.concatenate([crossed_sum[step][half:], crossed_sum[step][:half]], axis=0)
            out_ref[index * group + step] = direct_sum[step] + turned
        return carry

    lax.fori_loop(0, energies // group, load, 0, unroll=energies // group <= 2)
    copy.wait()
    lax.fori_loop(0, energies // group, combine, 0, unroll=energies // group <= 2)


def convolve(shifts, cells, coef):
    energies, height, _ = cells.shape
    return pl.pallas_call(
        convolve_kernel,
        out_shape=jax.ShapeDtypeStruct(cells.shape, jnp.float32),
        in_specs=[
            pl.BlockSpec(memory_space=pl.ANY),
            pl.BlockSpec(memory_space=VMEM),
            pl.BlockSpec(memory_space=VMEM),
        ],
        out_specs=pl.BlockSpec(memory_space=VMEM),
        scratch_shapes=[
            pltpu.VMEM((energies + 2 * HALO, height, LANES), jnp.float32),
            pltpu.SMEM(shifts.shape, jnp.int32),
            pltpu.SemaphoreType.DMA,
        ],
        compiler_params=pltpu.CompilerParams(vmem_limit_bytes=16 * 2**20),
        name="convolve",
    )(shifts, cells, coef)


def embed(pair):
    order = pair.shape[1] // 2
    return jnp.concatenate(
        [pair, jnp.concatenate([-pair[:, order:], pair[:, :order]], axis=1)], axis=0
    )


def pieces(value, count):
    parts = []
    for index in range(count):
        parts.append(value.astype(jnp.bfloat16))
        if index + 1 < count:
            value = value - parts[-1].astype(jnp.float32)
    return parts


def unit_pair(order):
    row = lax.broadcasted_iota(jnp.int32, (order, 2 * order), 0)
    column = lax.broadcasted_iota(jnp.int32, (order, 2 * order), 1)
    return jnp.where(row == column, 1.0, 0.0).astype(jnp.float32)


def square_sum(pair):
    squares = pair * pair
    return jnp.sum(jnp.sum(squares, axis=0, keepdims=True), axis=1, keepdims=True)


def adjoint(pair):
    order = pair.shape[0]
    return jnp.concatenate([pair[:, :order].T, -pair[:, order:].T], axis=1)


class Multiplier:
    def __init__(self, blocks):
        self.blocks = blocks
        self.turn = 0

    def load(self, factor, transpose=False):
        stage = self.turn
        self.turn = 1 - stage
        for unit in range(2):
            pltpu.matmul_push_rhs(factor, stage, unit, transpose=transpose)
        return stage

    def feed(self, stage, *rows):
        for block, left in rows:
            half = left.shape[0] // 2
            for unit in range(2):
                pltpu.matmul_acc_lhs(
                    self.blocks[block][unit],
                    left[unit * half : (unit + 1) * half],
                    load_staged_rhs=stage,
                )
            stage = None

    def take(self, block):
        return jnp.concatenate(
            [pltpu.matmul_pop(self.blocks[block][unit]) for unit in range(2)], axis=0
        )

    def product(self, left, right, transpose=False):
        for index, factor in enumerate(right):
            stage = self.load(factor, transpose)
            self.feed(stage, *[(0, piece) for piece in left[: len(left) - index]])
        return self.take(0)


def iterate(mxu, matrix, follow, count):
    order = matrix.shape[0]
    split = pieces(matrix, 2)
    product = mxu.product(split[:1], [embed(split[0])], transpose=True)
    scale = 1.0 / square_sum(matrix)
    x = adjoint(matrix) * scale
    y = product * scale
    for index in range(count):
        narrow = y.astype(jnp.bfloat16)
        stage = mxu.load(embed(narrow))
        mxu.feed(stage, (0, narrow))
        if index:
            x = (x - mxu.take(1)) + x
        mxu.feed(None, (1, x.astype(jnp.bfloat16)))
        y = (y - mxu.take(0)) + y
    x = (x - mxu.take(1)) + x

    high, low = pieces(x, 2)
    wide = mxu.load(embed(high))
    rest = mxu.load(embed(low))
    mxu.feed(rest, (0, split[0]), (1, follow[0]))
    mxu.feed(wide, (0, split[0]), (0, split[1]), (1, follow[0]), (1, follow[1]))
    residual = unit_pair(order) - mxu.take(0)
    t = mxu.take(1)
    r_high, r_low = pieces(residual, 2)
    t_high, t_low = pieces(t, 2)
    wide = mxu.load(embed(r_high))
    rest = mxu.load(embed(r_low))
    mxu.feed(wide, (0, r_high), (2, t_high), (2, t_low), (1, high), (1, low))
    mxu.feed(rest, (2, t_high), (1, high))
    residual = mxu.take(0)
    stage = mxu.load(embed(residual.astype(jnp.bfloat16)))
    t = t + mxu.take(2)
    x = x + mxu.take(1)
    mxu.feed(stage, (1, t.astype(jnp.bfloat16)), (0, x.astype(jnp.bfloat16)))
    t = t + mxu.take(1)
    return x + mxu.take(0), t, square_sum(residual)


def iterate_plain(mxu, matrix):
    split = pieces(matrix, 3)
    unit = unit_pair(matrix.shape[0])

    def step(index, x):
        right = [embed(piece) for piece in pieces(x, 3)]
        residue = 2.0 * unit - mxu.product(split, right)
        return mxu.product(pieces(x, 3), [embed(piece) for piece in pieces(residue, 3)])

    return lax.fori_loop(0, INV_STEPS, step, adjoint(matrix) * (1.0 / square_sum(matrix)))


def pick(values, index, axis):
    return jnp.take_along_axis(values, index, axis=axis, mode="promise_in_bounds")


def solve_kernel(own_ref, cells_ref, table_ref, diag_ref, coup_ref, out_ref, matrix_ref, stage_ref, sems, *, energies):
    slabs, order, _ = diag_ref.shape
    unit = unit_pair(order)
    position = jnp.full((8, LANES), own_ref[0], jnp.int32).astype(jnp.float32)
    energy = (ENERGY_LOW + ENERGY_SPAN * position / energies)[0:1, 0:1]
    row = lax.broadcasted_iota(jnp.int32, (8, LANES), 0)
    lines = cells_ref.shape[1] // 2
    line_of = row // (8 // lines)

    def assemble(slab):
        for block in range(order // 8):
            cell = cells_ref[slab * (order // 8) + block]
            rows = slice(block * 8, block * 8 + 8)
            table = table_ref[slab, rows, :]
            held = table >= 0
            lane = jnp.where(held, table, 0)
            for part in range(2):
                spread = pick(cell, line_of + part * lines, 0)
                sigma = jnp.where(held, pick(spread, lane, 1), 0.0)
                eye = unit[rows, :order]
                if part == 0:
                    entry = energy * eye - diag_ref[slab, rows, :] - sigma
                else:
                    entry = BROADEN * eye - sigma
                matrix_ref[slab, rows, part * order : (part + 1) * order] = entry

    assemble(1)
    coup = coup_ref[0]
    none = jnp.zeros_like(coup)
    coup_left = jnp.concatenate([coup, none], axis=1)
    coup_right = embed(jnp.concatenate([coup.T, none], axis=1))

    def send(slab, pair):
        for part in range(2):
            stage_ref[part, slab] = pair[:, part * order : (part + 1) * order]
            pltpu.make_async_copy(stage_ref.at[part, slab], out_ref.at[part, slab], sems.at[part, slab]).start()

    def sent():
        for slab in range(slabs):
            for part in range(2):
                pltpu.make_async_copy(stage_ref.at[part, slab], out_ref.at[part, slab], sems.at[part, slab]).wait()

    def body(*accumulators):
        mxu = Multiplier([accumulators[2 * i : 2 * i + 2] for i in range(3)])
        right = pieces(coup_right, 2)
        last, left_of, last_norm = iterate(mxu, matrix_ref[1], pieces(coup_left, 2), INV_STEPS - EXACT_STEPS)
        assemble(0)
        matrix = matrix_ref[0] - mxu.product(pieces(left_of, 2), right)
        right_of = mxu.product(pieces(last, 2), right)
        first, both, first_norm = iterate(mxu, matrix, pieces(right_of, 2), INV_STEPS - EXACT_STEPS)
        send(0, first)
        update = mxu.product(pieces(both, 2), [embed(piece) for piece in pieces(left_of, 2)])
        send(1, last + update)
        worst = jnp.maximum(last_norm, first_norm)[0, 0]
        settled = jnp.logical_and(worst <= RESIDUAL_LIMIT, last_norm[0, 0] + first_norm[0, 0] <= 2.0 * RESIDUAL_LIMIT)
        sent()

        @pl.when(jnp.logical_not(settled))
        def _():
            right = pieces(coup_right, 3)
            last = iterate_plain(mxu, matrix_ref[1])
            left_of = mxu.product(pieces(coup_left, 3), [embed(piece) for piece in pieces(last, 3)])
            right_of = mxu.product(pieces(last, 3), right)
            first = iterate_plain(mxu, matrix_ref[0] - mxu.product(pieces(left_of, 3), right))
            both = mxu.product(pieces(right_of, 3), [embed(piece) for piece in pieces(first, 3)])
            update = mxu.product(pieces(both, 3), [embed(piece) for piece in pieces(left_of, 3)])
            send(0, first)
            send(1, last + update)
            sent()

    shape = (order // 2, 2 * order)
    pl.run_scoped(body, *[pltpu.ACC(unit)(shape, jnp.float32) for _ in range(3) for unit in range(2)])


def solve(own, cells, table, ham_diag, ham_coup, energies):
    slabs, order, _ = ham_diag.shape
    vmem = pl.BlockSpec(memory_space=VMEM)
    return pl.pallas_call(
        functools.partial(solve_kernel, energies=energies),
        out_shape=jax.ShapeDtypeStruct((2, slabs, order, order), jnp.float32),
        in_specs=[pl.BlockSpec(memory_space=SMEM), vmem, vmem, vmem, vmem],
        out_specs=pl.BlockSpec(memory_space=pl.ANY),
        scratch_shapes=[
            pltpu.VMEM((slabs, order, 2 * order), jnp.float32),
            pltpu.VMEM((2, slabs, order, order), jnp.float32),
            pltpu.SemaphoreType.DMA((2, slabs)),
        ],
        compiler_params=pltpu.CompilerParams(vmem_limit_bytes=16 * 2**20),
        name="solve",
    )(own, cells, table, ham_diag, ham_coup)


def on_device(ham_diag, ham_coup, neighbors, pair_count, shifts, g_pairs, emit_coup, absorb_coup):
    slabs, order, _ = ham_diag.shape
    atoms, slots = neighbors.shape
    devices = lax.axis_size("freq") * lax.axis_size("atom")
    own = (lax.axis_index("freq") * lax.axis_size("atom") + lax.axis_index("atom")).astype(jnp.int32).reshape(1)
    rows = g_pairs.shape[2] // LANES
    rows_per = -(-rows // devices)
    spare = rows_per * devices - rows

    cells = g_pairs.reshape(2, rows, LANES)
    if spare:
        cells = jnp.pad(cells, ((0, 0), (0, spare), (0, 0)))
    cells = cells.reshape(2, devices, rows_per, LANES).transpose(1, 0, 2, 3)
    cells = cells.reshape(devices, 2 * rows_per, LANES)
    owned = lax.all_to_all(cells, AXES, 0, 0, tiled=True)
    table, coef = prepare(own, neighbors, pair_count, emit_coup, absorb_coup, slabs, order, rows_per)
    sigma = convolve(shifts, owned, coef)
    sigma = lax.all_to_all(sigma, AXES, 0, 0, tiled=True)
    lines = 8 * slots // LANES
    if rows_per != lines:
        sigma = sigma.reshape(devices, 2, rows_per, LANES).transpose(1, 0, 2, 3)
        sigma = sigma.reshape(2, devices * rows_per, LANES)[:, :rows]
        sigma = sigma.reshape(2, rows // lines, lines, LANES).transpose(1, 0, 2, 3)
        sigma = sigma.reshape(rows // lines, 2 * lines, LANES)
    green = solve(own, sigma, table, ham_diag, ham_coup, devices)
    return green.reshape(2, 1, slabs, order, order)


def solution(mesh):
    return jax.shard_map(
        on_device,
        mesh=mesh,
        in_specs=(P(), P(), P(), P(), P(), P(None, ("freq", "atom"), None), P(), P()),
        out_specs=P(None, ("freq", "atom"), None, None, None),
        check_vma=False,
    )
```

```python
import functools

import jax
import jax.numpy as jnp
from jax import lax
from jax.experimental import pallas as pl
from jax.experimental.pallas import tpu as pltpu
from jax.sharding import PartitionSpec as P

HALO = 16
INV_STEPS = 22
EXACT_STEPS = 2

BROADEN = 0.8
ENERGY_LOW = -2.5
ENERGY_SPAN = 5.0

LANES = 128
RESIDUAL_LIMIT = 2e-5

AXES = ("freq", "atom")
VMEM = pltpu.MemorySpace.VMEM
SMEM = pltpu.MemorySpace.SMEM


def prepare_kernel(
    own_ref,
    neighbors_hbm,
    count_hbm,
    shifts_hbm,
    emit_hbm,
    absorb_hbm,
    table_ref,
    coef_ref,
    steps_ref,
    energy_ref,
    neighbors_ref,
    count_ref,
    shifts_ref,
    weights_ref,
    sems,
    *,
    energies,
):
    slabs, order, _ = table_ref.shape
    slots = neighbors_ref.shape[0]
    half = coef_ref.shape[3] // 2
    width = half * LANES
    block = jnp.minimum(own_ref[0], emit_hbm.shape[2] // width - 1)
    lanes = pl.ds(pl.multiple_of(block * width, LANES), width)
    copies = [
        pltpu.make_async_copy(neighbors_hbm, neighbors_ref, sems.at[0]),
        pltpu.make_async_copy(count_hbm, count_ref, sems.at[1]),
        pltpu.make_async_copy(emit_hbm.at[:, :, lanes], weights_ref.at[0], sems.at[2]),
        pltpu.make_async_copy(absorb_hbm.at[:, :, lanes], weights_ref.at[1], sems.at[3]),
        pltpu.make_async_copy(shifts_hbm, shifts_ref, sems.at[4]),
    ]
    for copy in copies:
        copy.start()
    position = jnp.full(energy_ref.shape, own_ref[0], jnp.int32).astype(jnp.float32)
    energy_ref[...] = ENERGY_LOW + ENERGY_SPAN * position / energies
    copies[0].wait()
    copies[1].wait()
    slot_id = lax.broadcasted_iota(jnp.int32, (slots, order), 0)
    column = lax.broadcasted_iota(jnp.int32, (order, order), 0)
    lane = lax.broadcasted_iota(jnp.int32, (order, order), 1)
    offset = lax.rem(lane, LANES // slots) * slots
    for slab in range(slabs):
        listed = neighbors_ref[:, slab * order : (slab + 1) * order]
        listed = jnp.where(slot_id < count_ref[slab : slab + 1, :], listed, -1)
        found = jnp.full((order, order), -1, jnp.int32)
        for slot in range(slots):
            found = jnp.where(listed[slot : slot + 1, :] == column, slot, found)
        table_ref[slab] = jnp.where(found >= 0, found + offset, -1).T
    for copy in copies[2:]:
        copy.wait()
    for mode in range(steps_ref.shape[0]):
        steps_ref[mode] = jnp.full(steps_ref.shape[1:], shifts_ref[mode], jnp.int32)
    for side in range(2):
        for row in range(half):
            part = slice(row * LANES, (row + 1) * LANES)
            real = weights_ref[side, 0, :, part]
            imag = weights_ref[side, 1, :, part]
            coef_ref[side, 0, :, row, :] = real
            coef_ref[side, 0, :, half + row, :] = real
            coef_ref[side, 1, :, row, :] = imag
            coef_ref[side, 1, :, half + row, :] = -imag


def prepare(own, neighbors, pair_count, shifts, emit_coup, absorb_coup, slabs, order, rows_per, energies):
    modes = emit_coup.shape[1]
    atoms, slots = neighbors.shape
    arrays = (neighbors.T, pair_count.reshape(slabs, order), shifts, emit_coup, absorb_coup)
    whole = lambda *shape: pl.BlockSpec(shape, lambda i, own_ref: (0,) * len(shape))
    return pl.pallas_call(
        functools.partial(prepare_kernel, energies=energies),
        out_shape=(
            jax.ShapeDtypeStruct((slabs, order, order), jnp.int32),
            jax.ShapeDtypeStruct((2, 2, modes, 2 * rows_per, LANES), jnp.float32),
            jax.ShapeDtypeStruct((modes, 8, LANES), jnp.int32),
            jax.ShapeDtypeStruct((8, LANES), jnp.float32),
        ),
        grid_spec=pltpu.PrefetchScalarGridSpec(
            num_scalar_prefetch=1,
            grid=(1,),
            in_specs=[pl.BlockSpec(memory_space=pltpu.HBM)] * 5,
            out_specs=(
                whole(slabs, order, order),
                whole(2, 2, modes, 2 * rows_per, LANES),
                whole(modes, 8, LANES),
                whole(8, LANES),
            ),
            scratch_shapes=[
                pltpu.VMEM((slots, atoms), jnp.int32),
                pltpu.VMEM((slabs, order), jnp.int32),
                pltpu.SMEM((modes,), jnp.int32),
                pltpu.VMEM((2, 2, modes, rows_per * LANES), jnp.float32),
                pltpu.SemaphoreType.DMA((5,)),
            ],
        ),
        compiler_params=pltpu.CompilerParams(vmem_limit_bytes=16 * 2**20),
        name="prepare",
    )(own, *[pltpu.with_memory_space_constraint(array, pltpu.HBM) for array in arrays])


def convolve_kernel(steps_ref, cells_ref, coef_ref, out_ref, padded_ref):
    energies, height, _ = cells_ref.shape
    modes = coef_ref.shape[2]
    half = height // 2
    shifts = [steps_ref[mode][0, 0] for mode in range(modes)]
    edge = jnp.zeros((HALO, height, LANES), jnp.float32)
    padded_ref[0:HALO] = edge
    padded_ref[HALO + energies : 2 * HALO + energies] = edge
    group = 16 if energies % 16 == 0 else 1

    def load(index, carry):
        rows = pl.ds(index * group, group)
        padded_ref[pl.ds(HALO + index * group, group)] = cells_ref[rows]
        return carry

    def combine(index, carry):
        base = HALO + index * group
        direct_sum = [jnp.zeros((height, LANES), jnp.float32)] * group
        crossed_sum = list(direct_sum)
        for mode in range(modes):
            shift = shifts[mode]
            for side in range(2):
                first = base + (shift if side else -shift)
                direct = coef_ref[side, 0, mode]
                crossed = coef_ref[side, 1, mode]
                for step in range(group):
                    cell = padded_ref[first + step]
                    direct_sum[step] = direct_sum[step] + direct * cell
                    crossed_sum[step] = crossed_sum[step] + crossed * cell
        for step in range(group):
            turned = jnp.concatenate([crossed_sum[step][half:], crossed_sum[step][:half]], axis=0)
            out_ref[index * group + step] = direct_sum[step] + turned
        return carry

    lax.fori_loop(0, energies // group, load, 0, unroll=energies // group <= 2)
    lax.fori_loop(0, energies // group, combine, 0, unroll=energies // group <= 2)


def convolve(steps, cells, coef):
    energies, height, _ = cells.shape
    vmem = pl.BlockSpec(memory_space=VMEM)
    return pl.pallas_call(
        convolve_kernel,
        out_shape=jax.ShapeDtypeStruct(cells.shape, jnp.float32),
        in_specs=[vmem, vmem, vmem],
        out_specs=vmem,
        scratch_shapes=[pltpu.VMEM((energies + 2 * HALO, height, LANES), jnp.float32)],
        compiler_params=pltpu.CompilerParams(vmem_limit_bytes=16 * 2**20),
        name="convolve",
    )(steps, cells, coef)


def embed(pair):
    order = pair.shape[1] // 2
    return jnp.concatenate(
        [pair, jnp.concatenate([-pair[:, order:], pair[:, :order]], axis=1)], axis=0
    )


def pieces(value, count):
    parts = []
    for index in range(count):
        parts.append(value.astype(jnp.bfloat16))
        if index + 1 < count:
            value = value - parts[-1].astype(jnp.float32)
    return parts


def unit_pair(order):
    row = lax.broadcasted_iota(jnp.int32, (order, 2 * order), 0)
    column = lax.broadcasted_iota(jnp.int32, (order, 2 * order), 1)
    return jnp.where(row == column, 1.0, 0.0).astype(jnp.float32)


def square_sum(pair):
    squares = pair * pair
    return jnp.sum(jnp.sum(squares, axis=0, keepdims=True), axis=1, keepdims=True)


def adjoint(pair):
    order = pair.shape[0]
    return jnp.concatenate([pair[:, :order].T, -pair[:, order:].T], axis=1)


class Multiplier:
    def __init__(self, blocks):
        self.blocks = blocks
        self.turn = 0

    def load(self, factor, transpose=False):
        stage = self.turn
        self.turn = 1 - stage
        for unit in range(2):
            pltpu.matmul_push_rhs(factor, stage, unit, transpose=transpose)
        return stage

    def feed(self, stage, *rows):
        for block, left in rows:
            half = left.shape[0] // 2
            for unit in range(2):
                pltpu.matmul_acc_lhs(
                    self.blocks[block][unit],
                    left[unit * half : (unit + 1) * half],
                    load_staged_rhs=stage,
                )
            stage = None

    def take(self, block):
        return jnp.concatenate(
            [pltpu.matmul_pop(self.blocks[block][unit]) for unit in range(2)], axis=0
        )

    def product(self, left, right, transpose=False):
        for index, factor in enumerate(right):
            stage = self.load(factor, transpose)
            self.feed(stage, *[(0, piece) for piece in left[: len(left) - index]])
        return self.take(0)


def iterate(mxu, matrix, follow, count):
    order = matrix.shape[0]
    split = pieces(matrix, 2)
    product = mxu.product(split[:1], [embed(split[0])], transpose=True)
    scale = 1.0 / square_sum(matrix)
    x = adjoint(matrix) * scale
    y = product * scale
    for index in range(count):
        narrow = y.astype(jnp.bfloat16)
        stage = mxu.load(embed(narrow))
        mxu.feed(stage, (0, narrow))
        if index:
            x = (x - mxu.take(1)) + x
        mxu.feed(None, (1, x.astype(jnp.bfloat16)))
        y = (y - mxu.take(0)) + y
    x = (x - mxu.take(1)) + x

    high, low = pieces(x, 2)
    wide = mxu.load(embed(high))
    rest = mxu.load(embed(low))
    mxu.feed(rest, (0, split[0]), (1, follow[0]))
    mxu.feed(wide, (0, split[0]), (0, split[1]), (1, follow[0]), (1, follow[1]))
    residual = unit_pair(order) - mxu.take(0)
    t = mxu.take(1)
    r_high, r_low = pieces(residual, 2)
    t_high, t_low = pieces(t, 2)
    wide = mxu.load(embed(r_high))
    rest = mxu.load(embed(r_low))
    mxu.feed(wide, (0, r_high), (2, t_high), (2, t_low), (1, high), (1, low))
    mxu.feed(rest, (2, t_high), (1, high))
    residual = mxu.take(0)
    stage = mxu.load(embed(residual.astype(jnp.bfloat16)))
    t = t + mxu.take(2)
    x = x + mxu.take(1)
    mxu.feed(stage, (1, t.astype(jnp.bfloat16)), (0, x.astype(jnp.bfloat16)))
    t = t + mxu.take(1)
    return x + mxu.take(0), t, square_sum(residual)


def iterate_plain(mxu, matrix):
    split = pieces(matrix, 3)
    unit = unit_pair(matrix.shape[0])

    def step(index, x):
        right = [embed(piece) for piece in pieces(x, 3)]
        residue = 2.0 * unit - mxu.product(split, right)
        return mxu.product(pieces(x, 3), [embed(piece) for piece in pieces(residue, 3)])

    return lax.fori_loop(0, INV_STEPS, step, adjoint(matrix) * (1.0 / square_sum(matrix)))


def pick(values, index, axis):
    return jnp.take_along_axis(values, index, axis=axis, mode="promise_in_bounds")


def solve_kernel(energy_ref, cells_ref, table_ref, diag_ref, coup_ref, out_ref, matrix_ref, stage_ref, sems):
    slabs, order, _ = diag_ref.shape
    unit = unit_pair(order)
    energy = energy_ref[...]
    row = lax.broadcasted_iota(jnp.int32, (8, LANES), 0)
    lines = cells_ref.shape[1] // 2
    line_of = row // (8 // lines)

    def assemble(slab):
        for block in range(order // 8):
            cell = cells_ref[slab * (order // 8) + block]
            rows = slice(block * 8, block * 8 + 8)
            table = table_ref[slab, rows, :]
            held = table >= 0
            lane = jnp.where(held, table, 0)
            for part in range(2):
                spread = pick(cell, line_of + part * lines, 0)
                sigma = jnp.where(held, pick(spread, lane, 1), 0.0)
                eye = unit[rows, :order]
                if part == 0:
                    entry = energy * eye - diag_ref[slab, rows, :] - sigma
                else:
                    entry = BROADEN * eye - sigma
                matrix_ref[slab, rows, part * order : (part + 1) * order] = entry

    assemble(1)
    coup = coup_ref[0]
    none = jnp.zeros_like(coup)
    coup_left = jnp.concatenate([coup, none], axis=1)
    coup_right = embed(jnp.concatenate([coup.T, none], axis=1))

    def send(slab, pair):
        for part in range(2):
            stage_ref[part, slab] = pair[:, part * order : (part + 1) * order]
            pltpu.make_async_copy(stage_ref.at[part, slab], out_ref.at[part, slab], sems.at[part, slab]).start()

    def sent():
        for slab in range(slabs):
            for part in range(2):
                pltpu.make_async_copy(stage_ref.at[part, slab], out_ref.at[part, slab], sems.at[part, slab]).wait()

    def body(*accumulators):
        mxu = Multiplier([accumulators[2 * i : 2 * i + 2] for i in range(3)])
        right = pieces(coup_right, 2)
        last, left_of, last_norm = iterate(mxu, matrix_ref[1], pieces(coup_left, 2), INV_STEPS - EXACT_STEPS)
        assemble(0)
        matrix = matrix_ref[0] - mxu.product(pieces(left_of, 2), right)
        right_of = mxu.product(pieces(last, 2), right)
        first, both, first_norm = iterate(mxu, matrix, pieces(right_of, 2), INV_STEPS - EXACT_STEPS)
        send(0, first)
        update = mxu.product(pieces(both, 2), [embed(piece) for piece in pieces(left_of, 2)])
        send(1, last + update)
        worst = jnp.maximum(last_norm, first_norm)[0, 0]
        settled = jnp.logical_and(worst <= RESIDUAL_LIMIT, last_norm[0, 0] + first_norm[0, 0] <= 2.0 * RESIDUAL_LIMIT)
        sent()

        @pl.when(jnp.logical_not(settled))
        def _():
            right = pieces(coup_right, 3)
            last = iterate_plain(mxu, matrix_ref[1])
            left_of = mxu.product(pieces(coup_left, 3), [embed(piece) for piece in pieces(last, 3)])
            right_of = mxu.product(pieces(last, 3), right)
            first = iterate_plain(mxu, matrix_ref[0] - mxu.product(pieces(left_of, 3), right))
            both = mxu.product(pieces(right_of, 3), [embed(piece) for piece in pieces(first, 3)])
            update = mxu.product(pieces(both, 3), [embed(piece) for piece in pieces(left_of, 3)])
            send(0, first)
            send(1, last + update)
            sent()

    shape = (order // 2, 2 * order)
    pl.run_scoped(body, *[pltpu.ACC(unit)(shape, jnp.float32) for _ in range(3) for unit in range(2)])


def solve(energy, cells, table, ham_diag, ham_coup):
    slabs, order, _ = ham_diag.shape
    vmem = pl.BlockSpec(memory_space=VMEM)
    return pl.pallas_call(
        solve_kernel,
        out_shape=jax.ShapeDtypeStruct((2, slabs, order, order), jnp.float32),
        in_specs=[vmem] * 5,
        out_specs=pl.BlockSpec(memory_space=pl.ANY),
        scratch_shapes=[
            pltpu.VMEM((slabs, order, 2 * order), jnp.float32),
            pltpu.VMEM((2, slabs, order, order), jnp.float32),
            pltpu.SemaphoreType.DMA((2, slabs)),
        ],
        compiler_params=pltpu.CompilerParams(vmem_limit_bytes=16 * 2**20),
        name="solve",
    )(energy, cells, table, ham_diag, ham_coup)


def on_device(ham_diag, ham_coup, neighbors, pair_count, shifts, g_pairs, emit_coup, absorb_coup):
    slabs, order, _ = ham_diag.shape
    atoms, slots = neighbors.shape
    devices = lax.axis_size("freq") * lax.axis_size("atom")
    own = (lax.axis_index("freq") * lax.axis_size("atom") + lax.axis_index("atom")).astype(jnp.int32).reshape(1)
    rows = g_pairs.shape[2] // LANES
    rows_per = -(-rows // devices)
    spare = rows_per * devices - rows

    cells = g_pairs.reshape(2, rows, LANES)
    if spare:
        cells = jnp.pad(cells, ((0, 0), (0, spare), (0, 0)))
    cells = cells.reshape(2, devices, rows_per, LANES).transpose(1, 0, 2, 3)
    cells = cells.reshape(devices, 2 * rows_per, LANES)
    owned = lax.all_to_all(cells, AXES, 0, 0, tiled=True)
    table, coef, steps, energy = prepare(
        own, neighbors, pair_count, shifts, emit_coup, absorb_coup, slabs, order, rows_per, devices
    )
    sigma = convolve(steps, owned, coef)
    sigma = lax.all_to_all(sigma, AXES, 0, 0, tiled=True)
    lines = 8 * slots // LANES
    if rows_per != lines:
        sigma = sigma.reshape(devices, 2, rows_per, LANES).transpose(1, 0, 2, 3)
        sigma = sigma.reshape(2, devices * rows_per, LANES)[:, :rows]
        sigma = sigma.reshape(2, rows // lines, lines, LANES).transpose(1, 0, 2, 3)
        sigma = sigma.reshape(rows // lines, 2 * lines, LANES)
    green = solve(energy, sigma, table, ham_diag, ham_coup)
    return green.reshape(2, 1, slabs, order, order)


def solution(mesh):
    return jax.shard_map(
        on_device,
        mesh=mesh,
        in_specs=(P(), P(), P(), P(), P(), P(None, ("freq", "atom"), None), P(), P()),
        out_specs=P(None, ("freq", "atom"), None, None, None),
        check_vma=False,
    )
```

```python
import functools

import jax
import jax.numpy as jnp
from jax import lax
from jax.experimental import pallas as pl
from jax.experimental.pallas import tpu as pltpu
from jax.sharding import PartitionSpec as P

HALO = 16
INV_STEPS = 22
EXACT_STEPS = 2

BROADEN = 0.8
ENERGY_LOW = -2.5
ENERGY_SPAN = 5.0

LANES = 128
RESIDUAL_LIMIT = 2e-5

AXES = ("freq", "atom")
VMEM = pltpu.MemorySpace.VMEM
SMEM = pltpu.MemorySpace.SMEM


def prepare_kernel(
    cells_hbm,
    neighbors_hbm,
    count_hbm,
    shifts_hbm,
    emit_hbm,
    absorb_hbm,
    cells_ref,
    table_ref,
    coef_ref,
    steps_ref,
    energy_ref,
    neighbors_ref,
    count_ref,
    shifts_ref,
    weights_ref,
    sems,
    *,
    energies,
):
    own = lax.axis_index("freq") * lax.axis_size("atom") + lax.axis_index("atom")
    slabs, order, _ = table_ref.shape
    slots = neighbors_ref.shape[0]
    half = coef_ref.shape[3] // 2
    width = half * LANES
    block = jnp.minimum(own, emit_hbm.shape[2] // width - 1)
    lanes = pl.ds(pl.multiple_of(block * width, LANES), width)
    copies = [
        pltpu.make_async_copy(neighbors_hbm, neighbors_ref, sems.at[0]),
        pltpu.make_async_copy(count_hbm, count_ref, sems.at[1]),
        pltpu.make_async_copy(emit_hbm.at[:, :, lanes], weights_ref.at[0], sems.at[2]),
        pltpu.make_async_copy(absorb_hbm.at[:, :, lanes], weights_ref.at[1], sems.at[3]),
        pltpu.make_async_copy(shifts_hbm, shifts_ref, sems.at[4]),
    ]
    lines = cells_hbm.shape[2]
    for part in range(cells_hbm.shape[0]):
        rows = slice(part * lines, (part + 1) * lines)
        copies.append(pltpu.make_async_copy(cells_hbm.at[part], cells_ref.at[:, rows, :], sems.at[5 + part]))
    for copy in copies:
        copy.start()
    position = jnp.full(energy_ref.shape, own, jnp.int32).astype(jnp.float32)
    energy_ref[...] = ENERGY_LOW + ENERGY_SPAN * position / energies
    copies[0].wait()
    copies[1].wait()
    slot_id = lax.broadcasted_iota(jnp.int32, (slots, order), 0)
    column = lax.broadcasted_iota(jnp.int32, (order, order), 0)
    lane = lax.broadcasted_iota(jnp.int32, (order, order), 1)
    offset = lax.rem(lane, LANES // slots) * slots
    for slab in range(slabs):
        listed = neighbors_ref[:, slab * order : (slab + 1) * order]
        listed = jnp.where(slot_id < count_ref[slab : slab + 1, :], listed, -1)
        found = jnp.full((order, order), -1, jnp.int32)
        for slot in range(slots):
            found = jnp.where(listed[slot : slot + 1, :] == column, slot, found)
        table_ref[slab] = jnp.where(found >= 0, found + offset, -1).T
    for copy in copies[2:5]:
        copy.wait()
    for mode in range(steps_ref.shape[0]):
        steps_ref[mode] = jnp.full(steps_ref.shape[1:], shifts_ref[mode], jnp.int32)
    for side in range(2):
        for row in range(half):
            part = slice(row * LANES, (row + 1) * LANES)
            real = weights_ref[side, 0, :, part]
            imag = weights_ref[side, 1, :, part]
            coef_ref[side, 0, :, row, :] = real
            coef_ref[side, 0, :, half + row, :] = real
            coef_ref[side, 1, :, row, :] = imag
            coef_ref[side, 1, :, half + row, :] = -imag
    for copy in copies[5:]:
        copy.wait()


def prepare(cells, neighbors, pair_count, shifts, emit_coup, absorb_coup, slabs, order):
    parts, devices, rows_per, _ = cells.shape
    modes = emit_coup.shape[1]
    atoms, slots = neighbors.shape
    arrays = (cells, neighbors.T, pair_count.reshape(slabs, order), shifts, emit_coup, absorb_coup)
    return pl.pallas_call(
        functools.partial(prepare_kernel, energies=devices),
        out_shape=(
            jax.ShapeDtypeStruct((devices, parts * rows_per, LANES), jnp.float32),
            jax.ShapeDtypeStruct((slabs, order, order), jnp.int32),
            jax.ShapeDtypeStruct((2, 2, modes, 2 * rows_per, LANES), jnp.float32),
            jax.ShapeDtypeStruct((modes, 8, LANES), jnp.int32),
            jax.ShapeDtypeStruct((8, LANES), jnp.float32),
        ),
        in_specs=[pl.BlockSpec(memory_space=pltpu.HBM)] * 6,
        out_specs=(pl.BlockSpec(memory_space=VMEM),) * 5,
        scratch_shapes=[
            pltpu.VMEM((slots, atoms), jnp.int32),
            pltpu.VMEM((slabs, order), jnp.int32),
            pltpu.SMEM((modes,), jnp.int32),
            pltpu.VMEM((2, 2, modes, rows_per * LANES), jnp.float32),
            pltpu.SemaphoreType.DMA((7,)),
        ],
        compiler_params=pltpu.CompilerParams(vmem_limit_bytes=16 * 2**20),
        name="prepare",
    )(*[pltpu.with_memory_space_constraint(array, pltpu.HBM) for array in arrays])


def convolve_kernel(steps_ref, cells_ref, coef_ref, out_ref, padded_ref):
    energies, height, _ = cells_ref.shape
    modes = coef_ref.shape[2]
    half = height // 2
    shifts = [steps_ref[mode][0, 0] for mode in range(modes)]
    edge = jnp.zeros((HALO, height, LANES), jnp.float32)
    padded_ref[0:HALO] = edge
    padded_ref[HALO + energies : 2 * HALO + energies] = edge
    group = 16 if energies % 16 == 0 else 1

    def load(index, carry):
        rows = pl.ds(index * group, group)
        padded_ref[pl.ds(HALO + index * group, group)] = cells_ref[rows]
        return carry

    def combine(index, carry):
        base = HALO + index * group
        direct_sum = [jnp.zeros((height, LANES), jnp.float32)] * group
        crossed_sum = list(direct_sum)
        for mode in range(modes):
            shift = shifts[mode]
            for side in range(2):
                first = base + (shift if side else -shift)
                direct = coef_ref[side, 0, mode]
                crossed = coef_ref[side, 1, mode]
                for step in range(group):
                    cell = padded_ref[first + step]
                    direct_sum[step] = direct_sum[step] + direct * cell
                    crossed_sum[step] = crossed_sum[step] + crossed * cell
        for step in range(group):
            turned = jnp.concatenate([crossed_sum[step][half:], crossed_sum[step][:half]], axis=0)
            out_ref[index * group + step] = direct_sum[step] + turned
        return carry

    lax.fori_loop(0, energies // group, load, 0, unroll=energies // group <= 2)
    lax.fori_loop(0, energies // group, combine, 0, unroll=energies // group <= 2)


def convolve(steps, cells, coef):
    energies, height, _ = cells.shape
    vmem = pl.BlockSpec(memory_space=VMEM)
    return pl.pallas_call(
        convolve_kernel,
        out_shape=jax.ShapeDtypeStruct(cells.shape, jnp.float32),
        in_specs=[vmem, vmem, vmem],
        out_specs=vmem,
        scratch_shapes=[pltpu.VMEM((energies + 2 * HALO, height, LANES), jnp.float32)],
        compiler_params=pltpu.CompilerParams(vmem_limit_bytes=16 * 2**20),
        name="convolve",
    )(steps, cells, coef)


def embed(pair):
    order = pair.shape[1] // 2
    return jnp.concatenate(
        [pair, jnp.concatenate([-pair[:, order:], pair[:, :order]], axis=1)], axis=0
    )


def pieces(value, count):
    parts = []
    for index in range(count):
        parts.append(value.astype(jnp.bfloat16))
        if index + 1 < count:
            value = value - parts[-1].astype(jnp.float32)
    return parts


def unit_pair(order):
    row = lax.broadcasted_iota(jnp.int32, (order, 2 * order), 0)
    column = lax.broadcasted_iota(jnp.int32, (order, 2 * order), 1)
    return jnp.where(row == column, 1.0, 0.0).astype(jnp.float32)


def square_sum(pair):
    squares = pair * pair
    return jnp.sum(jnp.sum(squares, axis=0, keepdims=True), axis=1, keepdims=True)


def adjoint(pair):
    order = pair.shape[0]
    return jnp.concatenate([pair[:, :order].T, -pair[:, order:].T], axis=1)


class Multiplier:
    def __init__(self, blocks):
        self.blocks = blocks
        self.turn = 0

    def load(self, factor, transpose=False):
        stage = self.turn
        self.turn = 1 - stage
        for unit in range(2):
            pltpu.matmul_push_rhs(factor, stage, unit, transpose=transpose)
        return stage

    def feed(self, stage, *rows):
        for block, left in rows:
            half = left.shape[0] // 2
            for unit in range(2):
                pltpu.matmul_acc_lhs(
                    self.blocks[block][unit],
                    left[unit * half : (unit + 1) * half],
                    load_staged_rhs=stage,
                )
            stage = None

    def take(self, block):
        return jnp.concatenate(
            [pltpu.matmul_pop(self.blocks[block][unit]) for unit in range(2)], axis=0
        )

    def product(self, left, right, transpose=False):
        for index, factor in enumerate(right):
            stage = self.load(factor, transpose)
            self.feed(stage, *[(0, piece) for piece in left[: len(left) - index]])
        return self.take(0)


def iterate(mxu, matrix, follow, count):
    order = matrix.shape[0]
    split = pieces(matrix, 2)
    product = mxu.product(split[:1], [embed(split[0])], transpose=True)
    scale = 1.0 / square_sum(matrix)
    x = adjoint(matrix) * scale
    y = product * scale
    for index in range(count):
        narrow = y.astype(jnp.bfloat16)
        stage = mxu.load(embed(narrow))
        mxu.feed(stage, (0, narrow))
        if index:
            x = (x - mxu.take(1)) + x
        mxu.feed(None, (1, x.astype(jnp.bfloat16)))
        y = (y - mxu.take(0)) + y
    x = (x - mxu.take(1)) + x

    high, low = pieces(x, 2)
    wide = mxu.load(embed(high))
    rest = mxu.load(embed(low))
    mxu.feed(rest, (0, split[0]), (1, follow[0]))
    mxu.feed(wide, (0, split[0]), (0, split[1]), (1, follow[0]), (1, follow[1]))
    residual = unit_pair(order) - mxu.take(0)
    t = mxu.take(1)
    r_high, r_low = pieces(residual, 2)
    t_high, t_low = pieces(t, 2)
    wide = mxu.load(embed(r_high))
    rest = mxu.load(embed(r_low))
    mxu.feed(wide, (0, r_high), (2, t_high), (2, t_low), (1, high), (1, low))
    mxu.feed(rest, (2, t_high), (1, high))
    residual = mxu.take(0)
    stage = mxu.load(embed(residual.astype(jnp.bfloat16)))
    t = t + mxu.take(2)
    x = x + mxu.take(1)
    mxu.feed(stage, (1, t.astype(jnp.bfloat16)), (0, x.astype(jnp.bfloat16)))
    t = t + mxu.take(1)
    return x + mxu.take(0), t, square_sum(residual)


def iterate_plain(mxu, matrix):
    split = pieces(matrix, 3)
    unit = unit_pair(matrix.shape[0])

    def step(index, x):
        right = [embed(piece) for piece in pieces(x, 3)]
        residue = 2.0 * unit - mxu.product(split, right)
        return mxu.product(pieces(x, 3), [embed(piece) for piece in pieces(residue, 3)])

    return lax.fori_loop(0, INV_STEPS, step, adjoint(matrix) * (1.0 / square_sum(matrix)))


def pick(values, index, axis):
    return jnp.take_along_axis(values, index, axis=axis, mode="promise_in_bounds")


def solve_kernel(energy_ref, cells_ref, table_ref, diag_ref, coup_ref, out_ref, matrix_ref, stage_ref, sems):
    slabs, order, _ = diag_ref.shape
    unit = unit_pair(order)
    energy = energy_ref[...]
    row = lax.broadcasted_iota(jnp.int32, (8, LANES), 0)
    lines = cells_ref.shape[1] // 2
    line_of = row // (8 // lines)

    def assemble(slab):
        for block in range(order // 8):
            cell = cells_ref[slab * (order // 8) + block]
            rows = slice(block * 8, block * 8 + 8)
            table = table_ref[slab, rows, :]
            held = table >= 0
            lane = jnp.where(held, table, 0)
            for part in range(2):
                spread = pick(cell, line_of + part * lines, 0)
                sigma = jnp.where(held, pick(spread, lane, 1), 0.0)
                eye = unit[rows, :order]
                if part == 0:
                    entry = energy * eye - diag_ref[slab, rows, :] - sigma
                else:
                    entry = BROADEN * eye - sigma
                matrix_ref[slab, rows, part * order : (part + 1) * order] = entry

    assemble(1)
    coup = coup_ref[0]
    none = jnp.zeros_like(coup)
    coup_left = jnp.concatenate([coup, none], axis=1)
    coup_right = embed(jnp.concatenate([coup.T, none], axis=1))

    def send(slab, pair):
        for part in range(2):
            stage_ref[part, slab] = pair[:, part * order : (part + 1) * order]
            pltpu.make_async_copy(stage_ref.at[part, slab], out_ref.at[part, slab], sems.at[part, slab]).start()

    def sent():
        for slab in range(slabs):
            for part in range(2):
                pltpu.make_async_copy(stage_ref.at[part, slab], out_ref.at[part, slab], sems.at[part, slab]).wait()

    def body(*accumulators):
        mxu = Multiplier([accumulators[2 * i : 2 * i + 2] for i in range(3)])
        right = pieces(coup_right, 2)
        last, left_of, last_norm = iterate(mxu, matrix_ref[1], pieces(coup_left, 2), INV_STEPS - EXACT_STEPS)
        assemble(0)
        matrix = matrix_ref[0] - mxu.product(pieces(left_of, 2), right)
        right_of = mxu.product(pieces(last, 2), right)
        first, both, first_norm = iterate(mxu, matrix, pieces(right_of, 2), INV_STEPS - EXACT_STEPS)
        send(0, first)
        update = mxu.product(pieces(both, 2), [embed(piece) for piece in pieces(left_of, 2)])
        send(1, last + update)
        worst = jnp.maximum(last_norm, first_norm)[0, 0]
        settled = jnp.logical_and(worst <= RESIDUAL_LIMIT, last_norm[0, 0] + first_norm[0, 0] <= 2.0 * RESIDUAL_LIMIT)
        sent()

        @pl.when(jnp.logical_not(settled))
        def _():
            right = pieces(coup_right, 3)
            last = iterate_plain(mxu, matrix_ref[1])
            left_of = mxu.product(pieces(coup_left, 3), [embed(piece) for piece in pieces(last, 3)])
            right_of = mxu.product(pieces(last, 3), right)
            first = iterate_plain(mxu, matrix_ref[0] - mxu.product(pieces(left_of, 3), right))
            both = mxu.product(pieces(right_of, 3), [embed(piece) for piece in pieces(first, 3)])
            update = mxu.product(pieces(both, 3), [embed(piece) for piece in pieces(left_of, 3)])
            send(0, first)
            send(1, last + update)
            sent()

    shape = (order // 2, 2 * order)
    pl.run_scoped(body, *[pltpu.ACC(unit)(shape, jnp.float32) for _ in range(3) for unit in range(2)])


def solve(energy, cells, table, ham_diag, ham_coup):
    slabs, order, _ = ham_diag.shape
    vmem = pl.BlockSpec(memory_space=VMEM)
    return pl.pallas_call(
        solve_kernel,
        out_shape=jax.ShapeDtypeStruct((2, slabs, order, order), jnp.float32),
        in_specs=[vmem] * 5,
        out_specs=pl.BlockSpec(memory_space=pl.ANY),
        scratch_shapes=[
            pltpu.VMEM((slabs, order, 2 * order), jnp.float32),
            pltpu.VMEM((2, slabs, order, order), jnp.float32),
            pltpu.SemaphoreType.DMA((2, slabs)),
        ],
        compiler_params=pltpu.CompilerParams(vmem_limit_bytes=16 * 2**20),
        name="solve",
    )(energy, cells, table, ham_diag, ham_coup)


def on_device(ham_diag, ham_coup, neighbors, pair_count, shifts, g_pairs, emit_coup, absorb_coup):
    slabs, order, _ = ham_diag.shape
    atoms, slots = neighbors.shape
    devices = lax.axis_size("freq") * lax.axis_size("atom")
    rows = g_pairs.shape[2] // LANES
    rows_per = -(-rows // devices)
    spare = rows_per * devices - rows

    cells = g_pairs.reshape(2, rows, LANES)
    if spare:
        cells = jnp.pad(cells, ((0, 0), (0, spare), (0, 0)))
    cells, table, coef, steps, energy = prepare(
        cells.reshape(2, devices, rows_per, LANES), neighbors, pair_count, shifts, emit_coup, absorb_coup, slabs, order
    )
    owned = lax.all_to_all(cells, AXES, 0, 0, tiled=True)
    sigma = convolve(steps, owned, coef)
    sigma = lax.all_to_all(sigma, AXES, 0, 0, tiled=True)
    lines = 8 * slots // LANES
    if rows_per != lines:
        sigma = sigma.reshape(devices, 2, rows_per, LANES).transpose(1, 0, 2, 3)
        sigma = sigma.reshape(2, devices * rows_per, LANES)[:, :rows]
        sigma = sigma.reshape(2, rows // lines, lines, LANES).transpose(1, 0, 2, 3)
        sigma = sigma.reshape(rows // lines, 2 * lines, LANES)
    green = solve(energy, sigma, table, ham_diag, ham_coup)
    return green.reshape(2, 1, slabs, order, order)


def solution(mesh):
    return jax.shard_map(
        on_device,
        mesh=mesh,
        in_specs=(P(), P(), P(), P(), P(), P(None, ("freq", "atom"), None), P(), P()),
        out_specs=P(None, ("freq", "atom"), None, None, None),
        check_vma=False,
    )
```

```python
import functools

import jax
import jax.numpy as jnp
from jax import lax
from jax.experimental import pallas as pl
from jax.experimental.pallas import tpu as pltpu
from jax.sharding import PartitionSpec as P

HALO = 16
INV_STEPS = 22
EXACT_STEPS = 2

BROADEN = 0.8
ENERGY_LOW = -2.5
ENERGY_SPAN = 5.0

LANES = 128
RESIDUAL_LIMIT = 2e-5

AXES = ("freq", "atom")
VMEM = pltpu.MemorySpace.VMEM
SMEM = pltpu.MemorySpace.SMEM


def lanes_of(listed):
    slots, order = listed.shape
    column = lax.broadcasted_iota(jnp.int32, (order, order), 0).astype(jnp.float32).astype(jnp.bfloat16)
    column = column.reshape(order // 16, 16, order)
    found = jnp.full((order // 16, 16, order), -1.0, jnp.bfloat16)
    for slot in range(slots):
        row = jnp.broadcast_to(listed[slot : slot + 1, :], (16, order)).astype(jnp.bfloat16)
        found = jnp.where(row[None] == column, jnp.bfloat16(slot), found)
    found = found.reshape(order, order).astype(jnp.float32).astype(jnp.int32)
    lane = lax.broadcasted_iota(jnp.int32, (order, order), 1)
    offset = lax.rem(lane, LANES // slots) * slots
    return jnp.where(found >= 0, found + offset, -1).T


def prepare_kernel(
    cells_hbm,
    neighbors_hbm,
    count_hbm,
    shifts_hbm,
    emit_hbm,
    absorb_hbm,
    cells_ref,
    listed_ref,
    table_ref,
    coef_ref,
    steps_ref,
    energy_ref,
    neighbors_ref,
    count_ref,
    shifts_ref,
    weights_ref,
    sems,
    *,
    energies,
):
    own = lax.axis_index("freq") * lax.axis_size("atom") + lax.axis_index("atom")
    slabs, slots, order = listed_ref.shape
    half = coef_ref.shape[3] // 2
    width = half * LANES
    block = jnp.minimum(own, emit_hbm.shape[2] // width - 1)
    lanes = pl.ds(pl.multiple_of(block * width, LANES), width)
    copies = [
        pltpu.make_async_copy(neighbors_hbm, neighbors_ref, sems.at[0]),
        pltpu.make_async_copy(count_hbm, count_ref, sems.at[1]),
        pltpu.make_async_copy(emit_hbm.at[:, :, lanes], weights_ref.at[0], sems.at[2]),
        pltpu.make_async_copy(absorb_hbm.at[:, :, lanes], weights_ref.at[1], sems.at[3]),
        pltpu.make_async_copy(shifts_hbm, shifts_ref, sems.at[4]),
    ]
    lines = cells_hbm.shape[2]
    for part in range(cells_hbm.shape[0]):
        rows = slice(part * lines, (part + 1) * lines)
        copies.append(pltpu.make_async_copy(cells_hbm.at[part], cells_ref.at[:, rows, :], sems.at[5 + part]))
    for copy in copies:
        copy.start()
    position = jnp.full(energy_ref.shape, own, jnp.int32).astype(jnp.float32)
    energy_ref[...] = ENERGY_LOW + ENERGY_SPAN * position / energies
    copies[0].wait()
    copies[1].wait()
    slot_id = lax.broadcasted_iota(jnp.int32, (slots, order), 0)
    for slab in range(slabs):
        listed = neighbors_ref[:, slab * order : (slab + 1) * order]
        listed_ref[slab] = jnp.where(slot_id < count_ref[slab : slab + 1, :], listed, -1).astype(jnp.float32)
    table_ref[...] = lanes_of(listed_ref[slabs - 1])
    for copy in copies[2:5]:
        copy.wait()
    for mode in range(steps_ref.shape[0]):
        steps_ref[mode] = jnp.full(steps_ref.shape[1:], shifts_ref[mode], jnp.int32)
    for side in range(2):
        for row in range(half):
            part = slice(row * LANES, (row + 1) * LANES)
            real = weights_ref[side, 0, :, part]
            imag = weights_ref[side, 1, :, part]
            coef_ref[side, 0, :, row, :] = real
            coef_ref[side, 0, :, half + row, :] = real
            coef_ref[side, 1, :, row, :] = imag
            coef_ref[side, 1, :, half + row, :] = -imag
    for copy in copies[5:]:
        copy.wait()


def prepare(cells, neighbors, pair_count, shifts, emit_coup, absorb_coup, slabs, order):
    parts, devices, rows_per, _ = cells.shape
    modes = emit_coup.shape[1]
    atoms, slots = neighbors.shape
    arrays = (cells, neighbors.T, pair_count.reshape(slabs, order), shifts, emit_coup, absorb_coup)
    return pl.pallas_call(
        functools.partial(prepare_kernel, energies=devices),
        out_shape=(
            jax.ShapeDtypeStruct((devices, parts * rows_per, LANES), jnp.float32),
            jax.ShapeDtypeStruct((slabs, slots, order), jnp.float32),
            jax.ShapeDtypeStruct((order, order), jnp.int32),
            jax.ShapeDtypeStruct((2, 2, modes, 2 * rows_per, LANES), jnp.float32),
            jax.ShapeDtypeStruct((modes, 8, LANES), jnp.int32),
            jax.ShapeDtypeStruct((8, LANES), jnp.float32),
        ),
        in_specs=[pl.BlockSpec(memory_space=pltpu.HBM)] * 6,
        out_specs=(pl.BlockSpec(memory_space=VMEM),) * 6,
        scratch_shapes=[
            pltpu.VMEM((slots, atoms), jnp.int32),
            pltpu.VMEM((slabs, order), jnp.int32),
            pltpu.SMEM((modes,), jnp.int32),
            pltpu.VMEM((2, 2, modes, rows_per * LANES), jnp.float32),
            pltpu.SemaphoreType.DMA((7,)),
        ],
        compiler_params=pltpu.CompilerParams(vmem_limit_bytes=16 * 2**20),
        name="prepare",
    )(*[pltpu.with_memory_space_constraint(array, pltpu.HBM) for array in arrays])


def convolve_kernel(steps_ref, cells_ref, coef_ref, out_ref, padded_ref):
    energies, height, _ = cells_ref.shape
    modes = coef_ref.shape[2]
    half = height // 2
    shifts = [steps_ref[mode][0, 0] for mode in range(modes)]
    edge = jnp.zeros((HALO, height, LANES), jnp.float32)
    padded_ref[0:HALO] = edge
    padded_ref[HALO + energies : 2 * HALO + energies] = edge
    group = 16 if energies % 16 == 0 else 1

    def load(index, carry):
        rows = pl.ds(index * group, group)
        padded_ref[pl.ds(HALO + index * group, group)] = cells_ref[rows]
        return carry

    def combine(index, carry):
        base = HALO + index * group
        direct_sum = [jnp.zeros((height, LANES), jnp.float32)] * group
        crossed_sum = list(direct_sum)
        for mode in range(modes):
            shift = shifts[mode]
            for side in range(2):
                first = base + (shift if side else -shift)
                direct = coef_ref[side, 0, mode]
                crossed = coef_ref[side, 1, mode]
                for step in range(group):
                    cell = padded_ref[first + step]
                    direct_sum[step] = direct_sum[step] + direct * cell
                    crossed_sum[step] = crossed_sum[step] + crossed * cell
        for step in range(group):
            turned = jnp.concatenate([crossed_sum[step][half:], crossed_sum[step][:half]], axis=0)
            out_ref[index * group + step] = direct_sum[step] + turned
        return carry

    lax.fori_loop(0, energies // group, load, 0, unroll=energies // group <= 2)
    lax.fori_loop(0, energies // group, combine, 0, unroll=energies // group <= 2)


def convolve(steps, cells, coef):
    energies, height, _ = cells.shape
    vmem = pl.BlockSpec(memory_space=VMEM)
    return pl.pallas_call(
        convolve_kernel,
        out_shape=jax.ShapeDtypeStruct(cells.shape, jnp.float32),
        in_specs=[vmem, vmem, vmem],
        out_specs=vmem,
        scratch_shapes=[pltpu.VMEM((energies + 2 * HALO, height, LANES), jnp.float32)],
        compiler_params=pltpu.CompilerParams(vmem_limit_bytes=16 * 2**20),
        name="convolve",
    )(steps, cells, coef)


def embed(pair):
    order = pair.shape[1] // 2
    return jnp.concatenate(
        [pair, jnp.concatenate([-pair[:, order:], pair[:, :order]], axis=1)], axis=0
    )


def pieces(value, count):
    parts = []
    for index in range(count):
        parts.append(value.astype(jnp.bfloat16))
        if index + 1 < count:
            value = value - parts[-1].astype(jnp.float32)
    return parts


def unit_pair(order):
    row = lax.broadcasted_iota(jnp.int32, (order, 2 * order), 0)
    column = lax.broadcasted_iota(jnp.int32, (order, 2 * order), 1)
    return jnp.where(row == column, 1.0, 0.0).astype(jnp.float32)


def square_sum(pair):
    squares = pair * pair
    return jnp.sum(jnp.sum(squares, axis=0, keepdims=True), axis=1, keepdims=True)


def adjoint(pair):
    order = pair.shape[0]
    return jnp.concatenate([pair[:, :order].T, -pair[:, order:].T], axis=1)


class Multiplier:
    def __init__(self, blocks):
        self.blocks = blocks
        self.turn = 0

    def load(self, factor, transpose=False):
        stage = self.turn
        self.turn = 1 - stage
        for unit in range(2):
            pltpu.matmul_push_rhs(factor, stage, unit, transpose=transpose)
        return stage

    def feed(self, stage, *rows):
        for block, left in rows:
            for unit in range(2):
                mine = [left[row : row + 16] for row in range(16 * unit, left.shape[0], 32)]
                pltpu.matmul_acc_lhs(
                    self.blocks[block][unit],
                    jnp.concatenate(mine, axis=0),
                    load_staged_rhs=stage,
                )
            stage = None

    def take(self, block):
        halves = [pltpu.matmul_pop(self.blocks[block][unit]) for unit in range(2)]
        rows = range(0, halves[0].shape[0], 16)
        return jnp.concatenate([half[row : row + 16] for row in rows for half in halves], axis=0)

    def product(self, left, right, transpose=False):
        for index, factor in enumerate(right):
            stage = self.load(factor, transpose)
            self.feed(stage, *[(0, piece) for piece in left[: len(left) - index]])
        return self.take(0)


def iterate(mxu, matrix, follow, count):
    order = matrix.shape[0]
    split = pieces(matrix, 2)
    product = mxu.product(split[:1], [embed(split[0])], transpose=True)
    scale = 1.0 / square_sum(matrix)
    x = adjoint(matrix) * scale
    y = product * scale
    for index in range(count):
        narrow = y.astype(jnp.bfloat16)
        stage = mxu.load(embed(narrow))
        more = index + 1 < count
        if more:
            mxu.feed(stage, (0, narrow))
        if index:
            x = (x - mxu.take(1)) + x
        mxu.feed(None if more else stage, (1, x.astype(jnp.bfloat16)))
        if more:
            y = (y - mxu.take(0)) + y
    x = (x - mxu.take(1)) + x

    high, low = pieces(x, 2)
    wide = mxu.load(embed(high))
    rest = mxu.load(embed(low))
    mxu.feed(rest, (0, split[0]), (1, follow[0]))
    mxu.feed(wide, (0, split[0]), (0, split[1]), (1, follow[0]), (1, follow[1]))
    residual = unit_pair(order) - mxu.take(0)
    t = mxu.take(1)
    r_high, r_low = pieces(residual, 2)
    t_high, t_low = pieces(t, 2)
    wide = mxu.load(embed(r_high))
    rest = mxu.load(embed(r_low))
    mxu.feed(wide, (0, r_high), (2, t_high), (2, t_low), (1, high), (1, low))
    mxu.feed(rest, (2, t_high), (1, high))
    residual = mxu.take(0)
    stage = mxu.load(embed(residual.astype(jnp.bfloat16)))
    t = t + mxu.take(2)
    x = x + mxu.take(1)
    mxu.feed(stage, (1, t.astype(jnp.bfloat16)), (0, x.astype(jnp.bfloat16)))
    t = t + mxu.take(1)
    return x + mxu.take(0), t, square_sum(residual)


def iterate_plain(mxu, matrix):
    split = pieces(matrix, 3)
    unit = unit_pair(matrix.shape[0])

    def step(index, x):
        right = [embed(piece) for piece in pieces(x, 3)]
        residue = 2.0 * unit - mxu.product(split, right)
        return mxu.product(pieces(x, 3), [embed(piece) for piece in pieces(residue, 3)])

    return lax.fori_loop(0, INV_STEPS, step, adjoint(matrix) * (1.0 / square_sum(matrix)))


def pick(values, index, axis):
    return jnp.take_along_axis(values, index, axis=axis, mode="promise_in_bounds")


def solve_kernel(energy_ref, cells_ref, listed_ref, table_ref, diag_ref, coup_ref, out_ref, matrix_ref, stage_ref, sems):
    slabs, order, _ = diag_ref.shape
    unit = unit_pair(order)
    energy = energy_ref[...]
    row = lax.broadcasted_iota(jnp.int32, (8, LANES), 0)
    lines = cells_ref.shape[1] // 2
    line_of = row // (8 // lines)

    def assemble(slab, lanes):
        for block in range(order // 8):
            cell = cells_ref[slab * (order // 8) + block]
            rows = slice(block * 8, block * 8 + 8)
            table = lanes[rows, :]
            held = table >= 0
            lane = jnp.where(held, table, 0)
            for part in range(2):
                spread = pick(cell, line_of + part * lines, 0)
                sigma = jnp.where(held, pick(spread, lane, 1), 0.0)
                eye = unit[rows, :order]
                if part == 0:
                    entry = energy * eye - diag_ref[slab, rows, :] - sigma
                else:
                    entry = BROADEN * eye - sigma
                matrix_ref[slab, rows, part * order : (part + 1) * order] = entry

    assemble(1, table_ref[...])
    coup = coup_ref[0]
    none = jnp.zeros_like(coup)
    coup_left = jnp.concatenate([coup, none], axis=1)
    coup_right = embed(jnp.concatenate([coup.T, none], axis=1))

    def send(slab, pair):
        for part in range(2):
            stage_ref[part, slab] = pair[:, part * order : (part + 1) * order]
            pltpu.make_async_copy(stage_ref.at[part, slab], out_ref.at[part, slab], sems.at[part, slab]).start()

    def sent():
        for slab in range(slabs):
            for part in range(2):
                pltpu.make_async_copy(stage_ref.at[part, slab], out_ref.at[part, slab], sems.at[part, slab]).wait()

    def body(*accumulators):
        mxu = Multiplier([accumulators[2 * i : 2 * i + 2] for i in range(3)])
        right = pieces(coup_right, 2)
        last, left_of, last_norm = iterate(mxu, matrix_ref[1], pieces(coup_left, 2), INV_STEPS - EXACT_STEPS)
        assemble(0, lanes_of(listed_ref[0]))
        matrix = matrix_ref[0] - mxu.product(pieces(left_of, 2), right)
        right_of = mxu.product(pieces(last, 2), right)
        first, both, first_norm = iterate(mxu, matrix, pieces(right_of, 2), INV_STEPS - EXACT_STEPS)
        send(0, first)
        update = mxu.product(pieces(both, 2), [embed(piece) for piece in pieces(left_of, 2)])
        send(1, last + update)
        worst = jnp.maximum(last_norm, first_norm)[0, 0]
        settled = jnp.logical_and(worst <= RESIDUAL_LIMIT, last_norm[0, 0] + first_norm[0, 0] <= 2.0 * RESIDUAL_LIMIT)
        sent()

        @pl.when(jnp.logical_not(settled))
        def _():
            right = pieces(coup_right, 3)
            last = iterate_plain(mxu, matrix_ref[1])
            left_of = mxu.product(pieces(coup_left, 3), [embed(piece) for piece in pieces(last, 3)])
            right_of = mxu.product(pieces(last, 3), right)
            first = iterate_plain(mxu, matrix_ref[0] - mxu.product(pieces(left_of, 3), right))
            both = mxu.product(pieces(right_of, 3), [embed(piece) for piece in pieces(first, 3)])
            update = mxu.product(pieces(both, 3), [embed(piece) for piece in pieces(left_of, 3)])
            send(0, first)
            send(1, last + update)
            sent()

    shape = (order // 2, 2 * order)
    pl.run_scoped(body, *[pltpu.ACC(unit)(shape, jnp.float32) for _ in range(3) for unit in range(2)])


def solve(energy, cells, listed, table, ham_diag, ham_coup):
    slabs, order, _ = ham_diag.shape
    vmem = pl.BlockSpec(memory_space=VMEM)
    return pl.pallas_call(
        solve_kernel,
        out_shape=jax.ShapeDtypeStruct((2, slabs, order, order), jnp.float32),
        in_specs=[vmem] * 6,
        out_specs=pl.BlockSpec(memory_space=pl.ANY),
        scratch_shapes=[
            pltpu.VMEM((slabs, order, 2 * order), jnp.float32),
            pltpu.VMEM((2, slabs, order, order), jnp.float32),
            pltpu.SemaphoreType.DMA((2, slabs)),
        ],
        compiler_params=pltpu.CompilerParams(vmem_limit_bytes=16 * 2**20),
        name="solve",
    )(energy, cells, listed, table, ham_diag, ham_coup)


def on_device(ham_diag, ham_coup, neighbors, pair_count, shifts, g_pairs, emit_coup, absorb_coup):
    slabs, order, _ = ham_diag.shape
    atoms, slots = neighbors.shape
    devices = lax.axis_size("freq") * lax.axis_size("atom")
    rows = g_pairs.shape[2] // LANES
    rows_per = -(-rows // devices)
    spare = rows_per * devices - rows

    cells = g_pairs.reshape(2, rows, LANES)
    if spare:
        cells = jnp.pad(cells, ((0, 0), (0, spare), (0, 0)))
    cells, listed, table, coef, steps, energy = prepare(
        cells.reshape(2, devices, rows_per, LANES), neighbors, pair_count, shifts, emit_coup, absorb_coup, slabs, order
    )
    owned = lax.all_to_all(cells, AXES, 0, 0, tiled=True)
    sigma = convolve(steps, owned, coef)
    sigma = lax.all_to_all(sigma, AXES, 0, 0, tiled=True)
    lines = 8 * slots // LANES
    if rows_per != lines:
        sigma = sigma.reshape(devices, 2, rows_per, LANES).transpose(1, 0, 2, 3)
        sigma = sigma.reshape(2, devices * rows_per, LANES)[:, :rows]
        sigma = sigma.reshape(2, rows // lines, lines, LANES).transpose(1, 0, 2, 3)
        sigma = sigma.reshape(rows // lines, 2 * lines, LANES)
    green = solve(energy, sigma, listed, table, ham_diag, ham_coup)
    return green.reshape(2, 1, slabs, order, order)


def solution(mesh):
    return jax.shard_map(
        on_device,
        mesh=mesh,
        in_specs=(P(), P(), P(), P(), P(), P(None, ("freq", "atom"), None), P(), P()),
        out_specs=P(None, ("freq", "atom"), None, None, None),
        check_vma=False,
    )
```

```python
import functools

import jax
import jax.numpy as jnp
from jax import lax
from jax.experimental import pallas as pl
from jax.experimental.pallas import tpu as pltpu
from jax.sharding import PartitionSpec as P

HALO = 16
INV_STEPS = 22
EXACT_STEPS = 2

BROADEN = 0.8
ENERGY_LOW = -2.5
ENERGY_SPAN = 5.0

LANES = 128
RESIDUAL_LIMIT = 2e-5

AXES = ("freq", "atom")
VMEM = pltpu.MemorySpace.VMEM
SMEM = pltpu.MemorySpace.SMEM


def lanes_of(listed):
    slots, order = listed.shape
    column = lax.broadcasted_iota(jnp.int32, (order, order), 0).astype(jnp.float32).astype(jnp.bfloat16)
    column = column.reshape(order // 16, 16, order)
    found = jnp.full((order // 16, 16, order), -1.0, jnp.bfloat16)
    for slot in range(slots):
        row = jnp.broadcast_to(listed[slot : slot + 1, :], (16, order)).astype(jnp.bfloat16)
        found = jnp.where(row[None] == column, jnp.bfloat16(slot), found)
    found = found.reshape(order, order).astype(jnp.float32).astype(jnp.int32)
    lane = lax.broadcasted_iota(jnp.int32, (order, order), 1)
    offset = lax.rem(lane, LANES // slots) * slots
    return jnp.where(found >= 0, found + offset, -1).T


def prepare_kernel(
    cells_hbm,
    neighbors_hbm,
    count_hbm,
    shifts_hbm,
    emit_hbm,
    absorb_hbm,
    cells_ref,
    listed_ref,
    table_ref,
    coef_ref,
    steps_ref,
    energy_ref,
    neighbors_ref,
    count_ref,
    shifts_ref,
    weights_ref,
    sems,
    *,
    energies,
):
    own = lax.axis_index("freq") * lax.axis_size("atom") + lax.axis_index("atom")
    slabs, slots, order = listed_ref.shape
    half = coef_ref.shape[3] // 2
    width = half * LANES
    block = jnp.minimum(own, emit_hbm.shape[2] // width - 1)
    lanes = pl.ds(pl.multiple_of(block * width, LANES), width)
    copies = [
        pltpu.make_async_copy(neighbors_hbm, neighbors_ref, sems.at[0]),
        pltpu.make_async_copy(count_hbm, count_ref, sems.at[1]),
        pltpu.make_async_copy(emit_hbm.at[:, :, lanes], weights_ref.at[0], sems.at[2]),
        pltpu.make_async_copy(absorb_hbm.at[:, :, lanes], weights_ref.at[1], sems.at[3]),
        pltpu.make_async_copy(shifts_hbm, shifts_ref, sems.at[4]),
    ]
    lines = cells_hbm.shape[2]
    for part in range(cells_hbm.shape[0]):
        rows = slice(part * lines, (part + 1) * lines)
        copies.append(pltpu.make_async_copy(cells_hbm.at[part], cells_ref.at[:, rows, :], sems.at[5 + part]))
    for copy in copies:
        copy.start()
    position = jnp.full(energy_ref.shape, own, jnp.int32).astype(jnp.float32)
    energy_ref[...] = ENERGY_LOW + ENERGY_SPAN * position / energies
    copies[0].wait()
    copies[1].wait()
    slot_id = lax.broadcasted_iota(jnp.int32, (slots, order), 0)
    for slab in range(slabs):
        listed = neighbors_ref[:, slab * order : (slab + 1) * order]
        listed_ref[slab] = jnp.where(slot_id < count_ref[slab : slab + 1, :], listed, -1).astype(jnp.float32)
    table_ref[...] = lanes_of(listed_ref[slabs - 1])
    for copy in copies[2:5]:
        copy.wait()
    for mode in range(steps_ref.shape[0]):
        steps_ref[mode] = jnp.full(steps_ref.shape[1:], shifts_ref[mode], jnp.int32)
    for side in range(2):
        for row in range(half):
            part = slice(row * LANES, (row + 1) * LANES)
            real = weights_ref[side, 0, :, part]
            imag = weights_ref[side, 1, :, part]
            coef_ref[side, 0, :, row, :] = real
            coef_ref[side, 0, :, half + row, :] = real
            coef_ref[side, 1, :, row, :] = imag
            coef_ref[side, 1, :, half + row, :] = -imag
    for copy in copies[5:]:
        copy.wait()


def prepare(cells, neighbors, pair_count, shifts, emit_coup, absorb_coup, slabs, order):
    parts, devices, rows_per, _ = cells.shape
    modes = emit_coup.shape[1]
    atoms, slots = neighbors.shape
    arrays = (cells, neighbors.T, pair_count.reshape(slabs, order), shifts, emit_coup, absorb_coup)
    return pl.pallas_call(
        functools.partial(prepare_kernel, energies=devices),
        out_shape=(
            jax.ShapeDtypeStruct((devices, parts * rows_per, LANES), jnp.float32),
            jax.ShapeDtypeStruct((slabs, slots, order), jnp.float32),
            jax.ShapeDtypeStruct((order, order), jnp.int32),
            jax.ShapeDtypeStruct((2, 2, modes, 2 * rows_per, LANES), jnp.float32),
            jax.ShapeDtypeStruct((modes, 8, LANES), jnp.int32),
            jax.ShapeDtypeStruct((8, LANES), jnp.float32),
        ),
        in_specs=[pl.BlockSpec(memory_space=pltpu.HBM)] * 6,
        out_specs=(pl.BlockSpec(memory_space=VMEM),) * 6,
        scratch_shapes=[
            pltpu.VMEM((slots, atoms), jnp.int32),
            pltpu.VMEM((slabs, order), jnp.int32),
            pltpu.SMEM((modes,), jnp.int32),
            pltpu.VMEM((2, 2, modes, rows_per * LANES), jnp.float32),
            pltpu.SemaphoreType.DMA((7,)),
        ],
        compiler_params=pltpu.CompilerParams(vmem_limit_bytes=16 * 2**20),
        name="prepare",
    )(*[pltpu.with_memory_space_constraint(array, pltpu.HBM) for array in arrays])


def convolve_kernel(steps_ref, cells_ref, coef_ref, out_ref, padded_ref):
    energies, height, _ = cells_ref.shape
    modes = coef_ref.shape[2]
    half = height // 2
    shifts = [steps_ref[mode][0, 0] for mode in range(modes)]
    edge = jnp.zeros((HALO, height, LANES), jnp.float32)
    padded_ref[0:HALO] = edge
    padded_ref[HALO + energies : 2 * HALO + energies] = edge
    group = 16 if energies % 16 == 0 else 1

    def load(index, carry):
        rows = pl.ds(index * group, group)
        padded_ref[pl.ds(HALO + index * group, group)] = cells_ref[rows]
        return carry

    def combine(index, carry):
        base = HALO + index * group
        direct_sum = [jnp.zeros((height, LANES), jnp.float32)] * group
        crossed_sum = list(direct_sum)
        for mode in range(modes):
            shift = shifts[mode]
            for side in range(2):
                first = base + (shift if side else -shift)
                direct = coef_ref[side, 0, mode]
                crossed = coef_ref[side, 1, mode]
                for step in range(group):
                    cell = padded_ref[first + step]
                    direct_sum[step] = direct_sum[step] + direct * cell
                    crossed_sum[step] = crossed_sum[step] + crossed * cell
        for step in range(group):
            turned = jnp.concatenate([crossed_sum[step][half:], crossed_sum[step][:half]], axis=0)
            out_ref[index * group + step] = direct_sum[step] + turned
        return carry

    lax.fori_loop(0, energies // group, load, 0, unroll=energies // group <= 2)
    lax.fori_loop(0, energies // group, combine, 0, unroll=energies // group <= 2)


def convolve(steps, cells, coef):
    energies, height, _ = cells.shape
    vmem = pl.BlockSpec(memory_space=VMEM)
    return pl.pallas_call(
        convolve_kernel,
        out_shape=jax.ShapeDtypeStruct(cells.shape, jnp.float32),
        in_specs=[vmem, vmem, vmem],
        out_specs=vmem,
        scratch_shapes=[pltpu.VMEM((energies + 2 * HALO, height, LANES), jnp.float32)],
        compiler_params=pltpu.CompilerParams(vmem_limit_bytes=16 * 2**20),
        name="convolve",
    )(steps, cells, coef)


def embed(pair):
    order = pair.shape[1] // 2
    return jnp.concatenate(
        [pair, jnp.concatenate([-pair[:, order:], pair[:, :order]], axis=1)], axis=0
    )


def pieces(value, count):
    parts = []
    for index in range(count):
        parts.append(value.astype(jnp.bfloat16))
        if index + 1 < count:
            value = value - parts[-1].astype(jnp.float32)
    return parts


def unit_pair(order):
    row = lax.broadcasted_iota(jnp.int32, (order, 2 * order), 0)
    column = lax.broadcasted_iota(jnp.int32, (order, 2 * order), 1)
    return jnp.where(row == column, 1.0, 0.0).astype(jnp.float32)


def square_sum(pair):
    squares = pair * pair
    return jnp.sum(jnp.sum(squares, axis=0, keepdims=True), axis=1, keepdims=True)


def adjoint(pair):
    order = pair.shape[0]
    return jnp.concatenate([pair[:, :order].T, -pair[:, order:].T], axis=1)


class Multiplier:
    def __init__(self, blocks):
        self.blocks = blocks
        self.turn = 0

    def load(self, factor, transpose=False):
        stage = self.turn
        self.turn = 1 - stage
        for unit in range(2):
            pltpu.matmul_push_rhs(factor, stage, unit, transpose=transpose)
        return stage

    def feed(self, stage, *rows):
        for block, left in rows:
            for unit in range(2):
                mine = [left[row : row + 16] for row in range(16 * unit, left.shape[0], 32)]
                pltpu.matmul_acc_lhs(
                    self.blocks[block][unit],
                    jnp.concatenate(mine, axis=0),
                    load_staged_rhs=stage,
                )
            stage = None

    def take(self, block):
        halves = [pltpu.matmul_pop(self.blocks[block][unit]) for unit in range(2)]
        rows = range(0, halves[0].shape[0], 16)
        return jnp.concatenate([half[row : row + 16] for row in rows for half in halves], axis=0)

    def product(self, left, right, transpose=False):
        for index, factor in enumerate(right):
            stage = self.load(factor, transpose)
            self.feed(stage, *[(0, piece) for piece in left[: len(left) - index]])
        return self.take(0)


def iterate(mxu, matrix, follow, count):
    order = matrix.shape[0]
    split = pieces(matrix, 2)
    product = mxu.product(split[:1], [embed(split[0])], transpose=True)
    scale = 1.0 / square_sum(matrix)
    x = adjoint(matrix) * scale
    y = product * scale
    for index in range(count):
        narrow = y.astype(jnp.bfloat16)
        stage = mxu.load(embed(narrow))
        more = index + 1 < count
        if more:
            mxu.feed(stage, (0, narrow))
        if index:
            x = (x + x) - mxu.take(1)
        mxu.feed(None if more else stage, (1, x.astype(jnp.bfloat16)))
        if more:
            y = (y + y) - mxu.take(0)
    x = (x + x) - mxu.take(1)

    high, low = pieces(x, 2)
    wide = mxu.load(embed(high))
    rest = mxu.load(embed(low))
    mxu.feed(rest, (0, split[0]), (1, follow[0]))
    mxu.feed(wide, (0, split[0]), (0, split[1]), (1, follow[0]), (1, follow[1]))
    residual = unit_pair(order) - mxu.take(0)
    t = mxu.take(1)
    r_high, r_low = pieces(residual, 2)
    t_high, t_low = pieces(t, 2)
    wide = mxu.load(embed(r_high))
    rest = mxu.load(embed(r_low))
    mxu.feed(wide, (0, r_high), (2, t_high), (2, t_low), (1, high), (1, low))
    mxu.feed(rest, (2, t_high), (1, high))
    residual = mxu.take(0)
    stage = mxu.load(embed(residual.astype(jnp.bfloat16)))
    t = t + mxu.take(2)
    x = x + mxu.take(1)
    mxu.feed(stage, (1, t.astype(jnp.bfloat16)), (0, x.astype(jnp.bfloat16)))
    t = t + mxu.take(1)
    return x + mxu.take(0), t, square_sum(residual)


def iterate_plain(mxu, matrix):
    split = pieces(matrix, 3)
    unit = unit_pair(matrix.shape[0])

    def step(index, x):
        right = [embed(piece) for piece in pieces(x, 3)]
        residue = 2.0 * unit - mxu.product(split, right)
        return mxu.product(pieces(x, 3), [embed(piece) for piece in pieces(residue, 3)])

    return lax.fori_loop(0, INV_STEPS, step, adjoint(matrix) * (1.0 / square_sum(matrix)))


def pick(values, index, axis):
    return jnp.take_along_axis(values, index, axis=axis, mode="promise_in_bounds")


def solve_kernel(energy_ref, cells_ref, listed_ref, table_ref, diag_ref, coup_ref, out_ref, matrix_ref, stage_ref, sems):
    slabs, order, _ = diag_ref.shape
    unit = unit_pair(order)
    energy = energy_ref[...]
    row = lax.broadcasted_iota(jnp.int32, (8, LANES), 0)
    lines = cells_ref.shape[1] // 2
    line_of = row // (8 // lines)

    def assemble(slab, lanes):
        for block in range(order // 8):
            cell = cells_ref[slab * (order // 8) + block]
            rows = slice(block * 8, block * 8 + 8)
            table = lanes[rows, :]
            held = table >= 0
            lane = jnp.where(held, table, 0)
            for part in range(2):
                spread = pick(cell, line_of + part * lines, 0)
                sigma = jnp.where(held, pick(spread, lane, 1), 0.0)
                eye = unit[rows, :order]
                if part == 0:
                    entry = energy * eye - diag_ref[slab, rows, :] - sigma
                else:
                    entry = BROADEN * eye - sigma
                matrix_ref[slab, rows, part * order : (part + 1) * order] = entry

    assemble(1, table_ref[...])
    coup = coup_ref[0]
    none = jnp.zeros_like(coup)
    coup_left = jnp.concatenate([coup, none], axis=1)
    coup_right = embed(jnp.concatenate([coup.T, none], axis=1))

    def send(slab, pair):
        for part in range(2):
            stage_ref[part, slab] = pair[:, part * order : (part + 1) * order]
            pltpu.make_async_copy(stage_ref.at[part, slab], out_ref.at[part, slab], sems.at[part, slab]).start()

    def sent():
        for slab in range(slabs):
            for part in range(2):
                pltpu.make_async_copy(stage_ref.at[part, slab], out_ref.at[part, slab], sems.at[part, slab]).wait()

    def body(*accumulators):
        mxu = Multiplier([accumulators[2 * i : 2 * i + 2] for i in range(3)])
        right = pieces(coup_right, 2)
        last, left_of, last_norm = iterate(mxu, matrix_ref[1], pieces(coup_left, 2), INV_STEPS - EXACT_STEPS)
        assemble(0, lanes_of(listed_ref[0]))
        matrix = matrix_ref[0] - mxu.product(pieces(left_of, 2), right)
        right_of = mxu.product(pieces(last, 2), right)
        first, both, first_norm = iterate(mxu, matrix, pieces(right_of, 2), INV_STEPS - EXACT_STEPS)
        send(0, first)
        update = mxu.product(pieces(both, 2), [embed(piece) for piece in pieces(left_of, 2)])
        send(1, last + update)
        worst = jnp.maximum(last_norm, first_norm)[0, 0]
        settled = jnp.logical_and(worst <= RESIDUAL_LIMIT, last_norm[0, 0] + first_norm[0, 0] <= 2.0 * RESIDUAL_LIMIT)
        sent()

        @pl.when(jnp.logical_not(settled))
        def _():
            right = pieces(coup_right, 3)
            last = iterate_plain(mxu, matrix_ref[1])
            left_of = mxu.product(pieces(coup_left, 3), [embed(piece) for piece in pieces(last, 3)])
            right_of = mxu.product(pieces(last, 3), right)
            first = iterate_plain(mxu, matrix_ref[0] - mxu.product(pieces(left_of, 3), right))
            both = mxu.product(pieces(right_of, 3), [embed(piece) for piece in pieces(first, 3)])
            update = mxu.product(pieces(both, 3), [embed(piece) for piece in pieces(left_of, 3)])
            send(0, first)
            send(1, last + update)
            sent()

    shape = (order // 2, 2 * order)
    pl.run_scoped(body, *[pltpu.ACC(unit)(shape, jnp.float32) for _ in range(3) for unit in range(2)])


def solve(energy, cells, listed, table, ham_diag, ham_coup):
    slabs, order, _ = ham_diag.shape
    vmem = pl.BlockSpec(memory_space=VMEM)
    return pl.pallas_call(
        solve_kernel,
        out_shape=jax.ShapeDtypeStruct((2, slabs, order, order), jnp.float32),
        in_specs=[vmem] * 6,
        out_specs=pl.BlockSpec(memory_space=pl.ANY),
        scratch_shapes=[
            pltpu.VMEM((slabs, order, 2 * order), jnp.float32),
            pltpu.VMEM((2, slabs, order, order), jnp.float32),
            pltpu.SemaphoreType.DMA((2, slabs)),
        ],
        compiler_params=pltpu.CompilerParams(vmem_limit_bytes=16 * 2**20),
        name="solve",
    )(energy, cells, listed, table, ham_diag, ham_coup)


def on_device(ham_diag, ham_coup, neighbors, pair_count, shifts, g_pairs, emit_coup, absorb_coup):
    slabs, order, _ = ham_diag.shape
    atoms, slots = neighbors.shape
    devices = lax.axis_size("freq") * lax.axis_size("atom")
    rows = g_pairs.shape[2] // LANES
    rows_per = -(-rows // devices)
    spare = rows_per * devices - rows

    cells = g_pairs.reshape(2, rows, LANES)
    if spare:
        cells = jnp.pad(cells, ((0, 0), (0, spare), (0, 0)))
    cells, listed, table, coef, steps, energy = prepare(
        cells.reshape(2, devices, rows_per, LANES), neighbors, pair_count, shifts, emit_coup, absorb_coup, slabs, order
    )
    owned = lax.all_to_all(cells, AXES, 0, 0, tiled=True)
    sigma = convolve(steps, owned, coef)
    sigma = lax.all_to_all(sigma, AXES, 0, 0, tiled=True)
    lines = 8 * slots // LANES
    if rows_per != lines:
        sigma = sigma.reshape(devices, 2, rows_per, LANES).transpose(1, 0, 2, 3)
        sigma = sigma.reshape(2, devices * rows_per, LANES)[:, :rows]
        sigma = sigma.reshape(2, rows // lines, lines, LANES).transpose(1, 0, 2, 3)
        sigma = sigma.reshape(rows // lines, 2 * lines, LANES)
    green = solve(energy, sigma, listed, table, ham_diag, ham_coup)
    return green.reshape(2, 1, slabs, order, order)


def solution(mesh):
    return jax.shard_map(
        on_device,
        mesh=mesh,
        in_specs=(P(), P(), P(), P(), P(), P(None, ("freq", "atom"), None), P(), P()),
        out_specs=P(None, ("freq", "atom"), None, None, None),
        check_vma=False,
    )
```

```python
import functools

import jax
import jax.numpy as jnp
from jax import lax
from jax.experimental import pallas as pl
from jax.experimental.pallas import tpu as pltpu
from jax.sharding import PartitionSpec as P

HALO = 16
INV_STEPS = 22
EXACT_STEPS = 2

BROADEN = 0.8
ENERGY_LOW = -2.5
ENERGY_SPAN = 5.0

LANES = 128
RESIDUAL_LIMIT = 2e-5

AXES = ("freq", "atom")
VMEM = pltpu.MemorySpace.VMEM
SMEM = pltpu.MemorySpace.SMEM


def lanes_of(listed):
    slots, order = listed.shape
    column = lax.broadcasted_iota(jnp.int32, (order, order), 0).astype(jnp.float32).astype(jnp.bfloat16)
    column = column.reshape(order // 16, 16, order)
    found = jnp.full((order // 16, 16, order), -1.0, jnp.bfloat16)
    for slot in range(slots):
        row = jnp.broadcast_to(listed[slot : slot + 1, :], (16, order)).astype(jnp.bfloat16)
        found = jnp.where(row[None] == column, jnp.bfloat16(slot), found)
    found = found.reshape(order, order).astype(jnp.float32).astype(jnp.int32)
    lane = lax.broadcasted_iota(jnp.int32, (order, order), 1)
    offset = lax.rem(lane, LANES // slots) * slots
    return jnp.where(found >= 0, found + offset, -1).T


def prepare_kernel(
    cells_hbm,
    neighbors_hbm,
    count_hbm,
    shifts_hbm,
    emit_hbm,
    absorb_hbm,
    cells_ref,
    listed_ref,
    table_ref,
    coef_ref,
    steps_ref,
    energy_ref,
    neighbors_ref,
    count_ref,
    shifts_ref,
    weights_ref,
    sems,
    *,
    energies,
):
    own = lax.axis_index("freq") * lax.axis_size("atom") + lax.axis_index("atom")
    slabs, slots, order = listed_ref.shape
    half = coef_ref.shape[3] // 2
    width = half * LANES
    block = jnp.minimum(own, emit_hbm.shape[2] // width - 1)
    lanes = pl.ds(pl.multiple_of(block * width, LANES), width)
    copies = [
        pltpu.make_async_copy(neighbors_hbm, neighbors_ref, sems.at[0]),
        pltpu.make_async_copy(count_hbm, count_ref, sems.at[1]),
        pltpu.make_async_copy(emit_hbm.at[:, :, lanes], weights_ref.at[0], sems.at[2]),
        pltpu.make_async_copy(absorb_hbm.at[:, :, lanes], weights_ref.at[1], sems.at[3]),
        pltpu.make_async_copy(shifts_hbm, shifts_ref, sems.at[4]),
    ]
    lines = cells_hbm.shape[2]
    for part in range(cells_hbm.shape[0]):
        rows = slice(part * lines, (part + 1) * lines)
        copies.append(pltpu.make_async_copy(cells_hbm.at[part], cells_ref.at[:, rows, :], sems.at[5 + part]))
    for copy in copies:
        copy.start()
    position = jnp.full(energy_ref.shape, own, jnp.int32).astype(jnp.float32)
    energy_ref[...] = ENERGY_LOW + ENERGY_SPAN * position / energies
    for copy in copies[2:5]:
        copy.wait()
    for mode in range(steps_ref.shape[0]):
        steps_ref[mode] = jnp.full(steps_ref.shape[1:], shifts_ref[mode], jnp.int32)
    for side in range(2):
        for row in range(half):
            part = slice(row * LANES, (row + 1) * LANES)
            real = weights_ref[side, 0, :, part]
            imag = weights_ref[side, 1, :, part]
            coef_ref[side, 0, :, row, :] = real
            coef_ref[side, 0, :, half + row, :] = real
            coef_ref[side, 1, :, row, :] = imag
            coef_ref[side, 1, :, half + row, :] = -imag
    copies[0].wait()
    copies[1].wait()
    slot_id = lax.broadcasted_iota(jnp.int32, (slots, order), 0)
    for slab in range(slabs):
        listed = neighbors_ref[:, slab * order : (slab + 1) * order]
        listed_ref[slab] = jnp.where(slot_id < count_ref[slab : slab + 1, :], listed, -1).astype(jnp.float32)
    table_ref[...] = lanes_of(listed_ref[slabs - 1])
    for copy in copies[5:]:
        copy.wait()


def prepare(cells, neighbors, pair_count, shifts, emit_coup, absorb_coup, slabs, order):
    parts, devices, rows_per, _ = cells.shape
    modes = emit_coup.shape[1]
    atoms, slots = neighbors.shape
    arrays = (cells, neighbors.T, pair_count.reshape(slabs, order), shifts, emit_coup, absorb_coup)
    return pl.pallas_call(
        functools.partial(prepare_kernel, energies=devices),
        out_shape=(
            jax.ShapeDtypeStruct((devices, parts * rows_per, LANES), jnp.float32),
            jax.ShapeDtypeStruct((slabs, slots, order), jnp.float32),
            jax.ShapeDtypeStruct((order, order), jnp.int32),
            jax.ShapeDtypeStruct((2, 2, modes, 2 * rows_per, LANES), jnp.float32),
            jax.ShapeDtypeStruct((modes, 8, LANES), jnp.int32),
            jax.ShapeDtypeStruct((8, LANES), jnp.float32),
        ),
        in_specs=[pl.BlockSpec(memory_space=pltpu.HBM)] * 6,
        out_specs=(pl.BlockSpec(memory_space=VMEM),) * 6,
        scratch_shapes=[
            pltpu.VMEM((slots, atoms), jnp.int32),
            pltpu.VMEM((slabs, order), jnp.int32),
            pltpu.SMEM((modes,), jnp.int32),
            pltpu.VMEM((2, 2, modes, rows_per * LANES), jnp.float32),
            pltpu.SemaphoreType.DMA((7,)),
        ],
        compiler_params=pltpu.CompilerParams(vmem_limit_bytes=16 * 2**20),
        name="prepare",
    )(*[pltpu.with_memory_space_constraint(array, pltpu.HBM) for array in arrays])


def convolve_kernel(steps_ref, cells_ref, coef_ref, out_ref, padded_ref):
    energies, height, _ = cells_ref.shape
    modes = coef_ref.shape[2]
    half = height // 2
    shifts = [steps_ref[mode][0, 0] for mode in range(modes)]
    edge = jnp.zeros((HALO, height, LANES), jnp.float32)
    padded_ref[0:HALO] = edge
    padded_ref[HALO + energies : 2 * HALO + energies] = edge
    group = 16 if energies % 16 == 0 else 1

    def load(index, carry):
        rows = pl.ds(index * group, group)
        padded_ref[pl.ds(HALO + index * group, group)] = cells_ref[rows]
        return carry

    def combine(index, carry):
        base = HALO + index * group
        direct_sum = [jnp.zeros((height, LANES), jnp.float32)] * group
        crossed_sum = list(direct_sum)
        for mode in range(modes):
            shift = shifts[mode]
            for side in range(2):
                first = base + (shift if side else -shift)
                direct = coef_ref[side, 0, mode]
                crossed = coef_ref[side, 1, mode]
                for step in range(group):
                    cell = padded_ref[first + step]
                    direct_sum[step] = direct_sum[step] + direct * cell
                    crossed_sum[step] = crossed_sum[step] + crossed * cell
        for step in range(group):
            turned = jnp.concatenate([crossed_sum[step][half:], crossed_sum[step][:half]], axis=0)
            out_ref[index * group + step] = direct_sum[step] + turned
        return carry

    lax.fori_loop(0, energies // group, load, 0, unroll=energies // group <= 2)
    lax.fori_loop(0, energies // group, combine, 0, unroll=energies // group <= 2)


def convolve(steps, cells, coef):
    energies, height, _ = cells.shape
    vmem = pl.BlockSpec(memory_space=VMEM)
    return pl.pallas_call(
        convolve_kernel,
        out_shape=jax.ShapeDtypeStruct(cells.shape, jnp.float32),
        in_specs=[vmem, vmem, vmem],
        out_specs=vmem,
        scratch_shapes=[pltpu.VMEM((energies + 2 * HALO, height, LANES), jnp.float32)],
        compiler_params=pltpu.CompilerParams(vmem_limit_bytes=16 * 2**20),
        name="convolve",
    )(steps, cells, coef)


def embed(pair):
    order = pair.shape[1] // 2
    return jnp.concatenate(
        [pair, jnp.concatenate([-pair[:, order:], pair[:, :order]], axis=1)], axis=0
    )


def pieces(value, count):
    parts = []
    for index in range(count):
        parts.append(value.astype(jnp.bfloat16))
        if index + 1 < count:
            value = value - parts[-1].astype(jnp.float32)
    return parts


def unit_pair(order):
    row = lax.broadcasted_iota(jnp.int32, (order, 2 * order), 0)
    column = lax.broadcasted_iota(jnp.int32, (order, 2 * order), 1)
    return jnp.where(row == column, 1.0, 0.0).astype(jnp.float32)


def square_sum(pair):
    squares = pair * pair
    return jnp.sum(jnp.sum(squares, axis=0, keepdims=True), axis=1, keepdims=True)


def adjoint(pair):
    order = pair.shape[0]
    return jnp.concatenate([pair[:, :order].T, -pair[:, order:].T], axis=1)


class Multiplier:
    def __init__(self, blocks):
        self.blocks = blocks
        self.turn = 0

    def load(self, factor, transpose=False):
        stage = self.turn
        self.turn = 1 - stage
        for unit in range(2):
            pltpu.matmul_push_rhs(factor, stage, unit, transpose=transpose)
        return stage

    def feed(self, stage, *rows):
        for block, left in rows:
            for unit in range(2):
                mine = [left[row : row + 16] for row in range(16 * unit, left.shape[0], 32)]
                pltpu.matmul_acc_lhs(
                    self.blocks[block][unit],
                    jnp.concatenate(mine, axis=0),
                    load_staged_rhs=stage,
                )
            stage = None

    def take(self, block):
        halves = [pltpu.matmul_pop(self.blocks[block][unit]) for unit in range(2)]
        rows = range(0, halves[0].shape[0], 16)
        return jnp.concatenate([half[row : row + 16] for row in rows for half in halves], axis=0)

    def product(self, left, right, transpose=False):
        for index, factor in enumerate(right):
            stage = self.load(factor, transpose)
            self.feed(stage, *[(0, piece) for piece in left[: len(left) - index]])
        return self.take(0)


def iterate(mxu, matrix, follow, count):
    order = matrix.shape[0]
    split = pieces(matrix, 2)
    product = mxu.product(split[:1], [embed(split[0])], transpose=True)
    scale = 1.0 / square_sum(matrix)
    x = adjoint(matrix) * scale
    y = product * scale
    for index in range(count):
        narrow = y.astype(jnp.bfloat16)
        stage = mxu.load(embed(narrow))
        more = index + 1 < count
        if more:
            mxu.feed(stage, (0, narrow))
        if index:
            x = (x + x) - mxu.take(1)
        mxu.feed(None if more else stage, (1, x.astype(jnp.bfloat16)))
        if more:
            y = (y + y) - mxu.take(0)
    x = (x + x) - mxu.take(1)

    high, low = pieces(x, 2)
    wide = mxu.load(embed(high))
    rest = mxu.load(embed(low))
    mxu.feed(rest, (0, split[0]), (1, follow[0]))
    mxu.feed(wide, (0, split[0]), (0, split[1]), (1, follow[0]), (1, follow[1]))
    residual = unit_pair(order) - mxu.take(0)
    t = mxu.take(1)
    r_high, r_low = pieces(residual, 2)
    t_high, t_low = pieces(t, 2)
    wide = mxu.load(embed(r_high))
    rest = mxu.load(embed(r_low))
    mxu.feed(wide, (0, r_high), (2, t_high), (2, t_low), (1, high), (1, low))
    mxu.feed(rest, (2, t_high), (1, high))
    residual = mxu.take(0)
    stage = mxu.load(embed(residual.astype(jnp.bfloat16)))
    t = t + mxu.take(2)
    x = x + mxu.take(1)
    mxu.feed(stage, (1, t.astype(jnp.bfloat16)), (0, x.astype(jnp.bfloat16)))
    t = t + mxu.take(1)
    return x + mxu.take(0), t, square_sum(residual)


def iterate_plain(mxu, matrix):
    split = pieces(matrix, 3)
    unit = unit_pair(matrix.shape[0])

    def step(index, x):
        right = [embed(piece) for piece in pieces(x, 3)]
        residue = 2.0 * unit - mxu.product(split, right)
        return mxu.product(pieces(x, 3), [embed(piece) for piece in pieces(residue, 3)])

    return lax.fori_loop(0, INV_STEPS, step, adjoint(matrix) * (1.0 / square_sum(matrix)))


def pick(values, index, axis):
    return jnp.take_along_axis(values, index, axis=axis, mode="promise_in_bounds")


def solve_kernel(energy_ref, cells_ref, listed_ref, table_ref, diag_ref, coup_ref, out_ref, matrix_ref, stage_ref, sems):
    slabs, order, _ = diag_ref.shape
    unit = unit_pair(order)
    energy = energy_ref[...]
    row = lax.broadcasted_iota(jnp.int32, (8, LANES), 0)
    lines = cells_ref.shape[1] // 2
    line_of = row // (8 // lines)

    def assemble(slab, lanes):
        for block in range(order // 8):
            cell = cells_ref[slab * (order // 8) + block]
            rows = slice(block * 8, block * 8 + 8)
            table = lanes[rows, :]
            held = table >= 0
            lane = jnp.where(held, table, 0)
            for part in range(2):
                spread = pick(cell, line_of + part * lines, 0)
                sigma = jnp.where(held, pick(spread, lane, 1), 0.0)
                eye = unit[rows, :order]
                if part == 0:
                    entry = energy * eye - diag_ref[slab, rows, :] - sigma
                else:
                    entry = BROADEN * eye - sigma
                matrix_ref[slab, rows, part * order : (part + 1) * order] = entry

    assemble(1, table_ref[...])
    coup = coup_ref[0]
    none = jnp.zeros_like(coup)
    coup_left = jnp.concatenate([coup, none], axis=1)
    coup_right = embed(jnp.concatenate([coup.T, none], axis=1))

    def send(slab, pair):
        for part in range(2):
            stage_ref[part, slab] = pair[:, part * order : (part + 1) * order]
            pltpu.make_async_copy(stage_ref.at[part, slab], out_ref.at[part, slab], sems.at[part, slab]).start()

    def sent():
        for slab in range(slabs):
            for part in range(2):
                pltpu.make_async_copy(stage_ref.at[part, slab], out_ref.at[part, slab], sems.at[part, slab]).wait()

    def body(*accumulators):
        mxu = Multiplier([accumulators[2 * i : 2 * i + 2] for i in range(3)])
        right = pieces(coup_right, 2)
        last, left_of, last_norm = iterate(mxu, matrix_ref[1], pieces(coup_left, 2), INV_STEPS - EXACT_STEPS)
        assemble(0, lanes_of(listed_ref[0]))
        matrix = matrix_ref[0] - mxu.product(pieces(left_of, 2), right)
        right_of = mxu.product(pieces(last, 2), right)
        first, both, first_norm = iterate(mxu, matrix, pieces(right_of, 2), INV_STEPS - EXACT_STEPS)
        send(0, first)
        update = mxu.product(pieces(both, 2), [embed(piece) for piece in pieces(left_of, 2)])
        send(1, last + update)
        worst = jnp.maximum(last_norm, first_norm)[0, 0]
        settled = jnp.logical_and(worst <= RESIDUAL_LIMIT, last_norm[0, 0] + first_norm[0, 0] <= 2.0 * RESIDUAL_LIMIT)
        sent()

        @pl.when(jnp.logical_not(settled))
        def _():
            right = pieces(coup_right, 3)
            last = iterate_plain(mxu, matrix_ref[1])
            left_of = mxu.product(pieces(coup_left, 3), [embed(piece) for piece in pieces(last, 3)])
            right_of = mxu.product(pieces(last, 3), right)
            first = iterate_plain(mxu, matrix_ref[0] - mxu.product(pieces(left_of, 3), right))
            both = mxu.product(pieces(right_of, 3), [embed(piece) for piece in pieces(first, 3)])
            update = mxu.product(pieces(both, 3), [embed(piece) for piece in pieces(left_of, 3)])
            send(0, first)
            send(1, last + update)
            sent()

    shape = (order // 2, 2 * order)
    pl.run_scoped(body, *[pltpu.ACC(unit)(shape, jnp.float32) for _ in range(3) for unit in range(2)])


def solve(energy, cells, listed, table, ham_diag, ham_coup):
    slabs, order, _ = ham_diag.shape
    vmem = pl.BlockSpec(memory_space=VMEM)
    return pl.pallas_call(
        solve_kernel,
        out_shape=jax.ShapeDtypeStruct((2, slabs, order, order), jnp.float32),
        in_specs=[vmem] * 6,
        out_specs=pl.BlockSpec(memory_space=pl.ANY),
        scratch_shapes=[
            pltpu.VMEM((slabs, order, 2 * order), jnp.float32),
            pltpu.VMEM((2, slabs, order, order), jnp.float32),
            pltpu.SemaphoreType.DMA((2, slabs)),
        ],
        compiler_params=pltpu.CompilerParams(vmem_limit_bytes=16 * 2**20),
        name="solve",
    )(energy, cells, listed, table, ham_diag, ham_coup)


def on_device(ham_diag, ham_coup, neighbors, pair_count, shifts, g_pairs, emit_coup, absorb_coup):
    slabs, order, _ = ham_diag.shape
    atoms, slots = neighbors.shape
    devices = lax.axis_size("freq") * lax.axis_size("atom")
    rows = g_pairs.shape[2] // LANES
    rows_per = -(-rows // devices)
    spare = rows_per * devices - rows

    cells = g_pairs.reshape(2, rows, LANES)
    if spare:
        cells = jnp.pad(cells, ((0, 0), (0, spare), (0, 0)))
    cells, listed, table, coef, steps, energy = prepare(
        cells.reshape(2, devices, rows_per, LANES), neighbors, pair_count, shifts, emit_coup, absorb_coup, slabs, order
    )
    owned = lax.all_to_all(cells, AXES, 0, 0, tiled=True)
    sigma = convolve(steps, owned, coef)
    sigma = lax.all_to_all(sigma, AXES, 0, 0, tiled=True)
    lines = 8 * slots // LANES
    if rows_per != lines:
        sigma = sigma.reshape(devices, 2, rows_per, LANES).transpose(1, 0, 2, 3)
        sigma = sigma.reshape(2, devices * rows_per, LANES)[:, :rows]
        sigma = sigma.reshape(2, rows // lines, lines, LANES).transpose(1, 0, 2, 3)
        sigma = sigma.reshape(rows // lines, 2 * lines, LANES)
    green = solve(energy, sigma, listed, table, ham_diag, ham_coup)
    return green.reshape(2, 1, slabs, order, order)


def solution(mesh):
    return jax.shard_map(
        on_device,
        mesh=mesh,
        in_specs=(P(), P(), P(), P(), P(), P(None, ("freq", "atom"), None), P(), P()),
        out_specs=P(None, ("freq", "atom"), None, None, None),
        check_vma=False,
    )
```

```python
import functools

import jax
import jax.numpy as jnp
from jax import lax
from jax.experimental import pallas as pl
from jax.experimental.pallas import tpu as pltpu
from jax.sharding import PartitionSpec as P

HALO = 16
INV_STEPS = 22
EXACT_STEPS = 2

BROADEN = 0.8
ENERGY_LOW = -2.5
ENERGY_SPAN = 5.0

LANES = 128
RESIDUAL_LIMIT = 2e-5

AXES = ("freq", "atom")
VMEM = pltpu.MemorySpace.VMEM
SMEM = pltpu.MemorySpace.SMEM


def lanes_of(listed):
    slots, order = listed.shape
    column = lax.broadcasted_iota(jnp.int32, (order, order), 0).astype(jnp.float32).astype(jnp.bfloat16)
    column = column.reshape(order // 16, 16, order)
    found = jnp.full((order // 16, 16, order), -1.0, jnp.bfloat16)
    for slot in range(slots):
        row = jnp.broadcast_to(listed[slot : slot + 1, :], (16, order)).astype(jnp.bfloat16)
        found = jnp.where(row[None] == column, jnp.bfloat16(slot), found)
    found = found.reshape(order, order).astype(jnp.float32).astype(jnp.int32)
    lane = lax.broadcasted_iota(jnp.int32, (order, order), 1)
    offset = lax.rem(lane, LANES // slots) * slots
    return jnp.where(found >= 0, found + offset, -1).T


def prepare_kernel(
    cells_hbm,
    neighbors_hbm,
    count_hbm,
    shifts_hbm,
    emit_hbm,
    absorb_hbm,
    cells_ref,
    listed_ref,
    coef_ref,
    steps_ref,
    energy_ref,
    neighbors_ref,
    count_ref,
    shifts_ref,
    weights_ref,
    sems,
    *,
    energies,
):
    own = lax.axis_index("freq") * lax.axis_size("atom") + lax.axis_index("atom")
    slabs, slots, order = listed_ref.shape
    half = coef_ref.shape[3] // 2
    width = half * LANES
    block = jnp.minimum(own, emit_hbm.shape[2] // width - 1)
    lanes = pl.ds(pl.multiple_of(block * width, LANES), width)
    copies = [
        pltpu.make_async_copy(neighbors_hbm, neighbors_ref, sems.at[0]),
        pltpu.make_async_copy(count_hbm, count_ref, sems.at[1]),
        pltpu.make_async_copy(emit_hbm.at[:, :, lanes], weights_ref.at[0], sems.at[2]),
        pltpu.make_async_copy(absorb_hbm.at[:, :, lanes], weights_ref.at[1], sems.at[3]),
        pltpu.make_async_copy(shifts_hbm, shifts_ref, sems.at[4]),
    ]
    lines = cells_hbm.shape[2]
    for part in range(cells_hbm.shape[0]):
        rows = slice(part * lines, (part + 1) * lines)
        copies.append(pltpu.make_async_copy(cells_hbm.at[part], cells_ref.at[:, rows, :], sems.at[5 + part]))
    for copy in copies:
        copy.start()
    position = jnp.full(energy_ref.shape, own, jnp.int32).astype(jnp.float32)
    energy_ref[...] = ENERGY_LOW + ENERGY_SPAN * position / energies
    copies[0].wait()
    copies[1].wait()
    slot_id = lax.broadcasted_iota(jnp.int32, (slots, order), 0)
    for slab in range(slabs):
        listed = neighbors_ref[:, slab * order : (slab + 1) * order]
        listed_ref[slab] = jnp.where(slot_id < count_ref[slab : slab + 1, :], listed, -1).astype(jnp.float32)
    for copy in copies[2:5]:
        copy.wait()
    for mode in range(steps_ref.shape[0]):
        steps_ref[mode] = jnp.full(steps_ref.shape[1:], shifts_ref[mode], jnp.int32)
    for side in range(2):
        for row in range(half):
            part = slice(row * LANES, (row + 1) * LANES)
            real = weights_ref[side, 0, :, part]
            imag = weights_ref[side, 1, :, part]
            coef_ref[side, 0, :, row, :] = real
            coef_ref[side, 0, :, half + row, :] = real
            coef_ref[side, 1, :, row, :] = imag
            coef_ref[side, 1, :, half + row, :] = -imag
    for copy in copies[5:]:
        copy.wait()


def prepare(cells, neighbors, pair_count, shifts, emit_coup, absorb_coup, slabs, order):
    parts, devices, rows_per, _ = cells.shape
    modes = emit_coup.shape[1]
    atoms, slots = neighbors.shape
    arrays = (cells, neighbors.T, pair_count.reshape(slabs, order), shifts, emit_coup, absorb_coup)
    return pl.pallas_call(
        functools.partial(prepare_kernel, energies=devices),
        out_shape=(
            jax.ShapeDtypeStruct((devices, parts * rows_per, LANES), jnp.float32),
            jax.ShapeDtypeStruct((slabs, slots, order), jnp.float32),
            jax.ShapeDtypeStruct((2, 2, modes, 2 * rows_per, LANES), jnp.float32),
            jax.ShapeDtypeStruct((modes, 8, LANES), jnp.int32),
            jax.ShapeDtypeStruct((8, LANES), jnp.float32),
        ),
        in_specs=[pl.BlockSpec(memory_space=pltpu.HBM)] * 6,
        out_specs=(pl.BlockSpec(memory_space=VMEM),) * 5,
        scratch_shapes=[
            pltpu.VMEM((slots, atoms), jnp.int32),
            pltpu.VMEM((slabs, order), jnp.int32),
            pltpu.SMEM((modes,), jnp.int32),
            pltpu.VMEM((2, 2, modes, rows_per * LANES), jnp.float32),
            pltpu.SemaphoreType.DMA((7,)),
        ],
        compiler_params=pltpu.CompilerParams(vmem_limit_bytes=16 * 2**20),
        name="prepare",
    )(*[pltpu.with_memory_space_constraint(array, pltpu.HBM) for array in arrays])


def convolve_kernel(steps_ref, cells_ref, coef_ref, listed_ref, out_ref, table_ref, padded_ref):
    table_ref[...] = lanes_of(listed_ref[listed_ref.shape[0] - 1])
    energies, height, _ = cells_ref.shape
    modes = coef_ref.shape[2]
    half = height // 2
    shifts = [steps_ref[mode][0, 0] for mode in range(modes)]
    edge = jnp.zeros((HALO, height, LANES), jnp.float32)
    padded_ref[0:HALO] = edge
    padded_ref[HALO + energies : 2 * HALO + energies] = edge
    group = 16 if energies % 16 == 0 else 1

    def load(index, carry):
        rows = pl.ds(index * group, group)
        padded_ref[pl.ds(HALO + index * group, group)] = cells_ref[rows]
        return carry

    def combine(index, carry):
        base = HALO + index * group
        direct_sum = [jnp.zeros((height, LANES), jnp.float32)] * group
        crossed_sum = list(direct_sum)
        for mode in range(modes):
            shift = shifts[mode]
            for side in range(2):
                first = base + (shift if side else -shift)
                direct = coef_ref[side, 0, mode]
                crossed = coef_ref[side, 1, mode]
                for step in range(group):
                    cell = padded_ref[first + step]
                    direct_sum[step] = direct_sum[step] + direct * cell
                    crossed_sum[step] = crossed_sum[step] + crossed * cell
        for step in range(group):
            turned = jnp.concatenate([crossed_sum[step][half:], crossed_sum[step][:half]], axis=0)
            out_ref[index * group + step] = direct_sum[step] + turned
        return carry

    lax.fori_loop(0, energies // group, load, 0, unroll=energies // group <= 2)
    lax.fori_loop(0, energies // group, combine, 0, unroll=energies // group <= 2)


def convolve(steps, cells, coef, listed):
    energies, height, _ = cells.shape
    vmem = pl.BlockSpec(memory_space=VMEM)
    return pl.pallas_call(
        convolve_kernel,
        out_shape=(
            jax.ShapeDtypeStruct(cells.shape, jnp.float32),
            jax.ShapeDtypeStruct((listed.shape[2],) * 2, jnp.int32),
        ),
        in_specs=[vmem] * 4,
        out_specs=(vmem, vmem),
        scratch_shapes=[pltpu.VMEM((energies + 2 * HALO, height, LANES), jnp.float32)],
        compiler_params=pltpu.CompilerParams(vmem_limit_bytes=16 * 2**20),
        name="convolve",
    )(steps, cells, coef, listed)


def embed(pair):
    order = pair.shape[1] // 2
    return jnp.concatenate(
        [pair, jnp.concatenate([-pair[:, order:], pair[:, :order]], axis=1)], axis=0
    )


def pieces(value, count):
    parts = []
    for index in range(count):
        parts.append(value.astype(jnp.bfloat16))
        if index + 1 < count:
            value = value - parts[-1].astype(jnp.float32)
    return parts


def unit_pair(order):
    row = lax.broadcasted_iota(jnp.int32, (order, 2 * order), 0)
    column = lax.broadcasted_iota(jnp.int32, (order, 2 * order), 1)
    return jnp.where(row == column, 1.0, 0.0).astype(jnp.float32)


def square_sum(pair):
    squares = pair * pair
    return jnp.sum(jnp.sum(squares, axis=0, keepdims=True), axis=1, keepdims=True)


def adjoint(pair):
    order = pair.shape[0]
    return jnp.concatenate([pair[:, :order].T, -pair[:, order:].T], axis=1)


class Multiplier:
    def __init__(self, blocks):
        self.blocks = blocks
        self.turn = 0

    def load(self, factor, transpose=False):
        stage = self.turn
        self.turn = 1 - stage
        for unit in range(2):
            pltpu.matmul_push_rhs(factor, stage, unit, transpose=transpose)
        return stage

    def feed(self, stage, *rows):
        for block, left in rows:
            for unit in range(2):
                mine = [left[row : row + 16] for row in range(16 * unit, left.shape[0], 32)]
                pltpu.matmul_acc_lhs(
                    self.blocks[block][unit],
                    jnp.concatenate(mine, axis=0),
                    load_staged_rhs=stage,
                )
            stage = None

    def take(self, block):
        halves = [pltpu.matmul_pop(self.blocks[block][unit]) for unit in range(2)]
        rows = range(0, halves[0].shape[0], 16)
        return jnp.concatenate([half[row : row + 16] for row in rows for half in halves], axis=0)

    def product(self, left, right, transpose=False):
        for index, factor in enumerate(right):
            stage = self.load(factor, transpose)
            self.feed(stage, *[(0, piece) for piece in left[: len(left) - index]])
        return self.take(0)


def iterate(mxu, matrix, follow, count):
    order = matrix.shape[0]
    split = pieces(matrix, 2)
    product = mxu.product(split[:1], [embed(split[0])], transpose=True)
    scale = 1.0 / square_sum(matrix)
    x = adjoint(matrix) * scale
    y = product * scale
    for index in range(count):
        narrow = y.astype(jnp.bfloat16)
        stage = mxu.load(embed(narrow))
        more = index + 1 < count
        if more:
            mxu.feed(stage, (0, narrow))
        if index:
            x = (x + x) - mxu.take(1)
        mxu.feed(None if more else stage, (1, x.astype(jnp.bfloat16)))
        if more:
            y = (y + y) - mxu.take(0)
    x = (x + x) - mxu.take(1)

    high, low = pieces(x, 2)
    wide = mxu.load(embed(high))
    rest = mxu.load(embed(low))
    mxu.feed(rest, (0, split[0]), (1, follow[0]))
    mxu.feed(wide, (0, split[0]), (0, split[1]), (1, follow[0]), (1, follow[1]))
    residual = unit_pair(order) - mxu.take(0)
    t = mxu.take(1)
    r_high, r_low = pieces(residual, 2)
    t_high, t_low = pieces(t, 2)
    wide = mxu.load(embed(r_high))
    rest = mxu.load(embed(r_low))
    mxu.feed(wide, (0, r_high), (2, t_high), (2, t_low), (1, high), (1, low))
    mxu.feed(rest, (2, t_high), (1, high))
    residual = mxu.take(0)
    stage = mxu.load(embed(residual.astype(jnp.bfloat16)))
    t = t + mxu.take(2)
    x = x + mxu.take(1)
    mxu.feed(stage, (1, t.astype(jnp.bfloat16)), (0, x.astype(jnp.bfloat16)))
    t = t + mxu.take(1)
    return x + mxu.take(0), t, square_sum(residual)


def iterate_plain(mxu, matrix):
    split = pieces(matrix, 3)
    unit = unit_pair(matrix.shape[0])

    def step(index, x):
        right = [embed(piece) for piece in pieces(x, 3)]
        residue = 2.0 * unit - mxu.product(split, right)
        return mxu.product(pieces(x, 3), [embed(piece) for piece in pieces(residue, 3)])

    return lax.fori_loop(0, INV_STEPS, step, adjoint(matrix) * (1.0 / square_sum(matrix)))


def pick(values, index, axis):
    return jnp.take_along_axis(values, index, axis=axis, mode="promise_in_bounds")


def solve_kernel(energy_ref, cells_ref, listed_ref, table_ref, diag_ref, coup_ref, out_ref, matrix_ref, stage_ref, sems):
    slabs, order, _ = diag_ref.shape
    unit = unit_pair(order)
    energy = energy_ref[...]
    row = lax.broadcasted_iota(jnp.int32, (8, LANES), 0)
    lines = cells_ref.shape[1] // 2
    line_of = row // (8 // lines)

    def assemble(slab, lanes):
        for block in range(order // 8):
            cell = cells_ref[slab * (order // 8) + block]
            rows = slice(block * 8, block * 8 + 8)
            table = lanes[rows, :]
            held = table >= 0
            lane = jnp.where(held, table, 0)
            for part in range(2):
                spread = pick(cell, line_of + part * lines, 0)
                sigma = jnp.where(held, pick(spread, lane, 1), 0.0)
                eye = unit[rows, :order]
                if part == 0:
                    entry = energy * eye - diag_ref[slab, rows, :] - sigma
                else:
                    entry = BROADEN * eye - sigma
                matrix_ref[slab, rows, part * order : (part + 1) * order] = entry

    assemble(1, table_ref[...])
    coup = coup_ref[0]
    none = jnp.zeros_like(coup)
    coup_left = jnp.concatenate([coup, none], axis=1)
    coup_right = embed(jnp.concatenate([coup.T, none], axis=1))

    def send(slab, pair):
        for part in range(2):
            stage_ref[part, slab] = pair[:, part * order : (part + 1) * order]
            pltpu.make_async_copy(stage_ref.at[part, slab], out_ref.at[part, slab], sems.at[part, slab]).start()

    def sent():
        for slab in range(slabs):
            for part in range(2):
                pltpu.make_async_copy(stage_ref.at[part, slab], out_ref.at[part, slab], sems.at[part, slab]).wait()

    def body(*accumulators):
        mxu = Multiplier([accumulators[2 * i : 2 * i + 2] for i in range(3)])
        right = pieces(coup_right, 2)
        last, left_of, last_norm = iterate(mxu, matrix_ref[1], pieces(coup_left, 2), INV_STEPS - EXACT_STEPS)
        assemble(0, lanes_of(listed_ref[0]))
        matrix = matrix_ref[0] - mxu.product(pieces(left_of, 2), right)
        right_of = mxu.product(pieces(last, 2), right)
        first, both, first_norm = iterate(mxu, matrix, pieces(right_of, 2), INV_STEPS - EXACT_STEPS)
        send(0, first)
        update = mxu.product(pieces(both, 2), [embed(piece) for piece in pieces(left_of, 2)])
        send(1, last + update)
        worst = jnp.maximum(last_norm, first_norm)[0, 0]
        settled = jnp.logical_and(worst <= RESIDUAL_LIMIT, last_norm[0, 0] + first_norm[0, 0] <= 2.0 * RESIDUAL_LIMIT)
        sent()

        @pl.when(jnp.logical_not(settled))
        def _():
            right = pieces(coup_right, 3)
            last = iterate_plain(mxu, matrix_ref[1])
            left_of = mxu.product(pieces(coup_left, 3), [embed(piece) for piece in pieces(last, 3)])
            right_of = mxu.product(pieces(last, 3), right)
            first = iterate_plain(mxu, matrix_ref[0] - mxu.product(pieces(left_of, 3), right))
            both = mxu.product(pieces(right_of, 3), [embed(piece) for piece in pieces(first, 3)])
            update = mxu.product(pieces(both, 3), [embed(piece) for piece in pieces(left_of, 3)])
            send(0, first)
            send(1, last + update)
            sent()

    shape = (order // 2, 2 * order)
    pl.run_scoped(body, *[pltpu.ACC(unit)(shape, jnp.float32) for _ in range(3) for unit in range(2)])


def solve(energy, cells, listed, table, ham_diag, ham_coup):
    slabs, order, _ = ham_diag.shape
    vmem = pl.BlockSpec(memory_space=VMEM)
    return pl.pallas_call(
        solve_kernel,
        out_shape=jax.ShapeDtypeStruct((2, slabs, order, order), jnp.float32),
        in_specs=[vmem] * 6,
        out_specs=pl.BlockSpec(memory_space=pl.ANY),
        scratch_shapes=[
            pltpu.VMEM((slabs, order, 2 * order), jnp.float32),
            pltpu.VMEM((2, slabs, order, order), jnp.float32),
            pltpu.SemaphoreType.DMA((2, slabs)),
        ],
        compiler_params=pltpu.CompilerParams(vmem_limit_bytes=16 * 2**20),
        name="solve",
    )(energy, cells, listed, table, ham_diag, ham_coup)


def on_device(ham_diag, ham_coup, neighbors, pair_count, shifts, g_pairs, emit_coup, absorb_coup):
    slabs, order, _ = ham_diag.shape
    atoms, slots = neighbors.shape
    devices = lax.axis_size("freq") * lax.axis_size("atom")
    rows = g_pairs.shape[2] // LANES
    rows_per = -(-rows // devices)
    spare = rows_per * devices - rows

    cells = g_pairs.reshape(2, rows, LANES)
    if spare:
        cells = jnp.pad(cells, ((0, 0), (0, spare), (0, 0)))
    cells, listed, coef, steps, energy = prepare(
        cells.reshape(2, devices, rows_per, LANES), neighbors, pair_count, shifts, emit_coup, absorb_coup, slabs, order
    )
    owned = lax.all_to_all(cells, AXES, 0, 0, tiled=True)
    sigma, table = convolve(steps, owned, coef, listed)
    sigma = lax.all_to_all(sigma, AXES, 0, 0, tiled=True)
    lines = 8 * slots // LANES
    if rows_per != lines:
        sigma = sigma.reshape(devices, 2, rows_per, LANES).transpose(1, 0, 2, 3)
        sigma = sigma.reshape(2, devices * rows_per, LANES)[:, :rows]
        sigma = sigma.reshape(2, rows // lines, lines, LANES).transpose(1, 0, 2, 3)
        sigma = sigma.reshape(rows // lines, 2 * lines, LANES)
    green = solve(energy, sigma, listed, table, ham_diag, ham_coup)
    return green.reshape(2, 1, slabs, order, order)


def solution(mesh):
    return jax.shard_map(
        on_device,
        mesh=mesh,
        in_specs=(P(), P(), P(), P(), P(), P(None, ("freq", "atom"), None), P(), P()),
        out_specs=P(None, ("freq", "atom"), None, None, None),
        check_vma=False,
    )
```

```python
import functools

import jax
import jax.numpy as jnp
from jax import lax
from jax.experimental import pallas as pl
from jax.experimental.pallas import tpu as pltpu
from jax.sharding import PartitionSpec as P

HALO = 16
INV_STEPS = 22
EXACT_STEPS = 2

BROADEN = 0.8
ENERGY_LOW = -2.5
ENERGY_SPAN = 5.0

LANES = 128
RESIDUAL_LIMIT = 2e-5

AXES = ("freq", "atom")
VMEM = pltpu.MemorySpace.VMEM
SMEM = pltpu.MemorySpace.SMEM


def lanes_of(listed):
    slots, order = listed.shape
    column = lax.broadcasted_iota(jnp.int32, (order, order), 0).astype(jnp.float32).astype(jnp.bfloat16)
    column = column.reshape(order // 16, 16, order)
    found = jnp.full((order // 16, 16, order), -1.0, jnp.bfloat16)
    for slot in range(slots):
        row = jnp.broadcast_to(listed[slot : slot + 1, :], (16, order)).astype(jnp.bfloat16)
        found = jnp.where(row[None] == column, jnp.bfloat16(slot), found)
    found = found.reshape(order, order).astype(jnp.float32).astype(jnp.int32)
    lane = lax.broadcasted_iota(jnp.int32, (order, order), 1)
    offset = lax.rem(lane, LANES // slots) * slots
    return jnp.where(found >= 0, found + offset, -1).T


def prepare_kernel(
    cells_hbm,
    neighbors_hbm,
    count_hbm,
    shifts_hbm,
    emit_hbm,
    absorb_hbm,
    cells_ref,
    listed_ref,
    coef_ref,
    steps_ref,
    energy_ref,
    neighbors_ref,
    count_ref,
    shifts_ref,
    weights_ref,
    sems,
    *,
    energies,
):
    own = lax.axis_index("freq") * lax.axis_size("atom") + lax.axis_index("atom")
    slabs, slots, order = listed_ref.shape
    half = coef_ref.shape[3] // 2
    width = half * LANES
    block = jnp.minimum(own, emit_hbm.shape[2] // width - 1)
    lanes = pl.ds(pl.multiple_of(block * width, LANES), width)
    copies = [
        pltpu.make_async_copy(neighbors_hbm, neighbors_ref, sems.at[0]),
        pltpu.make_async_copy(count_hbm, count_ref, sems.at[1]),
        pltpu.make_async_copy(emit_hbm.at[:, :, lanes], weights_ref.at[0], sems.at[2]),
        pltpu.make_async_copy(absorb_hbm.at[:, :, lanes], weights_ref.at[1], sems.at[3]),
        pltpu.make_async_copy(shifts_hbm, shifts_ref, sems.at[4]),
    ]
    lines = cells_hbm.shape[2]
    for part in range(cells_hbm.shape[0]):
        rows = slice(part * lines, (part + 1) * lines)
        copies.append(pltpu.make_async_copy(cells_hbm.at[part], cells_ref.at[:, rows, :], sems.at[5 + part]))
    for copy in copies:
        copy.start()
    position = jnp.full(energy_ref.shape, own, jnp.int32).astype(jnp.float32)
    energy_ref[...] = ENERGY_LOW + ENERGY_SPAN * position / energies
    copies[0].wait()
    copies[1].wait()
    slot_id = lax.broadcasted_iota(jnp.int32, (slots, order), 0)
    for slab in range(slabs):
        listed = neighbors_ref[:, slab * order : (slab + 1) * order]
        listed_ref[slab] = jnp.where(slot_id < count_ref[slab : slab + 1, :], listed, -1).astype(jnp.float32)
    for copy in copies[2:5]:
        copy.wait()
    for mode in range(steps_ref.shape[0]):
        steps_ref[mode] = jnp.full(steps_ref.shape[1:], shifts_ref[mode], jnp.int32)
    for side in range(2):
        for row in range(half):
            part = slice(row * LANES, (row + 1) * LANES)
            real = weights_ref[side, 0, :, part]
            imag = weights_ref[side, 1, :, part]
            coef_ref[side, 0, :, row, :] = real
            coef_ref[side, 0, :, half + row, :] = real
            coef_ref[side, 1, :, row, :] = imag
            coef_ref[side, 1, :, half + row, :] = -imag
    for copy in copies[5:]:
        copy.wait()


def prepare(cells, neighbors, pair_count, shifts, emit_coup, absorb_coup, slabs, order):
    parts, devices, rows_per, _ = cells.shape
    modes = emit_coup.shape[1]
    atoms, slots = neighbors.shape
    arrays = (cells, neighbors.T, pair_count.reshape(slabs, order), shifts, emit_coup, absorb_coup)
    return pl.pallas_call(
        functools.partial(prepare_kernel, energies=devices),
        out_shape=(
            jax.ShapeDtypeStruct((devices, parts * rows_per, LANES), jnp.float32),
            jax.ShapeDtypeStruct((slabs, slots, order), jnp.float32),
            jax.ShapeDtypeStruct((2, 2, modes, 2 * rows_per, LANES), jnp.float32),
            jax.ShapeDtypeStruct((modes, 8, LANES), jnp.int32),
            jax.ShapeDtypeStruct((8, LANES), jnp.float32),
        ),
        in_specs=[pl.BlockSpec(memory_space=pltpu.HBM)] * 6,
        out_specs=(pl.BlockSpec(memory_space=VMEM),) * 5,
        scratch_shapes=[
            pltpu.VMEM((slots, atoms), jnp.int32),
            pltpu.VMEM((slabs, order), jnp.int32),
            pltpu.SMEM((modes,), jnp.int32),
            pltpu.VMEM((2, 2, modes, rows_per * LANES), jnp.float32),
            pltpu.SemaphoreType.DMA((7,)),
        ],
        compiler_params=pltpu.CompilerParams(vmem_limit_bytes=16 * 2**20),
        name="prepare",
    )(*[pltpu.with_memory_space_constraint(array, pltpu.HBM) for array in arrays])


def convolve_kernel(steps_ref, cells_ref, coef_ref, listed_ref, out_ref, table_ref, padded_ref):
    table_ref[...] = lanes_of(listed_ref[listed_ref.shape[0] - 1])
    energies, height, _ = cells_ref.shape
    modes = coef_ref.shape[2]
    half = height // 2
    shifts = [steps_ref[mode][0, 0] for mode in range(modes)]
    edge = jnp.zeros((HALO, height, LANES), jnp.float32)
    padded_ref[0:HALO] = edge
    padded_ref[HALO + energies : 2 * HALO + energies] = edge
    group = 16 if energies % 16 == 0 else 1

    def load(index, carry):
        rows = pl.ds(index * group, group)
        padded_ref[pl.ds(HALO + index * group, group)] = cells_ref[rows]
        return carry

    def combine(index, carry):
        base = HALO + index * group
        direct_sum = [jnp.zeros((height, LANES), jnp.float32)] * group
        crossed_sum = list(direct_sum)
        for mode in range(modes):
            shift = shifts[mode]
            for side in range(2):
                first = base + (shift if side else -shift)
                direct = coef_ref[side, 0, mode]
                crossed = coef_ref[side, 1, mode]
                for step in range(group):
                    cell = padded_ref[first + step]
                    direct_sum[step] = direct_sum[step] + direct * cell
                    crossed_sum[step] = crossed_sum[step] + crossed * cell
        for step in range(group):
            turned = jnp.concatenate([crossed_sum[step][half:], crossed_sum[step][:half]], axis=0)
            out_ref[index * group + step] = direct_sum[step] + turned
        return carry

    lax.fori_loop(0, energies // group, load, 0, unroll=energies // group <= 2)
    lax.fori_loop(0, energies // group, combine, 0, unroll=energies // group <= 2)


def convolve(steps, cells, coef, listed):
    energies, height, _ = cells.shape
    vmem = pl.BlockSpec(memory_space=VMEM)
    return pl.pallas_call(
        convolve_kernel,
        out_shape=(
            jax.ShapeDtypeStruct(cells.shape, jnp.float32),
            jax.ShapeDtypeStruct((listed.shape[2],) * 2, jnp.int32),
        ),
        in_specs=[vmem] * 4,
        out_specs=(vmem, vmem),
        scratch_shapes=[pltpu.VMEM((energies + 2 * HALO, height, LANES), jnp.float32)],
        compiler_params=pltpu.CompilerParams(vmem_limit_bytes=16 * 2**20),
        name="convolve",
    )(steps, cells, coef, listed)


def embed(pair):
    order = pair.shape[1] // 2
    return jnp.concatenate(
        [pair, jnp.concatenate([-pair[:, order:], pair[:, :order]], axis=1)], axis=0
    )


def pieces(value, count):
    parts = []
    for index in range(count):
        parts.append(value.astype(jnp.bfloat16))
        if index + 1 < count:
            value = value - parts[-1].astype(jnp.float32)
    return parts


def unit_pair(order):
    row = lax.broadcasted_iota(jnp.int32, (order, 2 * order), 0)
    column = lax.broadcasted_iota(jnp.int32, (order, 2 * order), 1)
    return jnp.where(row == column, 1.0, 0.0).astype(jnp.float32)


def square_sum(pair):
    squares = pair * pair
    return jnp.sum(jnp.sum(squares, axis=0, keepdims=True), axis=1, keepdims=True)


def adjoint(pair):
    order = pair.shape[0]
    return jnp.concatenate([pair[:, :order].T, -pair[:, order:].T], axis=1)


class Multiplier:
    def __init__(self, blocks):
        self.blocks = blocks
        self.turn = 0

    def load(self, factor, transpose=False):
        stage = self.turn
        self.turn = 1 - stage
        for unit in range(2):
            pltpu.matmul_push_rhs(factor, stage, unit, transpose=transpose)
        return stage

    def feed(self, stage, *rows):
        for block, left in rows:
            for unit in range(2):
                mine = [left[row : row + 16] for row in range(16 * unit, left.shape[0], 32)]
                pltpu.matmul_acc_lhs(
                    self.blocks[block][unit],
                    jnp.concatenate(mine, axis=0),
                    load_staged_rhs=stage,
                )
            stage = None

    def take(self, block):
        halves = [pltpu.matmul_pop(self.blocks[block][unit]) for unit in range(2)]
        rows = range(0, halves[0].shape[0], 16)
        return jnp.concatenate([half[row : row + 16] for row in rows for half in halves], axis=0)

    def product(self, left, right, transpose=False):
        for index, factor in enumerate(right):
            stage = self.load(factor, transpose)
            self.feed(stage, *[(0, piece) for piece in left[: len(left) - index]])
        return self.take(0)


def iterate(mxu, matrix, follow, count):
    order = matrix.shape[0]
    split = pieces(matrix, 2)
    product = mxu.product(split[:1], [embed(split[0])], transpose=True)
    scale = 1.0 / square_sum(matrix)
    x = adjoint(matrix) * scale
    y = product * scale
    for index in range(count):
        narrow = y.astype(jnp.bfloat16)
        turned = (-y[:, order:]).astype(jnp.bfloat16)
        stage = mxu.load(
            jnp.concatenate([narrow, jnp.concatenate([turned, narrow[:, :order]], axis=1)], axis=0)
        )
        more = index + 1 < count
        if more:
            mxu.feed(stage, (0, narrow))
        if index:
            x = (x + x) - mxu.take(1)
        mxu.feed(None if more else stage, (1, x.astype(jnp.bfloat16)))
        if more:
            y = (y + y) - mxu.take(0)
    x = (x + x) - mxu.take(1)

    high, low = pieces(x, 2)
    wide = mxu.load(embed(high))
    rest = mxu.load(embed(low))
    mxu.feed(rest, (0, split[0]), (1, follow[0]))
    mxu.feed(wide, (0, split[0]), (0, split[1]), (1, follow[0]), (1, follow[1]))
    residual = unit_pair(order) - mxu.take(0)
    t = mxu.take(1)
    r_high, r_low = pieces(residual, 2)
    t_high, t_low = pieces(t, 2)
    wide = mxu.load(embed(r_high))
    rest = mxu.load(embed(r_low))
    mxu.feed(wide, (0, r_high), (2, t_high), (2, t_low), (1, high), (1, low))
    mxu.feed(rest, (2, t_high), (1, high))
    residual = mxu.take(0)
    stage = mxu.load(embed(residual.astype(jnp.bfloat16)))
    t = t + mxu.take(2)
    x = x + mxu.take(1)
    mxu.feed(stage, (1, t.astype(jnp.bfloat16)), (0, x.astype(jnp.bfloat16)))
    t = t + mxu.take(1)
    return x + mxu.take(0), t, square_sum(residual)


def iterate_plain(mxu, matrix):
    split = pieces(matrix, 3)
    unit = unit_pair(matrix.shape[0])

    def step(index, x):
        right = [embed(piece) for piece in pieces(x, 3)]
        residue = 2.0 * unit - mxu.product(split, right)
        return mxu.product(pieces(x, 3), [embed(piece) for piece in pieces(residue, 3)])

    return lax.fori_loop(0, INV_STEPS, step, adjoint(matrix) * (1.0 / square_sum(matrix)))


def pick(values, index, axis):
    return jnp.take_along_axis(values, index, axis=axis, mode="promise_in_bounds")


def solve_kernel(energy_ref, cells_ref, listed_ref, table_ref, diag_ref, coup_ref, out_ref, matrix_ref, stage_ref, sems):
    slabs, order, _ = diag_ref.shape
    unit = unit_pair(order)
    energy = energy_ref[...]
    row = lax.broadcasted_iota(jnp.int32, (8, LANES), 0)
    lines = cells_ref.shape[1] // 2
    line_of = row // (8 // lines)

    def assemble(slab, lanes):
        for block in range(order // 8):
            cell = cells_ref[slab * (order // 8) + block]
            rows = slice(block * 8, block * 8 + 8)
            table = lanes[rows, :]
            held = table >= 0
            lane = jnp.where(held, table, 0)
            for part in range(2):
                spread = pick(cell, line_of + part * lines, 0)
                sigma = jnp.where(held, pick(spread, lane, 1), 0.0)
                eye = unit[rows, :order]
                if part == 0:
                    entry = energy * eye - diag_ref[slab, rows, :] - sigma
                else:
                    entry = BROADEN * eye - sigma
                matrix_ref[slab, rows, part * order : (part + 1) * order] = entry

    assemble(1, table_ref[...])
    coup = coup_ref[0]
    none = jnp.zeros_like(coup)
    coup_left = jnp.concatenate([coup, none], axis=1)
    coup_right = embed(jnp.concatenate([coup.T, none], axis=1))

    def send(slab, pair):
        for part in range(2):
            stage_ref[part, slab] = pair[:, part * order : (part + 1) * order]
            pltpu.make_async_copy(stage_ref.at[part, slab], out_ref.at[part, slab], sems.at[part, slab]).start()

    def sent():
        for slab in range(slabs):
            for part in range(2):
                pltpu.make_async_copy(stage_ref.at[part, slab], out_ref.at[part, slab], sems.at[part, slab]).wait()

    def body(*accumulators):
        mxu = Multiplier([accumulators[2 * i : 2 * i + 2] for i in range(3)])
        right = pieces(coup_right, 2)
        last, left_of, last_norm = iterate(mxu, matrix_ref[1], pieces(coup_left, 2), INV_STEPS - EXACT_STEPS)
        assemble(0, lanes_of(listed_ref[0]))
        matrix = matrix_ref[0] - mxu.product(pieces(left_of, 2), right)
        right_of = mxu.product(pieces(last, 2), right)
        first, both, first_norm = iterate(mxu, matrix, pieces(right_of, 2), INV_STEPS - EXACT_STEPS)
        send(0, first)
        update = mxu.product(pieces(both, 2), [embed(piece) for piece in pieces(left_of, 2)])
        send(1, last + update)
        worst = jnp.maximum(last_norm, first_norm)[0, 0]
        settled = jnp.logical_and(worst <= RESIDUAL_LIMIT, last_norm[0, 0] + first_norm[0, 0] <= 2.0 * RESIDUAL_LIMIT)
        sent()

        @pl.when(jnp.logical_not(settled))
        def _():
            right = pieces(coup_right, 3)
            last = iterate_plain(mxu, matrix_ref[1])
            left_of = mxu.product(pieces(coup_left, 3), [embed(piece) for piece in pieces(last, 3)])
            right_of = mxu.product(pieces(last, 3), right)
            first = iterate_plain(mxu, matrix_ref[0] - mxu.product(pieces(left_of, 3), right))
            both = mxu.product(pieces(right_of, 3), [embed(piece) for piece in pieces(first, 3)])
            update = mxu.product(pieces(both, 3), [embed(piece) for piece in pieces(left_of, 3)])
            send(0, first)
            send(1, last + update)
            sent()

    shape = (order // 2, 2 * order)
    pl.run_scoped(body, *[pltpu.ACC(unit)(shape, jnp.float32) for _ in range(3) for unit in range(2)])


def solve(energy, cells, listed, table, ham_diag, ham_coup):
    slabs, order, _ = ham_diag.shape
    vmem = pl.BlockSpec(memory_space=VMEM)
    return pl.pallas_call(
        solve_kernel,
        out_shape=jax.ShapeDtypeStruct((2, slabs, order, order), jnp.float32),
        in_specs=[vmem] * 6,
        out_specs=pl.BlockSpec(memory_space=pl.ANY),
        scratch_shapes=[
            pltpu.VMEM((slabs, order, 2 * order), jnp.float32),
            pltpu.VMEM((2, slabs, order, order), jnp.float32),
            pltpu.SemaphoreType.DMA((2, slabs)),
        ],
        compiler_params=pltpu.CompilerParams(vmem_limit_bytes=16 * 2**20),
        name="solve",
    )(energy, cells, listed, table, ham_diag, ham_coup)


def on_device(ham_diag, ham_coup, neighbors, pair_count, shifts, g_pairs, emit_coup, absorb_coup):
    slabs, order, _ = ham_diag.shape
    atoms, slots = neighbors.shape
    devices = lax.axis_size("freq") * lax.axis_size("atom")
    rows = g_pairs.shape[2] // LANES
    rows_per = -(-rows // devices)
    spare = rows_per * devices - rows

    cells = g_pairs.reshape(2, rows, LANES)
    if spare:
        cells = jnp.pad(cells, ((0, 0), (0, spare), (0, 0)))
    cells, listed, coef, steps, energy = prepare(
        cells.reshape(2, devices, rows_per, LANES), neighbors, pair_count, shifts, emit_coup, absorb_coup, slabs, order
    )
    owned = lax.all_to_all(cells, AXES, 0, 0, tiled=True)
    sigma, table = convolve(steps, owned, coef, listed)
    sigma = lax.all_to_all(sigma, AXES, 0, 0, tiled=True)
    lines = 8 * slots // LANES
    if rows_per != lines:
        sigma = sigma.reshape(devices, 2, rows_per, LANES).transpose(1, 0, 2, 3)
        sigma = sigma.reshape(2, devices * rows_per, LANES)[:, :rows]
        sigma = sigma.reshape(2, rows // lines, lines, LANES).transpose(1, 0, 2, 3)
        sigma = sigma.reshape(rows // lines, 2 * lines, LANES)
    green = solve(energy, sigma, listed, table, ham_diag, ham_coup)
    return green.reshape(2, 1, slabs, order, order)


def solution(mesh):
    return jax.shard_map(
        on_device,
        mesh=mesh,
        in_specs=(P(), P(), P(), P(), P(), P(None, ("freq", "atom"), None), P(), P()),
        out_specs=P(None, ("freq", "atom"), None, None, None),
        check_vma=False,
    )
```
